32 devices in a mesh: dp: 16 (over z, y, core), tensor: 2 (over x).
Axes of the slice: x: 2, y: 2, z: 4, core: 2. Of those that a mesh axis runs over, the one named last changes fastest.
Arguments:
- tokens: bfloat16 [16384, 768], P('dp'), may hold values from -6 to 6
- cotangent: bfloat16 [16384, 768], P('dp'), may hold values from -6 to 6
- bucket: int32 [16], P('dp'), may hold values from 0 to 1023
- mask: int32 [16384], P('dp'), may hold values 0 or 1
- time_embed: float32 [1024, 128], replicated, may hold values from -6 to 6
- mask_vec: float32 [768], replicated, may hold values from -6 to 6
- ln1_gain: float32 [768], replicated, may hold values from 0.5 to 1.5
- w_qkv: bfloat16 [3, 768, 768], P(None, None, 'tensor'), may hold values from -0.21875 to 0.21875
- w_out: bfloat16 [768, 768], P('tensor'), may hold values from -2 to 2
- ln2_gain: float32 [768], replicated, may hold values from 0.5 to 1.5
- w_up: bfloat16 [768, 3072], P(None, 'tensor'), may hold values from -0.21875 to 0.21875
- b_up: float32 [3072], P('tensor'), may hold values from -3 to 3
- w_down: bfloat16 [3072, 768], P('tensor'), may hold values from -0.109375 to 0.109375
- b_down: float32 [768], replicated, may hold values from -3 to 3
- w_ada: bfloat16 [128, 4608], replicated, may hold values from -0.5 to 0.5
- b_ada: float32 [4608], replicated, may hold values from -3 to 3
Outputs:
- result: bfloat16 [16384, 768], P('dp')
- grad_tokens: bfloat16 [16384, 768], P('dp')
- grad_mask_vec: float32 [768], P('dp')
- grad_ln1: float32 [768], P('dp')
- grad_w_qkv: float32 [3, 768, 768], P(None, 'dp', 'tensor')
- grad_w_out: float32 [768, 768], P('tensor', 'dp')
- grad_ln2: float32 [768], P('dp')
- grad_w_up: float32 [768, 3072], P('dp', 'tensor')
- grad_b_up: float32 [3072], P(('tensor', 'dp'))
- grad_w_down: float32 [3072, 768], P('tensor', 'dp')
- grad_b_down: float32 [768], P('dp')
- grad_w_ada: float32 [128, 4608], P(None, 'dp')
- grad_b_ada: float32 [4608], P('dp')
The draws below stay inside these ranges and needn't reach their ends.
All inputs are finite; a program needn't handle non-finite values. No bound on the sum of `mask` on one device may be relied on, other than what follows from the above.
Results may differ from the reference program's by a relative error of at most 0.013.
The reference program's roundings to bfloat16 on the way count: a program that leaves them out, or rounds other values in their place, can miss the bound.
Values sent between devices are 32-bit elements; how exact they have to be, the bound alone decides.
A program may use at most 192 MiB of HBM per device.

```python
import jax
import jax.numpy as jnp
from jax import lax

D = 768
H = 12
HD = 64
FF = 3072
TDIM = 128
BUCKETS = 1024
LEN = 1024
SEQS = 16
TOKENS = 16384


def place_ends(values, key, low, high):
    extent = values.shape
    index_at = [jax.random.randint(jax.random.fold_in(key, axis), (), 0, extent[axis]) for axis in range(len(extent))]
    values = values.at[tuple(index_at)].set(low)
    longest = extent.index(max(extent))
    index_at[longest] = (index_at[longest] + 1) % extent[longest]
    return values.at[tuple(index_at)].set(high)


def levels(stream_key, dims, cuts, low, high):
    loudness, own = 1.0, jax.random.fold_in(stream_key, 6)
    for axis_at, blocks in cuts:
        heights = jnp.exp(jax.random.uniform(jax.random.fold_in(own, axis_at), (blocks,), jnp.float32, low / len(cuts), high / len(cuts)))
        loudness = loudness * jnp.repeat(heights, dims[axis_at] // blocks).reshape([-1 if axis == axis_at else 1 for axis in range(len(dims))])
    return loudness


def bell_draw(stream_key, dims, width, reach, split=(), kind=jnp.bfloat16):
    loudness = levels(stream_key, dims, split, -0.22, 0.18) if split else 1.0
    values = jax.random.normal(stream_key, dims, jnp.float32) * width * loudness
    return jnp.minimum(jnp.maximum(values, -reach), reach).astype(kind)


def setup_inputs(seed: int = 0) -> dict:
    arg_keys = jax.random.split(jax.random.key(seed), 17)
    return {
        "tokens": bell_draw(arg_keys[0], (TOKENS, D), 1.0, 6.0, ((0, 16),)),
        "cotangent": bell_draw(arg_keys[1], (TOKENS, D), 1.0, 6.0, ((0, 16),)),
        "bucket": place_ends(jax.random.randint(arg_keys[2], (SEQS,), 0, BUCKETS), jax.random.fold_in(arg_keys[2], 1), 0, BUCKETS - 1).astype(jnp.int32),
        "mask": place_ends((jax.random.randint(arg_keys[3], (TOKENS,), 0, 2) < 1).astype(jnp.int32), jax.random.fold_in(arg_keys[3], 1), 0, 1),
        "time_embed": bell_draw(arg_keys[4], (BUCKETS, TDIM), 1.0, 6.0, (), jnp.float32),
        "mask_vec": bell_draw(arg_keys[5], (D,), 1.0, 6.0, (), jnp.float32),
        "ln1_gain": jnp.clip(jax.random.uniform(arg_keys[6], (D,), jnp.float32, 0.5, 1.5), 0.5, 1.5),
        "w_qkv": bell_draw(arg_keys[7], (3, D, D), D ** -0.5, 0.21875, ((2, 2),)),
        "w_out": bell_draw(arg_keys[8], (D, D), 8 ** -0.5, 2.0, ((0, 2),)),
        "ln2_gain": jnp.clip(jax.random.uniform(arg_keys[9], (D,), jnp.float32, 0.5, 1.5), 0.5, 1.5),
        "w_up": bell_draw(arg_keys[10], (D, FF), D ** -0.5, 0.21875, ((1, 2),)),
        "b_up": bell_draw(arg_keys[11], (FF,), 0.5, 3.0, ((0, 2),), jnp.float32),
        "w_down": bell_draw(arg_keys[12], (FF, D), FF ** -0.5, 0.109375, ((0, 2),)),
        "b_down": bell_draw(arg_keys[13], (D,), 0.5, 3.0, (), jnp.float32),
        "w_ada": bell_draw(arg_keys[14], (TDIM, 6 * D), TDIM ** -0.5, 0.5),
        "b_ada": bell_draw(arg_keys[15], (6 * D,), 0.5, 3.0, (), jnp.float32),
    }


@jax.custom_vjp
def low(v):
    return lax.optimization_barrier(v.astype(jnp.bfloat16)).astype(jnp.float32)

@jax.custom_vjp
def low_back(v):
    return v

def low_keep(v):
    return (low(v), None)

def low_pass(kept, grad):
    return (grad,)

def back_keep(v):
    return (v, None)

def back_low(kept, grad):
    return (low(grad),)
low.defvjp(low_keep, low_pass)
low_back.defvjp(back_keep, back_low)
HIGH_PRECISION = lax.Precision.HIGHEST
EPS = 1e-05

def modulate(x, gain, shift, scale):
    mean = lax.optimization_barrier(jnp.mean(x, axis=-1, keepdims=True))
    cent = x - mean
    var = lax.optimization_barrier(jnp.mean(cent * cent, axis=-1, keepdims=True))
    return cent * lax.rsqrt(var + EPS) * gain * (1.0 + scale) + shift

def rotate(t, sign):
    length = t.shape[-3]
    half = t.shape[-1] // 2
    freq = 10000.0 ** (-(jnp.arange(half, dtype=jnp.float32) / half))
    angle = jnp.arange(length, dtype=jnp.float32)[:, None] * freq[None, :]
    cosine = jnp.cos(angle)[:, None, :]
    sine = sign * jnp.sin(angle)[:, None, :]
    first_half = t[..., :half]
    second_half = t[..., half:]
    return jnp.concatenate([first_half * cosine - second_half * sine, second_half * cosine + first_half * sine], axis=-1)

def attend(blocks):
    query, keys, values = blocks
    scores = low_back(jnp.einsum('qhd,khd->hqk', query, keys, precision=HIGH_PRECISION) * 0.125)
    prob = jax.nn.softmax(scores, axis=-1)
    return jnp.einsum('hqk,khd->qhd', low(prob), values, precision=HIGH_PRECISION)

def reference(tokens, cotangent, bucket, mask, time_embed, mask_vec, ln1_gain, w_qkv, w_out, ln2_gain, w_up, b_up, w_down, b_down, w_ada, b_ada):
    cond = jax.nn.silu(time_embed[bucket])
    maskf = mask.astype(jnp.float32).reshape(SEQS, LEN, 1)

    def forward(xin, mvec, gain1, query_key_value_weight, output_weight, gain2, up_weight, up_bias, down_weight, down_bias, wada, bada):
        mods = (jnp.dot(cond, wada, precision=HIGH_PRECISION) + bada).reshape(SEQS, 6, 1, D)
        start = xin.reshape(SEQS, LEN, D) + maskf * mvec
        first_normed = low(modulate(start, gain1, mods[:, 0], mods[:, 1]))
        query_key_value = low_back(jnp.einsum('gov,avh->agoh', first_normed, query_key_value_weight, precision=HIGH_PRECISION))
        query = low(rotate(query_key_value[0].reshape(SEQS, LEN, H, HD), 1.0))
        keys = low(rotate(query_key_value[1].reshape(SEQS, LEN, H, HD), 1.0))
        values = low(query_key_value[2].reshape(SEQS, LEN, H, HD))
        mixed_heads = lax.map(jax.checkpoint(attend), (query, keys, values))
        mixed_heads = low(low_back(mixed_heads.reshape(SEQS, LEN, D)))
        attention_output = low_back(jnp.einsum('mnx,xp->mnp', mixed_heads, output_weight, precision=HIGH_PRECISION))
        middle = start + mods[:, 2] * attention_output
        second_normed = low(modulate(middle, gain2, mods[:, 3], mods[:, 4]))
        preactivation = low_back(jnp.einsum('hoq,qv->hov', second_normed, up_weight, precision=HIGH_PRECISION) + up_bias)
        activated_hidden = low(jax.nn.gelu(preactivation, approximate=True))
        feedforward_output = low_back(jnp.einsum('jox,xe->joe', activated_hidden, down_weight, precision=HIGH_PRECISION) + down_bias)
        return (middle + mods[:, 5] * feedforward_output).reshape(SEQS * LEN, D)
    primals = (tokens.astype(jnp.float32), mask_vec, ln1_gain, w_qkv.astype(jnp.float32), w_out.astype(jnp.float32), ln2_gain, w_up.astype(jnp.float32), b_up, w_down.astype(jnp.float32), b_down, w_ada.astype(jnp.float32), b_ada)
    out, pullback = jax.vjp(forward, *primals)
    grads = pullback(cotangent.astype(jnp.float32))
    return (out.astype(jnp.bfloat16), grads[0].astype(jnp.bfloat16), grads[1], grads[2], grads[3], grads[4], grads[5], grads[6], grads[7], grads[8], grads[9], grads[10], grads[11])
```

```python
import functools

import jax
import jax.numpy as jnp
import numpy as np
from jax import lax
from jax.experimental import pallas as pl
from jax.experimental.pallas import tpu as pltpu
from jax.sharding import PartitionSpec as P

HD = 64
EPS = 1e-05
LOG2E = 1.4426950408889634
C2 = 0.125 * LOG2E
BF = jnp.bfloat16
F32 = jnp.float32
AXES = ("dp", "tensor")
MESH = pl.DeviceIdType.MESH
RB = 256
VMEM_ALL = 62 * 2**20


def dot(a, b, ca=1, cb=0):
    return lax.dot_general(a, b, (((ca,), (cb,)), ((), ())), preferred_element_type=F32)


def sds(shape, dtype):
    return jax.ShapeDtypeStruct(shape, dtype)


def whole(shape):
    return pl.BlockSpec(shape, lambda *_: (0,) * len(shape))


def params(**kw):
    return pltpu.CompilerParams(vmem_limit_bytes=VMEM_ALL, **kw)


def normed(x):
    mean = jnp.mean(x, axis=-1, keepdims=True)
    cent = x - mean
    var = jnp.mean(cent * cent, axis=-1, keepdims=True)
    rs = lax.rsqrt(var + EPS)
    return cent * rs, rs


def mask_column(mask_ref, step, rows):
    m = mask_ref[...].astype(F32).T
    lane = lax.broadcasted_iota(jnp.int32, m.shape, 1)
    per = rows // 128
    parts = [
        jnp.sum(jnp.where(lane == step * per + j, m, 0.0), axis=1, keepdims=True) for j in range(per)
    ]
    return jnp.concatenate(parts, axis=0)


def rope(x, cos, sin):
    lane = lax.broadcasted_iota(jnp.int32, x.shape, 1)
    other = jnp.where(lane % HD < HD // 2, pltpu.roll(x, 128 - HD // 2, 1), pltpu.roll(x, HD // 2, 1))
    return x * cos + other * sin


def project(h, w_ref, cos_ref, sin_ref, q_ref, k_ref, v_ref):
    cos, sin = cos_ref[...], sin_ref[...]
    cols = q_ref.shape[1]
    for i, out in ((0, q_ref), (1, k_ref)):
        y = dot(h, w_ref[i])
        for c in range(0, cols, 128):
            out[:, c : c + 128] = rope(y[:, c : c + 128], cos, sin).astype(BF)
    v_ref[...] = dot(h, w_ref[2]).astype(BF)


def front_kernel(
    bucket, tok, mask, mvec, gain, te, wada, bada, w, cos, sin,
    h_ref, q_ref, k_ref, v_ref, mods_ref, cond_ref, mod_s,
):
    step = pl.program_id(0)

    @pl.when(step == 0)
    def _():
        row = te[...]
        row = row * (1.0 / (1.0 + jnp.exp(-row)))
        sub = lax.broadcasted_iota(jnp.int32, row.shape, 0)
        pick = jnp.sum(jnp.where(sub == bucket[0] % 8, row, 0.0), axis=0, keepdims=True)
        cond_ref[...] = pick
        col = jnp.broadcast_to(pick, (8, pick.shape[1])).T[:, 0:1]
        width = mod_s.shape[1]
        for i in range(6):
            cs = slice(i * width, (i + 1) * width)
            mod_s[i : i + 1, :] = (
                jnp.sum(wada[:, cs].astype(F32) * col, axis=0, keepdims=True) + bada[:, cs]
            )
        mods_ref[...] = mod_s[...]

    x = tok[...].astype(F32) + mask_column(mask, step, tok.shape[0]) * mvec[...]
    n, _ = normed(x)
    h = (n * gain[...] * (1.0 + mod_s[1:2, :]) + mod_s[0:1, :]).astype(BF)
    h_ref[...] = h
    project(h, w, cos, sin, q_ref, k_ref, v_ref)


def front(bucket, tokens, mask2, mvec, gain, te, wada, bada, w, cos, sin):
    rows, width = tokens.shape
    cols = w.shape[2]
    nb = rows // RB
    blk = lambda c: pl.BlockSpec((RB, c), lambda i, b: (i, 0))
    return pl.pallas_call(
        front_kernel,
        grid_spec=pltpu.PrefetchScalarGridSpec(
            num_scalar_prefetch=1,
            grid=(nb,),
            in_specs=[
                blk(width), whole(mask2.shape), whole((1, width)), whole((1, width)),
                pl.BlockSpec((8, te.shape[1]), lambda i, b: (b[0] // 8, 0)),
                whole(wada.shape), whole(bada.shape), whole(w.shape), blk(128), blk(128),
            ],
            out_specs=[
                blk(width), blk(cols), blk(cols), blk(cols), whole((8, width)), whole((1, te.shape[1])),
            ],
            scratch_shapes=[pltpu.VMEM((8, width), F32)],
        ),
        out_shape=[
            sds((rows, width), BF), sds((rows, cols), BF), sds((rows, cols), BF), sds((rows, cols), BF),
            sds((8, width), F32), sds((1, te.shape[1]), F32),
        ],
        compiler_params=params(),
        name="front",
    )(bucket, tokens, mask2, mvec, gain, te, wada, bada, w, cos, sin)


def assemble_kernel(n, pid, *refs):
    slots, (out, stage, sem) = refs[:n], refs[n:]
    rows = slots[0].shape[0]
    copies = []
    for r in range(n):
        at = pl.multiple_of((pid[0] ^ r) * rows, 8)
        copies.append(pltpu.make_async_copy(slots[r], stage.at[pl.ds(at, rows), :], sem.at[r]))
    for c in copies:
        c.start()
    for c in copies:
        c.wait()
    out[...] = stage[...].astype(BF)


def assemble(pid, slots):
    n = len(slots)
    rows, cols = slots[0].shape
    return pl.pallas_call(
        functools.partial(assemble_kernel, n),
        grid_spec=pltpu.PrefetchScalarGridSpec(
            num_scalar_prefetch=1,
            grid=(1,),
            in_specs=[pl.BlockSpec(memory_space=pl.ANY)] * n,
            out_specs=whole((n * rows, cols)),
            scratch_shapes=[pltpu.VMEM((n * rows, cols), F32), pltpu.SemaphoreType.DMA((n,))],
        ),
        out_shape=sds((n * rows, cols), BF),
        compiler_params=params(),
        name="assemble",
    )(pid, *slots)


def project_other_kernel(h, w, cos, sin, q_ref, k_ref, v_ref):
    project(h[...], w, cos, sin, q_ref, k_ref, v_ref)


def project_other(h, w, cos, sin):
    rows, width = h.shape
    cols = w.shape[2]
    blk = lambda c: pl.BlockSpec((RB, c), lambda i: (i, 0))
    return pl.pallas_call(
        project_other_kernel,
        grid=(rows // RB,),
        in_specs=[blk(width), whole(w.shape), blk(128), blk(128)],
        out_specs=[blk(cols)] * 3,
        out_shape=[sds((rows, cols), BF)] * 3,
        compiler_params=params(),
        name="project_other",
    )(h, w, cos, sin)


def attend_kernel(q_ref, k_ref, v_ref, o_ref, lse_ref, oT):
    length = q_ref.shape[0]
    kk = k_ref[...]
    qT, vT = q_ref[...].T, v_ref[...].T
    kf = kk.astype(F32)
    qf = qT.astype(F32)
    ksq = kf * kf
    row = lax.broadcasted_iota(jnp.int32, (128, length), 0)
    lane = lax.broadcasted_iota(jnp.int32, kf.shape, 1)
    for h in range(2):
        hs = slice(h * HD, (h + 1) * HD)
        qm = jnp.where((row < HD) == (h == 0), qT, jnp.zeros_like(qT))
        kn = jnp.max(jnp.sum(jnp.where((lane < HD) == (h == 0), ksq, 0.0), axis=1, keepdims=True))
        qn = jnp.max(jnp.sum(qf[hs, :] * qf[hs, :], axis=0, keepdims=True))
        safe = qn * kn * (C2 * C2) <= 3600.0

        @pl.when(safe)
        def _():
            p = jnp.exp2(dot(kk, qm) * C2)
            total = jnp.sum(p, axis=0, keepdims=True)
            oT[hs, :] = dot(vT[hs, :], p.astype(BF)) * (1.0 / total)
            lse_ref[0, h : h + 1, :] = jnp.log2(total)

        @pl.when(jnp.logical_not(safe))
        def _():
            s = dot(kk, qm)
            top = jnp.max(s, axis=0, keepdims=True)
            p = jnp.exp2((s - top) * C2)
            total = jnp.sum(p, axis=0, keepdims=True)
            oT[hs, :] = dot(vT[hs, :], p.astype(BF)) * (1.0 / total)
            lse_ref[0, h : h + 1, :] = top * C2 + jnp.log2(total)

    o_ref[...] = oT[...].T.astype(BF)


def attend(q, k, v):
    length, cols = q.shape
    pairs = cols // 128
    blk = pl.BlockSpec((length, 128), lambda i: (0, i))
    return pl.pallas_call(
        attend_kernel,
        grid=(pairs,),
        in_specs=[blk] * 3,
        out_specs=[blk, pl.BlockSpec((1, 2, length), lambda i: (i, 0, 0))],
        out_shape=[sds((length, cols), BF), sds((pairs, 2, length), F32)],
        scratch_shapes=[pltpu.VMEM((128, length), F32)],
        compiler_params=params(),
        name="attend",
    )(q, k, v)


def attend_back_kernel(q_ref, k_ref, v_ref, o_ref, do_ref, lse_ref, cosT, sinT, g_ref, gT):
    length = q_ref.shape[0]
    kk, vv = k_ref[...], v_ref[...]
    kT, qT, doT = kk.T, q_ref[...].T, do_ref[...].T
    oT = o_ref[...].T
    prod = doT.astype(F32) * oT.astype(F32)
    row = lax.broadcasted_iota(jnp.int32, (128, length), 0)
    half = HD // 2
    for h in range(2):
        hs = slice(h * HD, (h + 1) * HD)
        sel = (row < HD) == (h == 0)
        qm = jnp.where(sel, qT, jnp.zeros_like(qT))
        dm = jnp.where(sel, doT, jnp.zeros_like(doT))
        inner = jnp.sum(prod[hs, :], axis=0, keepdims=True)
        p = jnp.exp2(dot(kk, qm) * C2 - lse_ref[0, h : h + 1, :])
        ds = (p * (dot(vv, dm) - inner)).astype(BF)
        dv = dot(doT[hs, :], p.astype(BF), 1, 1)
        dk = dot(qT[hs, :], ds, 1, 1) * 0.125
        dq = dot(kT[hs, :], ds) * 0.125
        c, s = cosT[...], sinT[...]
        for i, d in ((0, dq), (1, dk)):
            a, b = d[:half, :], d[half:, :]
            gT[i, h * HD : h * HD + half, :] = a * c + b * s
            gT[i, h * HD + half : (h + 1) * HD, :] = b * c - a * s
        gT[2, hs, :] = dv
    for i in range(3):
        g_ref[i] = gT[i].T.astype(BF)


def attend_back(q, k, v, o, do, lse, cosT, sinT):
    length, cols = q.shape
    pairs = cols // 128
    blk = pl.BlockSpec((length, 128), lambda i: (0, i))
    return pl.pallas_call(
        attend_back_kernel,
        grid=(pairs,),
        in_specs=[blk] * 5
        + [pl.BlockSpec((1, 2, length), lambda i: (i, 0, 0)), whole(cosT.shape), whole(sinT.shape)],
        out_specs=pl.BlockSpec((3, length, 128), lambda i: (0, 0, i)),
        out_shape=sds((3, length, cols), BF),
        scratch_shapes=[pltpu.VMEM((3, 128, length), F32)],
        compiler_params=params(),
        name="attend_back",
    )(q, k, v, o, do, lse, cosT, sinT)


def emit_slots(dp, me, acc, keep, send):
    order = list(range(dp.bit_length() - 1))
    rows = acc.shape[0] // dp
    for first in range(2):

        @pl.when(me % 2 == first)
        def _():
            for b in range(dp):
                rest = (me ^ b) >> 1
                at = sum(((rest >> j) & 1) << (len(order) - 2 - j) for j in range(len(order) - 1))
                target = keep if b % 2 == first else send
                target[pl.ds(at, 1)] = acc[b * rows : (b + 1) * rows, :][None]


def slot_shapes(dp, rows, cols):
    one = sds((dp // 2, rows // dp, cols), F32)
    return [one, one]


def gelu_parts(x):
    c0, c1 = 0.7978845608028654, 0.044715
    x2 = x * x
    t = jnp.tanh(x * (c0 + (c0 * c1) * x2))
    a = 0.5 + 0.5 * t
    d = a + (x * (0.5 - 0.5 * (t * t))) * (c0 + (3.0 * c0 * c1) * x2)
    return x * a, d


def mlp_own_kernel(
    dp, me, tok, mask, mvec, mods, gain, mo, mx, wo, wx, cot, wup, bup, wdown,
    attn_ref, h_ref, feed_ref, gh_ref, gbup_ref, ku, su, kd, sd, accu, accd,
):
    step, last = pl.program_id(0), pl.num_programs(0) - 1
    x = tok[...].astype(F32) + mask_column(mask, step, tok.shape[0]) * mvec[...]
    attn = dot(mo[...], wo[...]) + dot(mx[...], wx[...])
    attn_ref[...] = attn
    n, _ = normed(x + mods[2:3, :] * attn)
    h = (n * gain[...] * (1.0 + mods[4:5, :]) + mods[3:4, :]).astype(BF)
    h_ref[...] = h
    act, slope = gelu_parts(dot(h, wup[...]) + bup[...])
    act = act.astype(BF)
    feed_ref[...] = dot(act, wdown[...])
    gf = (mods[5:6, :] * cot[...].astype(F32)).astype(BF)
    gp = (dot(gf, wdown[...], 1, 1) * slope).astype(BF)
    gh_ref[...] = dot(gp, wup[...], 1, 1)
    gb = jnp.sum(gp.astype(F32), axis=0, keepdims=True)
    du = dot(h, gp, 0, 0)
    dd = dot(gf, act, 0, 0)

    @pl.when(step == 0)
    def _():
        gbup_ref[...] = gb
        accu[...] = du
        accd[...] = dd

    @pl.when(step > 0)
    def _():
        gbup_ref[...] += gb
        accu[...] += du
        accd[...] += dd

    @pl.when(step == last)
    def _():
        emit_slots(dp, me[0], accu, ku, su)
        emit_slots(dp, me[0], accd, kd, sd)


def mlp_own(dp, me, tokens, mask2, mvec, mods, gain, mo, mx, wo, wx, cot, wup, bup, wdown):
    rows, width = tokens.shape
    ff, cols = wup.shape[1], mo.shape[1]
    blk = lambda c: pl.BlockSpec((RB, c), lambda i, b: (i, 0))
    slots = slot_shapes(dp, width, ff)
    sw = whole(slots[0].shape)
    return pl.pallas_call(
        functools.partial(mlp_own_kernel, dp),
        grid_spec=pltpu.PrefetchScalarGridSpec(
            num_scalar_prefetch=1,
            grid=(rows // RB,),
            in_specs=[
                blk(width), whole(mask2.shape), whole((1, width)), whole(mods.shape), whole((1, width)),
                blk(cols), blk(cols), whole(wo.shape), whole(wx.shape), blk(width),
                whole(wup.shape), whole((1, ff)), whole(wdown.shape),
            ],
            out_specs=[blk(width), blk(width), blk(width), blk(width), whole((1, ff)), sw, sw, sw, sw],
            scratch_shapes=[pltpu.VMEM((width, ff), F32), pltpu.VMEM((width, ff), F32)],
        ),
        out_shape=[
            sds((rows, width), F32), sds((rows, width), BF), sds((rows, width), F32), sds((rows, width), F32),
            sds((1, ff), F32), *slots, *slots,
        ],
        compiler_params=params(),
        name="mlp_own",
    )(me, tokens, mask2, mvec, mods, gain, mo, mx, wo, wx, cot, wup, bup, wdown)


def mlp_other_kernel(
    dp, me, tok, mask, mvec, mods, gain, attn_ref, h_ref, feed_ref, gh_ref, cot, wup, bup, wdown, bdown,
    mo, wo, wx, res_ref, gmid_ref, go_ref, gx_ref, sums, kw, sw, acc,
):
    step, last = pl.program_id(0), pl.num_programs(0) - 1

    @pl.when(step == 0)
    def _():
        sums[...] = jnp.zeros_like(sums)

    x = tok[...].astype(F32) + mask_column(mask, step, tok.shape[0]) * mvec[...]
    attn = attn_ref[...]
    middle = x + mods[2:3, :] * attn
    n2, rs = normed(middle)
    act, slope = gelu_parts(dot(h_ref[...], wup[...]) + bup[...])
    feed = (feed_ref[...] + dot(act.astype(BF), wdown[...])) + bdown[...]
    g = cot[...].astype(F32)
    res_ref[...] = (middle + mods[5:6, :] * feed).astype(BF)
    gf = (mods[5:6, :] * g).astype(BF)
    gp = (dot(gf, wdown[...], 1, 1) * slope).astype(BF)
    gh = gh_ref[...] + dot(gp, wup[...], 1, 1)
    e = gh * ((1.0 + mods[4:5, :]) * gain[...])
    inner = jnp.mean(e * n2, axis=-1, keepdims=True)
    gmid = g + (e - jnp.mean(e, axis=-1, keepdims=True) - n2 * inner) * rs
    gmid_ref[...] = gmid
    ga = (mods[2:3, :] * gmid).astype(BF)
    go_ref[...] = dot(ga, wo[...], 1, 1).astype(BF)
    gx_ref[...] = dot(ga, wx[...], 1, 1).astype(BF)
    col = lambda v: jnp.sum(v, axis=0, keepdims=True)
    sums[0:1, :] += col(g * feed)
    sums[1:2, :] += col(gf.astype(F32))
    sums[2:3, :] += col(gh)
    sums[3:4, :] += col(gh * n2)
    sums[4:5, :] += col(gmid * attn)
    dw = dot(ga, mo[...], 0, 0)

    @pl.when(step == 0)
    def _():
        acc[...] = dw

    @pl.when(step > 0)
    def _():
        acc[...] += dw

    @pl.when(step == last)
    def _():
        emit_slots(dp, me[0], acc, kw, sw)


def mlp_other(dp, me, tokens, mask2, mvec, mods, gain, attn, h, feed, gh, cot, wup, bup, wdown, bdown, mo, wo, wx):
    rows, width = tokens.shape
    ff, cols = wup.shape[1], mo.shape[1]
    blk = lambda c: pl.BlockSpec((RB, c), lambda i, b: (i, 0))
    slots = slot_shapes(dp, width, cols)
    sw = whole(slots[0].shape)
    return pl.pallas_call(
        functools.partial(mlp_other_kernel, dp),
        grid_spec=pltpu.PrefetchScalarGridSpec(
            num_scalar_prefetch=1,
            grid=(rows // RB,),
            in_specs=[
                blk(width), whole(mask2.shape), whole((1, width)), whole(mods.shape), whole((1, width)),
                blk(width), blk(width), blk(width), blk(width), blk(width),
                whole(wup.shape), whole((1, ff)), whole(wdown.shape), whole((1, width)),
                blk(cols), whole(wo.shape), whole(wx.shape),
            ],
            out_specs=[blk(width), blk(width), blk(cols), blk(cols), whole((8, width)), sw, sw],
            scratch_shapes=[pltpu.VMEM((width, cols), F32)],
        ),
        out_shape=[
            sds((rows, width), BF), sds((rows, width), F32), sds((rows, cols), BF), sds((rows, cols), BF),
            sds((8, width), F32), *slots,
        ],
        compiler_params=params(),
        name="mlp_other",
    )(me, tokens, mask2, mvec, mods, gain, attn, h, feed, gh, cot, wup, bup, wdown, bdown, mo, wo, wx)


def back_own_kernel(dp, me, h, g, w, part_ref, keep, send, acc):
    step, last = pl.program_id(0), pl.num_programs(0) - 1
    cols = w.shape[2]
    part = dot(g[0], w[0], 1, 1) + dot(g[1], w[1], 1, 1)
    part_ref[...] = part + dot(g[2], w[2], 1, 1)
    for i in range(3):
        d = dot(h[...], g[i], 0, 0)
        at = slice(i * cols, (i + 1) * cols)

        @pl.when(step == 0)
        def _():
            acc[:, at] = d

        @pl.when(step > 0)
        def _():
            acc[:, at] += d

    @pl.when(step == last)
    def _():
        emit_slots(dp, me[0], acc, keep, send)


def back_own(dp, me, h, g, w):
    rows, width = h.shape
    cols = w.shape[2]
    blk = lambda c: pl.BlockSpec((RB, c), lambda i, b: (i, 0))
    slots = slot_shapes(dp, width, 3 * cols)
    sw = whole(slots[0].shape)
    return pl.pallas_call(
        functools.partial(back_own_kernel, dp),
        grid_spec=pltpu.PrefetchScalarGridSpec(
            num_scalar_prefetch=1,
            grid=(rows // RB,),
            in_specs=[blk(width), pl.BlockSpec((3, RB, cols), lambda i, b: (0, i, 0)), whole(w.shape)],
            out_specs=[blk(width), sw, sw],
            scratch_shapes=[pltpu.VMEM((width, 3 * cols), F32)],
        ),
        out_shape=[sds((rows, width), F32), *slots],
        compiler_params=params(),
        name="back_own",
    )(me, h, g, w)


def back_other_kernel(tok, mask, mvec, mods, gain, g, w, part_ref, gmid_ref, gt_ref, sums):
    step = pl.program_id(0)

    @pl.when(step == 0)
    def _():
        sums[...] = jnp.zeros_like(sums)

    m = mask_column(mask, step, tok.shape[0])
    n1, rs = normed(tok[...].astype(F32) + m * mvec[...])
    part = dot(g[0], w[0], 1, 1) + dot(g[1], w[1], 1, 1)
    gh = part_ref[...] + (part + dot(g[2], w[2], 1, 1))
    e = gh * ((1.0 + mods[1:2, :]) * gain[...])
    inner = jnp.mean(e * n1, axis=-1, keepdims=True)
    gs = gmid_ref[...] + (e - jnp.mean(e, axis=-1, keepdims=True) - n1 * inner) * rs
    gt_ref[...] = gs.astype(BF)
    col = lambda v: jnp.sum(v, axis=0, keepdims=True)
    sums[0:1, :] += col(gh)
    sums[1:2, :] += col(gh * n1)
    sums[2:3, :] += col(m * gs)


def back_other(tokens, mask2, mvec, mods, gain, g, w, part, gmid):
    rows, width = tokens.shape
    cols = w.shape[2]
    blk = lambda c: pl.BlockSpec((RB, c), lambda i: (i, 0))
    return pl.pallas_call(
        back_other_kernel,
        grid=(rows // RB,),
        in_specs=[
            blk(width), whole(mask2.shape), whole((1, width)), whole(mods.shape), whole((1, width)),
            pl.BlockSpec((3, RB, cols), lambda i: (0, i, 0)), whole(w.shape), blk(width), blk(width),
        ],
        out_specs=[blk(width), whole((8, width))],
        out_shape=[sds((rows, width), BF), sds((8, width), F32)],
        compiler_params=params(),
        name="back_other",
    )(tokens, mask2, mvec, mods, gain, g, w, part, gmid)


def swap_kernel(dp, x, out, send_sem, recv_sem, own_sem):
    me, t = lax.axis_index("dp"), lax.axis_index("tensor")
    barrier = pltpu.get_barrier_semaphore()

    @pl.loop(1, dp)
    def _(r):
        pl.semaphore_signal(barrier, inc=1, device_id=((me + r) % dp, t), device_id_type=MESH)

    pl.semaphore_wait(barrier, dp - 1)
    own = pltpu.make_async_copy(x.at[me], out.at[me], own_sem)
    own.start()

    def copy(r):
        to = (me + r) % dp
        return pltpu.make_async_remote_copy(
            src_ref=x.at[to],
            dst_ref=out.at[me],
            send_sem=send_sem.at[r],
            recv_sem=recv_sem.at[r],
            device_id=(to, t),
            device_id_type=MESH,
        )

    @pl.loop(1, dp)
    def _(r):
        copy(r).start()

    @pl.loop(1, dp)
    def _(r):
        copy(r).wait()

    own.wait()


def swap(dp, x):
    return pl.pallas_call(
        functools.partial(swap_kernel, dp),
        in_specs=[pl.BlockSpec(memory_space=pltpu.VMEM)],
        out_specs=pl.BlockSpec(memory_space=pltpu.VMEM),
        out_shape=sds(x.shape, F32),
        scratch_shapes=[pltpu.SemaphoreType.DMA((dp,)), pltpu.SemaphoreType.DMA((dp,)), pltpu.SemaphoreType.DMA],
        compiler_params=pltpu.CompilerParams(collective_id=1, has_side_effects=True),
        name="swap",
    )(x)


def flip(dp, bit):
    return [(d * 2 + t, (d ^ (1 << bit)) * 2 + t) for d in range(dp) for t in range(2)]


def flip_tensor(dp):
    return [(d * 2 + t, d * 2 + 1 - t) for d in range(dp) for t in range(2)]


def permute(x, pairs):
    return lax.ppermute(x, AXES, pairs)


def gather_pair(dp, me, first, second):
    core, y, z = (flip(dp, b) for b in range(3))
    across = flip_tensor(dp)

    def piece(w):
        rows = w.shape[0] // 8
        return lax.optimization_barrier(
            lax.dynamic_slice_in_dim(w, (me % 8) * rows, rows, 0).astype(F32)
        )

    a, b = {}, {}
    a[0] = permute(piece(first), across)
    b[0] = permute(piece(second), across)
    a[2], b[4] = permute(a[0], y), permute(b[0], z)
    a[4], b[2] = permute(a[0], z), permute(b[0], y)
    a[6], b[6] = permute(a[2], z), permute(b[4], y)
    for r in (0, 2, 4, 6):
        a[r + 1], b[r + 1] = permute(a[r], core), permute(b[r], core)
    return [a[r] for r in range(8)], [b[r] for r in range(8)]


def reduce_home(dp, keep, send):
    for bit in range(dp.bit_length() - 1):
        got = permute(send, flip(dp, bit))
        half = keep.shape[0] // 2
        if half == 0:
            return (keep + got)[0]
        keep, send = keep[:half] + got[:half], keep[half:] + got[half:]


def rope_tables(length):
    half = HD // 2
    freq = 10000.0 ** (-(np.arange(half, dtype=np.float64) / half))
    angle = np.arange(length, dtype=np.float64)[:, None] * freq[None, :]
    return np.cos(angle).astype(np.float32), np.sin(angle).astype(np.float32)


def body(
    dp, tokens, cotangent, bucket, mask, time_embed, mask_vec, ln1_gain, w_qkv, w_out, ln2_gain,
    w_up, b_up, w_down, b_down, w_ada, b_ada,
):
    rows, width = tokens.shape
    cols, ff = w_out.shape[0], w_up.shape[1]
    me = lax.axis_index("dp").astype(jnp.int32)
    mes = me.reshape(1)
    pid = mes % 8
    line = lambda v: v.reshape(1, -1)
    mvec, gain1, gain2, bdown, bup = map(line, (mask_vec, ln1_gain, ln2_gain, b_down, b_up))
    mask2 = mask.reshape(rows // 128, 128)
    c, s = rope_tables(rows)
    cos, sin = jnp.asarray(np.tile(c, (1, 4))), jnp.asarray(np.tile(np.concatenate([-s, s], 1), (1, 2)))
    cosT, sinT = jnp.asarray(np.ascontiguousarray(c.T)), jnp.asarray(np.ascontiguousarray(s.T))

    flat = w_qkv.reshape(3 * width, cols)
    qa, qb = gather_pair(dp, me, flat[: 3 * width // 2], flat[3 * width // 2 :])
    oa, ob = gather_pair(dp, me, w_out[: cols // 2], w_out[cols // 2 :])
    ua, da = gather_pair(dp, me, w_up, w_down)
    bup_x = permute(bup, flip_tensor(dp))

    h1, q, k, v, mods, cond = front(
        bucket, tokens, mask2, mvec, gain1, time_embed, w_ada, line(b_ada), w_qkv, cos, sin
    )
    mixed, lse = attend(q, k, v)
    wx_qkv = jnp.concatenate([assemble(pid, qa), assemble(pid, qb)]).reshape(3, width, cols)
    qx, kx, vx = project_other(h1, wx_qkv, cos, sin)
    mixed_x, lse_x = attend(qx, kx, vx)
    wx_out = jnp.concatenate([assemble(pid, oa), assemble(pid, ob)])
    attn, h2, feed, gh2, gbup, ku, su, kd, sd = mlp_own(
        dp, mes, tokens, mask2, mvec, mods, gain2, mixed, mixed_x, w_out, wx_out, cotangent, w_up, bup, w_down
    )
    wx_up, wx_down = assemble(pid, ua), assemble(pid, da)
    result, gmid, gmix, gmix_x, sums2, kw, sw = mlp_other(
        dp, mes, tokens, mask2, mvec, mods, gain2, attn, h2, feed, gh2, cotangent,
        wx_up, bup_x, wx_down, bdown, mixed, w_out, wx_out,
    )
    sum_up, sum_down = reduce_home(dp, ku, su), reduce_home(dp, kd, sd)
    g = attend_back(q, k, v, mixed, gmix, lse, cosT, sinT)
    part, kq, sq = back_own(dp, mes, h1, g, w_qkv)
    sum_out = reduce_home(dp, kw, sw)
    sum_qkv = reduce_home(dp, kq, sq)
    gx = attend_back(qx, kx, vx, mixed_x, gmix_x, lse_x, cosT, sinT)
    grad_tokens, sums1 = back_other(tokens, mask2, mvec, mods, gain1, gx, wx_qkv, part, gmid)

    gmod = jnp.concatenate(
        [sums1[0:1], sums1[1:2] * gain1, sums2[4:5], sums2[2:3], sums2[3:4] * gain2, sums2[0:1]], axis=0
    )
    small = [
        sums1[2:3].reshape(dp, -1),
        (sums1[1:2] * (1.0 + mods[1:2])).reshape(dp, -1),
        (sums2[3:4] * (1.0 + mods[4:5])).reshape(dp, -1),
        sums2[1:2].reshape(dp, -1),
        gbup.reshape(dp, -1),
        gmod.reshape(dp, -1),
        jnp.broadcast_to(cond, (dp, cond.shape[1])),
    ]
    sizes = [x.shape[1] for x in small]
    at = np.cumsum([0] + sizes)
    pad = -at[-1] % 128
    packed = jnp.concatenate(small + [jnp.zeros((dp, pad), F32)], axis=1)
    got = swap(dp, packed[:, None, :])[:, 0, :]
    total = jnp.sum(got, axis=0)
    part_of = lambda i: total[at[i] : at[i + 1]]
    sum_mask, sum_ln1, sum_ln2, sum_bdown, sum_bup, sum_bada = (part_of(i) for i in range(6))
    sum_wada = lax.dot_general(
        got[:, at[6] : at[7]], got[:, at[5] : at[6]], (((0,), (0,)), ((), ())),
        precision=lax.Precision.HIGHEST,
    )
    return (
        result,
        grad_tokens,
        sum_mask,
        sum_ln1,
        sum_qkv.reshape(-1, 3, cols).transpose(1, 0, 2),
        sum_out.T,
        sum_ln2,
        sum_up,
        sum_bup,
        sum_down.T,
        sum_bdown,
        sum_wada,
        sum_bada,
    )


def solution(mesh):
    in_specs = (
        P("dp", None), P("dp", None), P("dp"), P("dp"), P(), P(), P(), P(None, None, "tensor"),
        P("tensor", None), P(), P(None, "tensor"), P("tensor"), P("tensor", None), P(), P(), P(),
    )
    out_specs = (
        P("dp", None), P("dp", None), P("dp"), P("dp"), P(None, "dp", "tensor"), P("tensor", "dp"),
        P("dp"), P("dp", "tensor"), P(("tensor", "dp")), P("tensor", "dp"), P("dp"), P(None, "dp"), P("dp"),
    )
    step = functools.partial(body, mesh.shape["dp"])
    return jax.shard_map(step, mesh=mesh, in_specs=in_specs, out_specs=out_specs, check_vma=False)
```

```python
import functools

import jax
import jax.numpy as jnp
import numpy as np
from jax import lax
from jax.experimental import pallas as pl
from jax.experimental.pallas import tpu as pltpu
from jax.sharding import PartitionSpec as P

HD = 64
EPS = 1e-05
LOG2E = 1.4426950408889634
C2 = 0.125 * LOG2E
BF = jnp.bfloat16
F32 = jnp.float32
AXES = ("dp", "tensor")
MESH = pl.DeviceIdType.MESH
RB = 256
VMEM_ALL = 62 * 2**20


def dot(a, b, ca=1, cb=0):
    return lax.dot_general(a, b, (((ca,), (cb,)), ((), ())), preferred_element_type=F32)


def sds(shape, dtype):
    return jax.ShapeDtypeStruct(shape, dtype)


def whole(shape):
    return pl.BlockSpec(shape, lambda *_: (0,) * len(shape))


def params(**kw):
    return pltpu.CompilerParams(vmem_limit_bytes=VMEM_ALL, **kw)


def normed(x):
    mean = jnp.mean(x, axis=-1, keepdims=True)
    cent = x - mean
    var = jnp.mean(cent * cent, axis=-1, keepdims=True)
    rs = lax.rsqrt(var + EPS)
    return cent * rs, rs


def mask_column(mask_ref, step, rows):
    m = mask_ref[...].astype(F32).T
    lane = lax.broadcasted_iota(jnp.int32, m.shape, 1)
    per = rows // 128
    parts = [
        jnp.sum(jnp.where(lane == step * per + j, m, 0.0), axis=1, keepdims=True) for j in range(per)
    ]
    return jnp.concatenate(parts, axis=0)


def flipped(me, bit):
    return me + (1 << bit) * (1 - 2 * ((me // (1 << bit)) % 2))


class Gather:
    ops = 8

    def __init__(self, me, tensor, items, send_sem, recv_sem):
        self.me, self.tensor, self.items, self.send_sem, self.recv_sem = me, tensor, items, send_sem, recv_sem

    def copy(self, i, op):
        src, dst, block, first, rows, yz = self.items[i]
        one, two = (1, 2) if yz else (2, 1)
        piece = self.me % 8
        if op in (4, 5, 7):
            piece = flipped(piece, one)
        if op in (6, 7):
            piece = flipped(piece, two)
        at = dst.at[pl.ds(pl.multiple_of(piece * block + first, 8), rows), :]
        if op == 0:
            device = {"tensor": 1 - self.tensor}
        else:
            bit = {1: 0, 2: one, 3: two, 4: two, 5: 0, 6: 0, 7: 0}[op]
            device = {"dp": flipped(self.me, bit)}
        k = i * self.ops + op
        return pltpu.make_async_remote_copy(
            src_ref=src.at[pl.ds(first, rows), :] if op == 0 else at,
            dst_ref=at,
            send_sem=self.send_sem.at[k],
            recv_sem=self.recv_sem.at[k],
            device_id=device,
            device_id_type=MESH,
        )

    def stage(self, i, s):
        waits = {0: (), 1: (0,), 2: (2,), 3: (3, 4), 4: (1, 5, 6, 7)}[s]
        starts = {0: (0,), 1: (2, 3, 1), 2: (4, 5), 3: (6, 7), 4: ()}[s]
        for op in waits:
            self.copy(i, op).wait_recv()
        for op in starts:
            self.copy(i, op).start()
        if s == 4:
            for op in range(self.ops):
                self.copy(i, op).wait_send()


def greet_gather(me, tensor):
    barrier = pltpu.get_barrier_semaphore()
    pl.semaphore_signal(barrier, inc=1, device_id={"tensor": 1 - tensor}, device_id_type=MESH)
    for bit in range(3):
        pl.semaphore_signal(barrier, inc=1, device_id={"dp": flipped(me, bit)}, device_id_type=MESH)
    pl.semaphore_wait(barrier, 4)


def rope(x, cos, sin):
    lane = lax.broadcasted_iota(jnp.int32, x.shape, 1)
    other = jnp.where(lane % HD < HD // 2, pltpu.roll(x, 128 - HD // 2, 1), pltpu.roll(x, HD // 2, 1))
    return x * cos + other * sin


def project(h, w_ref, cos_ref, sin_ref, q_ref, k_ref, v_ref):
    cos, sin = cos_ref[...], sin_ref[...]
    cols = q_ref.shape[1]
    for i, out in ((0, q_ref), (1, k_ref)):
        y = dot(h, w_ref[i])
        for c in range(0, cols, 128):
            out[:, c : c + 128] = rope(y[:, c : c + 128], cos, sin).astype(BF)
    v_ref[...] = dot(h, w_ref[2]).astype(BF)


def attend_pair(q_ref, k_ref, v_ref, at, o_ref, lse_ref, pair, oT, sbuf):
    length = q_ref.shape[0]
    wide = sbuf.shape[2]
    kk = k_ref[:, at]
    qT, vT = q_ref[:, at].T, v_ref[:, at].T
    row = lax.broadcasted_iota(jnp.int32, (128, wide), 0)
    items = [(h, c) for h in range(2) for c in range(0, length, wide)]

    def scores(i):
        h, c = items[i]
        qq = qT[:, c : c + wide]
        s = dot(kk, jnp.where((row < HD) == (h == 0), qq, jnp.zeros_like(qq)))
        sbuf[i % 2] = s
        return jnp.max(s, axis=0, keepdims=True)

    top = scores(0)
    for i, (h, c) in enumerate(items):
        following = scores(i + 1) if i + 1 < len(items) else None
        p = jnp.exp2((sbuf[i % 2] - top) * C2)
        total = jnp.sum(p, axis=0, keepdims=True)
        oT[h * HD : (h + 1) * HD, c : c + wide] = dot(vT[h * HD : (h + 1) * HD, :], p.astype(BF)) * (1.0 / total)
        lse_ref[pl.ds(pair, 1), h : h + 1, c : c + wide] = (top * C2 + jnp.log2(total))[None]
        top = following
    o_ref[:, at] = oT[...].T.astype(BF)


def front_kernel(
    nb, plan, bucket, tok, mask, mvec, gain, te, wada, bada, w, cos, sin, pq, po,
    h_ref, q_ref, k_ref, v_ref, mods_ref, cond_ref, o_ref, lse_ref, fq, fo,
    mod_s, oT, sbuf, send_sem, recv_sem,
):
    step = pl.program_id(0)
    me, tensor = lax.axis_index("dp"), lax.axis_index("tensor")
    bq, bo = pq.shape[0], po.shape[0]
    items = [(pq, fq, bq, i * (bq // 4), bq // 4, i % 2 == 0) for i in range(4)]
    items += [(po, fo, bo, i * (bo // 2), bo // 2, i == 0) for i in range(2)]
    gather = Gather(me, tensor, items, send_sem, recv_sem)

    @pl.when(step == 0)
    def _():
        greet_gather(me, tensor)

    for at, todo in plan.items():

        @pl.when(step == at)
        def _():
            for i, s in todo:
                gather.stage(i, s)

    @pl.when(step == 0)
    def _():
        row = te[...]
        row = row * (1.0 / (1.0 + jnp.exp(-row)))
        sub = lax.broadcasted_iota(jnp.int32, row.shape, 0)
        pick = jnp.sum(jnp.where(sub == bucket[...] % 8, row, 0.0), axis=0, keepdims=True)
        cond_ref[...] = pick
        col = jnp.broadcast_to(pick, (8, pick.shape[1])).T[:, 0:1]
        width = mod_s.shape[1]
        for i in range(6):
            cs = slice(i * width, (i + 1) * width)
            mod_s[i : i + 1, :] = (
                jnp.sum(wada[:, cs].astype(F32) * col, axis=0, keepdims=True) + bada[:, cs]
            )
        mods_ref[...] = mod_s[...]

    @pl.when(step < nb)
    def _():
        x = tok[...].astype(F32) + mask_column(mask, step, tok.shape[0]) * mvec[...]
        n, _ = normed(x)
        h = (n * gain[...] * (1.0 + mod_s[1:2, :]) + mod_s[0:1, :]).astype(BF)
        h_ref[...] = h
        rows = pl.ds(pl.multiple_of(step * RB, RB), RB)
        project(h, w, cos, sin, q_ref.at[rows, :], k_ref.at[rows, :], v_ref.at[rows, :])

    @pl.when(step >= nb)
    def _():
        pair = step - nb
        attend_pair(q_ref, k_ref, v_ref, pl.ds(pl.multiple_of(pair * 128, 128), 128), o_ref, lse_ref, pair, oT, sbuf)

    @pl.when(step == pl.num_programs(0) - 1)
    def _():
        for i in range(len(items)):
            gather.stage(i, 4)


def front(bucket, tokens, mask2, mvec, gain, te, wada, bada, w, cos, sin, piece_qkv, piece_out):
    rows, width = tokens.shape
    cols = w.shape[2]
    nb, pairs = rows // RB, cols // 128
    plan = {
        0: [(i, 0) for i in range(6)],
        2: [(0, 1), (1, 1)],
        3: [(2, 1), (3, 1)],
        4: [(0, 2), (1, 2), (4, 1), (5, 1)],
        5: [(0, 3), (1, 3), (2, 2), (3, 2)],
        6: [(2, 3), (3, 3), (4, 2), (5, 2), (4, 3), (5, 3)],
    }
    blk = lambda c: pl.BlockSpec((RB, c), lambda i: (jnp.minimum(i, nb - 1), 0))
    anys = pl.BlockSpec(memory_space=pl.ANY)
    fq = (8 * piece_qkv.shape[0], piece_qkv.shape[1])
    fo = (8 * piece_out.shape[0], piece_out.shape[1])
    act = (rows, cols)
    return pl.pallas_call(
        functools.partial(front_kernel, nb, plan),
        grid=(nb + pairs,),
        in_specs=[
            whole((1, 1)), blk(width), whole(mask2.shape), whole((1, width)), whole((1, width)),
            whole(te.shape), whole(wada.shape), whole(bada.shape), whole(w.shape), blk(128), blk(128),
            anys, anys,
        ],
        out_specs=[
            blk(width), whole(act), whole(act), whole(act), whole((8, width)), whole((1, te.shape[1])),
            whole(act), whole((pairs, 2, rows)), anys, anys,
        ],
        scratch_shapes=[
            pltpu.VMEM((8, width), F32), pltpu.VMEM((128, rows), F32), pltpu.VMEM((2, rows, 512), F32),
            pltpu.SemaphoreType.DMA((48,)), pltpu.SemaphoreType.DMA((48,)),
        ],
        out_shape=[
            sds((rows, width), BF), sds(act, BF), sds(act, BF), sds(act, BF),
            sds((8, width), F32), sds((1, te.shape[1]), F32), sds(act, BF), sds((pairs, 2, rows), F32),
            sds(fq, F32), sds(fo, F32),
        ],
        compiler_params=params(collective_id=2, has_side_effects=True),
        name="front",
    )(bucket, tokens, mask2, mvec, gain, te, wada, bada, w, cos, sin, piece_qkv, piece_out)


def assemble_kernel(n, pid, *refs):
    slots, (out, stage, sem) = refs[:n], refs[n:]
    rows = slots[0].shape[0]
    copies = []
    for r in range(n):
        at = pl.multiple_of((pid[0] ^ r) * rows, 8)
        copies.append(pltpu.make_async_copy(slots[r], stage.at[pl.ds(at, rows), :], sem.at[r]))
    for c in copies:
        c.start()
    for c in copies:
        c.wait()
    out[...] = stage[...].astype(BF)


def assemble(pid, slots):
    n = len(slots)
    rows, cols = slots[0].shape
    return pl.pallas_call(
        functools.partial(assemble_kernel, n),
        grid_spec=pltpu.PrefetchScalarGridSpec(
            num_scalar_prefetch=1,
            grid=(1,),
            in_specs=[pl.BlockSpec(memory_space=pl.ANY)] * n,
            out_specs=whole((n * rows, cols)),
            scratch_shapes=[pltpu.VMEM((n * rows, cols), F32), pltpu.SemaphoreType.DMA((n,))],
        ),
        out_shape=sds((n * rows, cols), BF),
        compiler_params=params(),
        name="assemble",
    )(pid, *slots)


def project_other_kernel(h, w, cos, sin, q_ref, k_ref, v_ref):
    project(h[...], w, cos, sin, q_ref, k_ref, v_ref)


def project_other(h, w, cos, sin):
    rows, width = h.shape
    cols = w.shape[2]
    blk = lambda c: pl.BlockSpec((RB, c), lambda i: (i, 0))
    return pl.pallas_call(
        project_other_kernel,
        grid=(rows // RB,),
        in_specs=[blk(width), whole(w.shape), blk(128), blk(128)],
        out_specs=[blk(cols)] * 3,
        out_shape=[sds((rows, cols), BF)] * 3,
        compiler_params=params(),
        name="project_other",
    )(h, w, cos, sin)


def attend_kernel(q_ref, k_ref, v_ref, o_ref, lse_ref, oT):
    length = q_ref.shape[0]
    kk = k_ref[...]
    qT, vT = q_ref[...].T, v_ref[...].T
    kf = kk.astype(F32)
    qf = qT.astype(F32)
    ksq = kf * kf
    row = lax.broadcasted_iota(jnp.int32, (128, length), 0)
    lane = lax.broadcasted_iota(jnp.int32, kf.shape, 1)
    for h in range(2):
        hs = slice(h * HD, (h + 1) * HD)
        qm = jnp.where((row < HD) == (h == 0), qT, jnp.zeros_like(qT))
        kn = jnp.max(jnp.sum(jnp.where((lane < HD) == (h == 0), ksq, 0.0), axis=1, keepdims=True))
        qn = jnp.max(jnp.sum(qf[hs, :] * qf[hs, :], axis=0, keepdims=True))
        safe = qn * kn * (C2 * C2) <= 3600.0

        @pl.when(safe)
        def _():
            p = jnp.exp2(dot(kk, qm) * C2)
            total = jnp.sum(p, axis=0, keepdims=True)
            oT[hs, :] = dot(vT[hs, :], p.astype(BF)) * (1.0 / total)
            lse_ref[0, h : h + 1, :] = jnp.log2(total)

        @pl.when(jnp.logical_not(safe))
        def _():
            s = dot(kk, qm)
            top = jnp.max(s, axis=0, keepdims=True)
            p = jnp.exp2((s - top) * C2)
            total = jnp.sum(p, axis=0, keepdims=True)
            oT[hs, :] = dot(vT[hs, :], p.astype(BF)) * (1.0 / total)
            lse_ref[0, h : h + 1, :] = top * C2 + jnp.log2(total)

    o_ref[...] = oT[...].T.astype(BF)


def attend(q, k, v):
    length, cols = q.shape
    pairs = cols // 128
    blk = pl.BlockSpec((length, 128), lambda i: (0, i))
    return pl.pallas_call(
        attend_kernel,
        grid=(pairs,),
        in_specs=[blk] * 3,
        out_specs=[blk, pl.BlockSpec((1, 2, length), lambda i: (i, 0, 0))],
        out_shape=[sds((length, cols), BF), sds((pairs, 2, length), F32)],
        scratch_shapes=[pltpu.VMEM((128, length), F32)],
        compiler_params=params(),
        name="attend",
    )(q, k, v)


def attend_back_kernel(q_ref, k_ref, v_ref, o_ref, do_ref, lse_ref, cosT, sinT, g_ref, gT):
    length = q_ref.shape[0]
    kk, vv = k_ref[...], v_ref[...]
    kT, qT, doT = kk.T, q_ref[...].T, do_ref[...].T
    oT = o_ref[...].T
    prod = doT.astype(F32) * oT.astype(F32)
    row = lax.broadcasted_iota(jnp.int32, (128, length), 0)
    half = HD // 2
    for h in range(2):
        hs = slice(h * HD, (h + 1) * HD)
        sel = (row < HD) == (h == 0)
        qm = jnp.where(sel, qT, jnp.zeros_like(qT))
        dm = jnp.where(sel, doT, jnp.zeros_like(doT))
        inner = jnp.sum(prod[hs, :], axis=0, keepdims=True)
        p = jnp.exp2(dot(kk, qm) * C2 - lse_ref[0, h : h + 1, :])
        ds = (p * (dot(vv, dm) - inner)).astype(BF)
        dv = dot(doT[hs, :], p.astype(BF), 1, 1)
        dk = dot(qT[hs, :], ds, 1, 1) * 0.125
        dq = dot(kT[hs, :], ds) * 0.125
        c, s = cosT[...], sinT[...]
        for i, d in ((0, dq), (1, dk)):
            a, b = d[:half, :], d[half:, :]
            gT[i, h * HD : h * HD + half, :] = a * c + b * s
            gT[i, h * HD + half : (h + 1) * HD, :] = b * c - a * s
        gT[2, hs, :] = dv
    for i in range(3):
        g_ref[i] = gT[i].T.astype(BF)


def attend_back(q, k, v, o, do, lse, cosT, sinT):
    length, cols = q.shape
    pairs = cols // 128
    blk = pl.BlockSpec((length, 128), lambda i: (0, i))
    return pl.pallas_call(
        attend_back_kernel,
        grid=(pairs,),
        in_specs=[blk] * 5
        + [pl.BlockSpec((1, 2, length), lambda i: (i, 0, 0)), whole(cosT.shape), whole(sinT.shape)],
        out_specs=pl.BlockSpec((3, length, 128), lambda i: (0, 0, i)),
        out_shape=sds((3, length, cols), BF),
        scratch_shapes=[pltpu.VMEM((3, 128, length), F32)],
        compiler_params=params(),
        name="attend_back",
    )(q, k, v, o, do, lse, cosT, sinT)


def emit_slots(dp, me, acc, keep, send):
    order = list(range(dp.bit_length() - 1))
    rows = acc.shape[0] // dp
    for first in range(2):

        @pl.when(me % 2 == first)
        def _():
            for b in range(dp):
                rest = (me ^ b) >> 1
                at = sum(((rest >> j) & 1) << (len(order) - 2 - j) for j in range(len(order) - 1))
                target = keep if b % 2 == first else send
                target[pl.ds(at, 1)] = acc[b * rows : (b + 1) * rows, :][None]


def slot_shapes(dp, rows, cols):
    one = sds((dp // 2, rows // dp, cols), F32)
    return [one, one]


def gelu_parts(x):
    c0, c1 = 0.7978845608028654, 0.044715
    x2 = x * x
    t = jnp.tanh(x * (c0 + (c0 * c1) * x2))
    a = 0.5 + 0.5 * t
    d = a + (x * (0.5 - 0.5 * (t * t))) * (c0 + (3.0 * c0 * c1) * x2)
    return x * a, d


def mlp_own_kernel(
    dp, me, tok, mask, mvec, mods, gain, mo, mx, wo, wx, cot, wup, bup, wdown,
    attn_ref, h_ref, feed_ref, gh_ref, gbup_ref, ku, su, kd, sd, accu, accd,
):
    step, last = pl.program_id(0), pl.num_programs(0) - 1
    x = tok[...].astype(F32) + mask_column(mask, step, tok.shape[0]) * mvec[...]
    attn = dot(mo[...], wo[...]) + dot(mx[...], wx[...])
    attn_ref[...] = attn
    n, _ = normed(x + mods[2:3, :] * attn)
    h = (n * gain[...] * (1.0 + mods[4:5, :]) + mods[3:4, :]).astype(BF)
    h_ref[...] = h
    act, slope = gelu_parts(dot(h, wup[...]) + bup[...])
    act = act.astype(BF)
    feed_ref[...] = dot(act, wdown[...])
    gf = (mods[5:6, :] * cot[...].astype(F32)).astype(BF)
    gp = (dot(gf, wdown[...], 1, 1) * slope).astype(BF)
    gh_ref[...] = dot(gp, wup[...], 1, 1)
    gb = jnp.sum(gp.astype(F32), axis=0, keepdims=True)
    du = dot(h, gp, 0, 0)
    dd = dot(gf, act, 0, 0)

    @pl.when(step == 0)
    def _():
        gbup_ref[...] = gb
        accu[...] = du
        accd[...] = dd

    @pl.when(step > 0)
    def _():
        gbup_ref[...] += gb
        accu[...] += du
        accd[...] += dd

    @pl.when(step == last)
    def _():
        emit_slots(dp, me[0], accu, ku, su)
        emit_slots(dp, me[0], accd, kd, sd)


def mlp_own(dp, me, tokens, mask2, mvec, mods, gain, mo, mx, wo, wx, cot, wup, bup, wdown):
    rows, width = tokens.shape
    ff, cols = wup.shape[1], mo.shape[1]
    blk = lambda c: pl.BlockSpec((RB, c), lambda i, b: (i, 0))
    slots = slot_shapes(dp, width, ff)
    sw = whole(slots[0].shape)
    return pl.pallas_call(
        functools.partial(mlp_own_kernel, dp),
        grid_spec=pltpu.PrefetchScalarGridSpec(
            num_scalar_prefetch=1,
            grid=(rows // RB,),
            in_specs=[
                blk(width), whole(mask2.shape), whole((1, width)), whole(mods.shape), whole((1, width)),
                blk(cols), blk(cols), whole(wo.shape), whole(wx.shape), blk(width),
                whole(wup.shape), whole((1, ff)), whole(wdown.shape),
            ],
            out_specs=[blk(width), blk(width), blk(width), blk(width), whole((1, ff)), sw, sw, sw, sw],
            scratch_shapes=[pltpu.VMEM((width, ff), F32), pltpu.VMEM((width, ff), F32)],
        ),
        out_shape=[
            sds((rows, width), F32), sds((rows, width), BF), sds((rows, width), F32), sds((rows, width), F32),
            sds((1, ff), F32), *slots, *slots,
        ],
        compiler_params=params(),
        name="mlp_own",
    )(me, tokens, mask2, mvec, mods, gain, mo, mx, wo, wx, cot, wup, bup, wdown)


def mlp_other_kernel(
    dp, me, tok, mask, mvec, mods, gain, attn_ref, h_ref, feed_ref, gh_ref, cot, wup, bup, wdown, bdown,
    mo, wo, wx, res_ref, gmid_ref, go_ref, gx_ref, sums, kw, sw, acc,
):
    step, last = pl.program_id(0), pl.num_programs(0) - 1

    @pl.when(step == 0)
    def _():
        sums[...] = jnp.zeros_like(sums)

    x = tok[...].astype(F32) + mask_column(mask, step, tok.shape[0]) * mvec[...]
    attn = attn_ref[...]
    middle = x + mods[2:3, :] * attn
    n2, rs = normed(middle)
    act, slope = gelu_parts(dot(h_ref[...], wup[...]) + bup[...])
    feed = (feed_ref[...] + dot(act.astype(BF), wdown[...])) + bdown[...]
    g = cot[...].astype(F32)
    res_ref[...] = (middle + mods[5:6, :] * feed).astype(BF)
    gf = (mods[5:6, :] * g).astype(BF)
    gp = (dot(gf, wdown[...], 1, 1) * slope).astype(BF)
    gh = gh_ref[...] + dot(gp, wup[...], 1, 1)
    e = gh * ((1.0 + mods[4:5, :]) * gain[...])
    inner = jnp.mean(e * n2, axis=-1, keepdims=True)
    gmid = g + (e - jnp.mean(e, axis=-1, keepdims=True) - n2 * inner) * rs
    gmid_ref[...] = gmid
    ga = (mods[2:3, :] * gmid).astype(BF)
    go_ref[...] = dot(ga, wo[...], 1, 1).astype(BF)
    gx_ref[...] = dot(ga, wx[...], 1, 1).astype(BF)
    col = lambda v: jnp.sum(v, axis=0, keepdims=True)
    sums[0:1, :] += col(g * feed)
    sums[1:2, :] += col(gf.astype(F32))
    sums[2:3, :] += col(gh)
    sums[3:4, :] += col(gh * n2)
    sums[4:5, :] += col(gmid * attn)
    dw = dot(ga, mo[...], 0, 0)

    @pl.when(step == 0)
    def _():
        acc[...] = dw

    @pl.when(step > 0)
    def _():
        acc[...] += dw

    @pl.when(step == last)
    def _():
        emit_slots(dp, me[0], acc, kw, sw)


def mlp_other(dp, me, tokens, mask2, mvec, mods, gain, attn, h, feed, gh, cot, wup, bup, wdown, bdown, mo, wo, wx):
    rows, width = tokens.shape
    ff, cols = wup.shape[1], mo.shape[1]
    blk = lambda c: pl.BlockSpec((RB, c), lambda i, b: (i, 0))
    slots = slot_shapes(dp, width, cols)
    sw = whole(slots[0].shape)
    return pl.pallas_call(
        functools.partial(mlp_other_kernel, dp),
        grid_spec=pltpu.PrefetchScalarGridSpec(
            num_scalar_prefetch=1,
            grid=(rows // RB,),
            in_specs=[
                blk(width), whole(mask2.shape), whole((1, width)), whole(mods.shape), whole((1, width)),
                blk(width), blk(width), blk(width), blk(width), blk(width),
                whole(wup.shape), whole((1, ff)), whole(wdown.shape), whole((1, width)),
                blk(cols), whole(wo.shape), whole(wx.shape),
            ],
            out_specs=[blk(width), blk(width), blk(cols), blk(cols), whole((8, width)), sw, sw],
            scratch_shapes=[pltpu.VMEM((width, cols), F32)],
        ),
        out_shape=[
            sds((rows, width), BF), sds((rows, width), F32), sds((rows, cols), BF), sds((rows, cols), BF),
            sds((8, width), F32), *slots,
        ],
        compiler_params=params(),
        name="mlp_other",
    )(me, tokens, mask2, mvec, mods, gain, attn, h, feed, gh, cot, wup, bup, wdown, bdown, mo, wo, wx)


def back_own_kernel(dp, me, h, g, w, part_ref, keep, send, acc):
    step, last = pl.program_id(0), pl.num_programs(0) - 1
    cols = w.shape[2]
    part = dot(g[0], w[0], 1, 1) + dot(g[1], w[1], 1, 1)
    part_ref[...] = part + dot(g[2], w[2], 1, 1)
    for i in range(3):
        d = dot(h[...], g[i], 0, 0)
        at = slice(i * cols, (i + 1) * cols)

        @pl.when(step == 0)
        def _():
            acc[:, at] = d

        @pl.when(step > 0)
        def _():
            acc[:, at] += d

    @pl.when(step == last)
    def _():
        emit_slots(dp, me[0], acc, keep, send)


def back_own(dp, me, h, g, w):
    rows, width = h.shape
    cols = w.shape[2]
    blk = lambda c: pl.BlockSpec((RB, c), lambda i, b: (i, 0))
    slots = slot_shapes(dp, width, 3 * cols)
    sw = whole(slots[0].shape)
    return pl.pallas_call(
        functools.partial(back_own_kernel, dp),
        grid_spec=pltpu.PrefetchScalarGridSpec(
            num_scalar_prefetch=1,
            grid=(rows // RB,),
            in_specs=[blk(width), pl.BlockSpec((3, RB, cols), lambda i, b: (0, i, 0)), whole(w.shape)],
            out_specs=[blk(width), sw, sw],
            scratch_shapes=[pltpu.VMEM((width, 3 * cols), F32)],
        ),
        out_shape=[sds((rows, width), F32), *slots],
        compiler_params=params(),
        name="back_own",
    )(me, h, g, w)


def back_other_kernel(tok, mask, mvec, mods, gain, g, w, part_ref, gmid_ref, gt_ref, sums):
    step = pl.program_id(0)

    @pl.when(step == 0)
    def _():
        sums[...] = jnp.zeros_like(sums)

    m = mask_column(mask, step, tok.shape[0])
    n1, rs = normed(tok[...].astype(F32) + m * mvec[...])
    part = dot(g[0], w[0], 1, 1) + dot(g[1], w[1], 1, 1)
    gh = part_ref[...] + (part + dot(g[2], w[2], 1, 1))
    e = gh * ((1.0 + mods[1:2, :]) * gain[...])
    inner = jnp.mean(e * n1, axis=-1, keepdims=True)
    gs = gmid_ref[...] + (e - jnp.mean(e, axis=-1, keepdims=True) - n1 * inner) * rs
    gt_ref[...] = gs.astype(BF)
    col = lambda v: jnp.sum(v, axis=0, keepdims=True)
    sums[0:1, :] += col(gh)
    sums[1:2, :] += col(gh * n1)
    sums[2:3, :] += col(m * gs)


def back_other(tokens, mask2, mvec, mods, gain, g, w, part, gmid):
    rows, width = tokens.shape
    cols = w.shape[2]
    blk = lambda c: pl.BlockSpec((RB, c), lambda i: (i, 0))
    return pl.pallas_call(
        back_other_kernel,
        grid=(rows // RB,),
        in_specs=[
            blk(width), whole(mask2.shape), whole((1, width)), whole(mods.shape), whole((1, width)),
            pl.BlockSpec((3, RB, cols), lambda i: (0, i, 0)), whole(w.shape), blk(width), blk(width),
        ],
        out_specs=[blk(width), whole((8, width))],
        out_shape=[sds((rows, width), BF), sds((8, width), F32)],
        compiler_params=params(),
        name="back_other",
    )(tokens, mask2, mvec, mods, gain, g, w, part, gmid)


def swap_kernel(dp, x, out, send_sem, recv_sem, own_sem):
    me, t = lax.axis_index("dp"), lax.axis_index("tensor")
    barrier = pltpu.get_barrier_semaphore()

    @pl.loop(1, dp)
    def _(r):
        pl.semaphore_signal(barrier, inc=1, device_id=((me + r) % dp, t), device_id_type=MESH)

    pl.semaphore_wait(barrier, dp - 1)
    own = pltpu.make_async_copy(x.at[me], out.at[me], own_sem)
    own.start()

    def copy(r):
        to = (me + r) % dp
        return pltpu.make_async_remote_copy(
            src_ref=x.at[to],
            dst_ref=out.at[me],
            send_sem=send_sem.at[r],
            recv_sem=recv_sem.at[r],
            device_id=(to, t),
            device_id_type=MESH,
        )

    @pl.loop(1, dp)
    def _(r):
        copy(r).start()

    @pl.loop(1, dp)
    def _(r):
        copy(r).wait()

    own.wait()


def swap(dp, x):
    return pl.pallas_call(
        functools.partial(swap_kernel, dp),
        in_specs=[pl.BlockSpec(memory_space=pltpu.VMEM)],
        out_specs=pl.BlockSpec(memory_space=pltpu.VMEM),
        out_shape=sds(x.shape, F32),
        scratch_shapes=[pltpu.SemaphoreType.DMA((dp,)), pltpu.SemaphoreType.DMA((dp,)), pltpu.SemaphoreType.DMA],
        compiler_params=pltpu.CompilerParams(collective_id=1, has_side_effects=True),
        name="swap",
    )(x)


def flip(dp, bit):
    return [(d * 2 + t, (d ^ (1 << bit)) * 2 + t) for d in range(dp) for t in range(2)]


def flip_tensor(dp):
    return [(d * 2 + t, d * 2 + 1 - t) for d in range(dp) for t in range(2)]


def permute(x, pairs):
    return lax.ppermute(x, AXES, pairs)


def gather_pair(dp, me, first, second):
    core, y, z = (flip(dp, b) for b in range(3))
    across = flip_tensor(dp)

    def piece(w):
        rows = w.shape[0] // 8
        return lax.optimization_barrier(
            lax.dynamic_slice_in_dim(w, (me % 8) * rows, rows, 0).astype(F32)
        )

    a, b = {}, {}
    a[0] = permute(piece(first), across)
    b[0] = permute(piece(second), across)
    a[2], b[4] = permute(a[0], y), permute(b[0], z)
    a[4], b[2] = permute(a[0], z), permute(b[0], y)
    a[6], b[6] = permute(a[2], z), permute(b[4], y)
    for r in (0, 2, 4, 6):
        a[r + 1], b[r + 1] = permute(a[r], core), permute(b[r], core)
    return [a[r] for r in range(8)], [b[r] for r in range(8)]


def reduce_home(dp, keep, send):
    for bit in range(dp.bit_length() - 1):
        got = permute(send, flip(dp, bit))
        half = keep.shape[0] // 2
        if half == 0:
            return (keep + got)[0]
        keep, send = keep[:half] + got[:half], keep[half:] + got[half:]


def rope_tables(length):
    half = HD // 2
    freq = 10000.0 ** (-(np.arange(half, dtype=np.float64) / half))
    angle = np.arange(length, dtype=np.float64)[:, None] * freq[None, :]
    return np.cos(angle).astype(np.float32), np.sin(angle).astype(np.float32)


def body(
    dp, tokens, cotangent, bucket, mask, time_embed, mask_vec, ln1_gain, w_qkv, w_out, ln2_gain,
    w_up, b_up, w_down, b_down, w_ada, b_ada,
):
    rows, width = tokens.shape
    cols, ff = w_out.shape[0], w_up.shape[1]
    me = lax.axis_index("dp").astype(jnp.int32)
    mes = me.reshape(1)
    pid = mes % 8
    line = lambda v: v.reshape(1, -1)
    mvec, gain1, gain2, bdown, bup = map(line, (mask_vec, ln1_gain, ln2_gain, b_down, b_up))
    mask2 = mask.reshape(rows // 128, 128)
    c, s = rope_tables(rows)
    cos, sin = jnp.asarray(np.tile(c, (1, 4))), jnp.asarray(np.tile(np.concatenate([-s, s], 1), (1, 2)))
    cosT, sinT = jnp.asarray(np.ascontiguousarray(c.T)), jnp.asarray(np.ascontiguousarray(s.T))

    flat = w_qkv.reshape(3 * width, cols)

    def piece(w):
        n = w.shape[0] // 8
        return lax.optimization_barrier(lax.dynamic_slice_in_dim(w, (me % 8) * n, n, 0).astype(F32))

    ua, da = gather_pair(dp, me, w_up, w_down)
    bup_x = permute(bup, flip_tensor(dp))

    te_row = lax.dynamic_slice_in_dim(time_embed, (bucket[0] // 8) * 8, 8, 0)
    h1, q, k, v, mods, cond, mixed, lse, wx_qkv, wx_out = front(
        bucket.reshape(1, 1), tokens, mask2, mvec, gain1, te_row, w_ada, line(b_ada), w_qkv, cos, sin,
        piece(flat), piece(w_out),
    )
    wx_qkv, wx_out = wx_qkv.astype(BF).reshape(3, width, cols), wx_out.astype(BF)
    qx, kx, vx = project_other(h1, wx_qkv, cos, sin)
    mixed_x, lse_x = attend(qx, kx, vx)
    attn, h2, feed, gh2, gbup, ku, su, kd, sd = mlp_own(
        dp, mes, tokens, mask2, mvec, mods, gain2, mixed, mixed_x, w_out, wx_out, cotangent, w_up, bup, w_down
    )
    wx_up, wx_down = assemble(pid, ua), assemble(pid, da)
    result, gmid, gmix, gmix_x, sums2, kw, sw = mlp_other(
        dp, mes, tokens, mask2, mvec, mods, gain2, attn, h2, feed, gh2, cotangent,
        wx_up, bup_x, wx_down, bdown, mixed, w_out, wx_out,
    )
    sum_up, sum_down = reduce_home(dp, ku, su), reduce_home(dp, kd, sd)
    g = attend_back(q, k, v, mixed, gmix, lse, cosT, sinT)
    part, kq, sq = back_own(dp, mes, h1, g, w_qkv)
    sum_out = reduce_home(dp, kw, sw)
    sum_qkv = reduce_home(dp, kq, sq)
    gx = attend_back(qx, kx, vx, mixed_x, gmix_x, lse_x, cosT, sinT)
    grad_tokens, sums1 = back_other(tokens, mask2, mvec, mods, gain1, gx, wx_qkv, part, gmid)

    gmod = jnp.concatenate(
        [sums1[0:1], sums1[1:2] * gain1, sums2[4:5], sums2[2:3], sums2[3:4] * gain2, sums2[0:1]], axis=0
    )
    small = [
        sums1[2:3].reshape(dp, -1),
        (sums1[1:2] * (1.0 + mods[1:2])).reshape(dp, -1),
        (sums2[3:4] * (1.0 + mods[4:5])).reshape(dp, -1),
        sums2[1:2].reshape(dp, -1),
        gbup.reshape(dp, -1),
        gmod.reshape(dp, -1),
        jnp.broadcast_to(cond, (dp, cond.shape[1])),
    ]
    sizes = [x.shape[1] for x in small]
    at = np.cumsum([0] + sizes)
    pad = -at[-1] % 128
    packed = jnp.concatenate(small + [jnp.zeros((dp, pad), F32)], axis=1)
    got = swap(dp, packed[:, None, :])[:, 0, :]
    total = jnp.sum(got, axis=0)
    part_of = lambda i: total[at[i] : at[i + 1]]
    sum_mask, sum_ln1, sum_ln2, sum_bdown, sum_bup, sum_bada = (part_of(i) for i in range(6))
    sum_wada = lax.dot_general(
        got[:, at[6] : at[7]], got[:, at[5] : at[6]], (((0,), (0,)), ((), ())),
        precision=lax.Precision.HIGHEST,
    )
    return (
        result,
        grad_tokens,
        sum_mask,
        sum_ln1,
        sum_qkv.reshape(-1, 3, cols).transpose(1, 0, 2),
        sum_out.T,
        sum_ln2,
        sum_up,
        sum_bup,
        sum_down.T,
        sum_bdown,
        sum_wada,
        sum_bada,
    )


def solution(mesh):
    in_specs = (
        P("dp", None), P("dp", None), P("dp"), P("dp"), P(), P(), P(), P(None, None, "tensor"),
        P("tensor", None), P(), P(None, "tensor"), P("tensor"), P("tensor", None), P(), P(), P(),
    )
    out_specs = (
        P("dp", None), P("dp", None), P("dp"), P("dp"), P(None, "dp", "tensor"), P("tensor", "dp"),
        P("dp"), P("dp", "tensor"), P(("tensor", "dp")), P("tensor", "dp"), P("dp"), P(None, "dp"), P("dp"),
    )
    step = functools.partial(body, mesh.shape["dp"])
    return jax.shard_map(step, mesh=mesh, in_specs=in_specs, out_specs=out_specs, check_vma=False)
```

```python
import functools

import jax
import jax.numpy as jnp
import numpy as np
from jax import lax
from jax.experimental import pallas as pl
from jax.experimental.pallas import tpu as pltpu
from jax.sharding import PartitionSpec as P

HD = 64
EPS = 1e-05
LOG2E = 1.4426950408889634
C2 = 0.125 * LOG2E
BF = jnp.bfloat16
F32 = jnp.float32
AXES = ("dp", "tensor")
MESH = pl.DeviceIdType.MESH
RB = 256
VMEM_ALL = 67_000_000


def dot(a, b, ca=1, cb=0):
    return lax.dot_general(a, b, (((ca,), (cb,)), ((), ())), preferred_element_type=F32)


def sds(shape, dtype):
    return jax.ShapeDtypeStruct(shape, dtype)


def whole(shape):
    return pl.BlockSpec(shape, lambda *_: (0,) * len(shape))


def params(**kw):
    return pltpu.CompilerParams(vmem_limit_bytes=VMEM_ALL, **kw)


def normed(x):
    mean = jnp.mean(x, axis=-1, keepdims=True)
    cent = x - mean
    var = jnp.mean(cent * cent, axis=-1, keepdims=True)
    rs = lax.rsqrt(var + EPS)
    return cent * rs, rs


def mask_column(mask_ref, step, rows):
    m = mask_ref[...].astype(F32).T
    lane = lax.broadcasted_iota(jnp.int32, m.shape, 1)
    per = rows // 128
    parts = [
        jnp.sum(jnp.where(lane == step * per + j, m, 0.0), axis=1, keepdims=True) for j in range(per)
    ]
    return jnp.concatenate(parts, axis=0)


def flipped(me, bit):
    return me + (1 << bit) * (1 - 2 * ((me // (1 << bit)) % 2))


class Gather:
    ops = 8

    def __init__(self, me, tensor, items, send_sem, recv_sem):
        self.me, self.tensor, self.items, self.send_sem, self.recv_sem = me, tensor, items, send_sem, recv_sem

    def copy(self, i, op):
        src, dst, block, first, rows, yz = self.items[i]
        one, two = (1, 2) if yz else (2, 1)
        piece = self.me % 8
        if op in (4, 5, 7):
            piece = flipped(piece, one)
        if op in (6, 7):
            piece = flipped(piece, two)
        at = dst.at[pl.ds(pl.multiple_of(piece * block + first, 8), rows), :]
        if op == 0:
            device = {"tensor": 1 - self.tensor}
        else:
            bit = {1: 0, 2: one, 3: two, 4: two, 5: 0, 6: 0, 7: 0}[op]
            device = {"dp": flipped(self.me, bit)}
        k = i * self.ops + op
        return pltpu.make_async_remote_copy(
            src_ref=src.at[pl.ds(first, rows), :] if op == 0 else at,
            dst_ref=at,
            send_sem=self.send_sem.at[k],
            recv_sem=self.recv_sem.at[k],
            device_id=device,
            device_id_type=MESH,
        )

    def stage(self, i, s):
        waits = {0: (), 1: (0,), 2: (2,), 3: (3, 4), 4: (1, 5, 6, 7)}[s]
        starts = {0: (0,), 1: (2, 3, 1), 2: (4, 5), 3: (6, 7), 4: ()}[s]
        for op in waits:
            self.copy(i, op).wait_recv()
        for op in starts:
            self.copy(i, op).start()
        if s == 4:
            for op in range(self.ops):
                self.copy(i, op).wait_send()


def greet_gather(me, tensor):
    barrier = pltpu.get_barrier_semaphore()
    pl.semaphore_signal(barrier, inc=1, device_id={"tensor": 1 - tensor}, device_id_type=MESH)
    for bit in range(3):
        pl.semaphore_signal(barrier, inc=1, device_id={"dp": flipped(me, bit)}, device_id_type=MESH)
    pl.semaphore_wait(barrier, 4)


class Reduce:
    def __init__(self, dp, me, source, home, more, send_sem, recv_sem):
        self.dp, self.me, self.source, self.home, self.more = dp, me, source, home, more
        self.send_sem, self.recv_sem = send_sem, recv_sem
        self.hops = dp.bit_length() - 1

    def block(self, j, m, keep):
        low = self.me % (1 << j)
        bit = (self.me // (1 << j)) % 2
        return low + (1 << j) * (bit if keep else 1 - bit) + (1 << (j + 1)) * m

    def count(self, j):
        return self.dp >> (j + 1)

    def base(self, j):
        return self.dp // 2 - (self.dp >> j)

    def copy(self, j, m):
        b = self.block(j, m, False)
        if j == 0:
            src, dst, k = self.source.at[b], self.home.at[m], m
        else:
            at = self.base(j) + m
            src, dst, k = self.home.at[b // 2], self.more.at[at], self.dp // 2 + at
        return pltpu.make_async_remote_copy(
            src_ref=src,
            dst_ref=dst,
            send_sem=self.send_sem.at[k],
            recv_sem=self.recv_sem.at[k],
            device_id={"dp": flipped(self.me, j)},
            device_id_type=MESH,
        )

    def each(self, j, ms, do):
        first, last = (0, self.count(j)) if ms is None else ms
        if last - first > 4:

            @pl.loop(first, last)
            def _(m):
                do(m)
        else:
            for m in range(first, last):
                do(m)

    def start(self, j, ms=None):
        self.each(j, ms, lambda m: self.copy(j, m).start())

    def finish_send(self, j, ms=None):
        self.each(j, ms, lambda m: self.copy(j, m).wait_send())

    def add(self, j, ms=None, kept=None):
        def do(m):
            self.copy(j, m).wait_recv()
            b = self.block(j, m, True)
            if j == 0:
                own = self.source[b] if kept is None else kept[m]
                self.home[m] = self.home[m] + own
            else:
                self.home[b // 2] = self.home[b // 2] + self.more[self.base(j) + m]

        self.each(j, ms, do)


def greet_all(dp, me, tensor):
    barrier = pltpu.get_barrier_semaphore()

    @pl.loop(1, dp)
    def _(r):
        pl.semaphore_signal(barrier, inc=1, device_id=((me + r) % dp, tensor), device_id_type=MESH)

    pl.semaphore_wait(barrier, dp - 1)


def reduce_scratch(dp, rows, cols, home=True):
    half = [pltpu.VMEM((dp // 2, rows, cols), F32)] if home else []
    return half + [
        pltpu.VMEM((max(dp // 2 - 1, 1), rows, cols), F32),
        pltpu.SemaphoreType.DMA((dp - 1,)),
        pltpu.SemaphoreType.DMA((dp - 1,)),
    ]


def rope(x, cos, sin):
    lane = lax.broadcasted_iota(jnp.int32, x.shape, 1)
    other = jnp.where(lane % HD < HD // 2, pltpu.roll(x, 128 - HD // 2, 1), pltpu.roll(x, HD // 2, 1))
    return x * cos + other * sin


def project(h, w_ref, cos_ref, sin_ref, q_ref, k_ref, v_ref):
    cos, sin = cos_ref[...], sin_ref[...]
    cols = q_ref.shape[1]
    for i, out in ((0, q_ref), (1, k_ref)):
        y = dot(h, w_ref[i])
        for c in range(0, cols, 128):
            out[:, c : c + 128] = rope(y[:, c : c + 128], cos, sin).astype(BF)
    v_ref[...] = dot(h, w_ref[2]).astype(BF)


def attend_pair(q_ref, k_ref, v_ref, at, o_ref, lse_ref, pair, oT, sbuf):
    length = q_ref.shape[0]
    wide = sbuf.shape[2]
    kk = k_ref[:, at]
    qT, vT = q_ref[:, at].T, v_ref[:, at].T
    row = lax.broadcasted_iota(jnp.int32, (128, wide), 0)
    items = [(h, c) for h in range(2) for c in range(0, length, wide)]

    def scores(i):
        h, c = items[i]
        qq = qT[:, c : c + wide]
        s = dot(kk, jnp.where((row < HD) == (h == 0), qq, jnp.zeros_like(qq)))
        sbuf[i % 2] = s
        return jnp.max(s, axis=0, keepdims=True)

    top = scores(0)
    for i, (h, c) in enumerate(items):
        following = scores(i + 1) if i + 1 < len(items) else None
        p = jnp.exp2((sbuf[i % 2] - top) * C2)
        total = jnp.sum(p, axis=0, keepdims=True)
        oT[h * HD : (h + 1) * HD, c : c + wide] = dot(vT[h * HD : (h + 1) * HD, :], p.astype(BF)) * (1.0 / total)
        lse_ref[pl.ds(pair, 1), h : h + 1, c : c + wide] = (top * C2 + jnp.log2(total))[None]
        top = following
    o_ref[:, at] = oT[...].T.astype(BF)


def store_blocks(out, value, first=0):
    rows = out.shape[1]
    n = value.shape[0] // rows
    if rows % 8 == 0:
        out[pl.ds(first, n)] = value.reshape(n, rows, value.shape[1])
    else:
        for b in range(n):
            out[first + b] = value[b * rows : (b + 1) * rows, :]


def forward_kernel(
    nb, plan, bucket, tok, mask, mvec, gain1, gain2, te, wada, bada, wq, cos, sin, bup,
    wo_h, wup_h, wdown_h, cot_h, pq, po, pu, pd,
    h1_ref, q_ref, k_ref, v_ref, mods_ref, cond_ref, o_ref, lse_ref, wxq_ref, wxo_ref,
    attn_ref, h2_ref, feed_ref, gh_ref, gbup_ref, du_ref, dd_ref, fu, fd,
    oT, sbuf, fq, fo, wo, wup, wdown, cot, act_s, gp_s, gf_s, load_sem, send_sem, recv_sem,
):
    step = pl.program_id(0)
    me, tensor = lax.axis_index("dp"), lax.axis_index("tensor")
    pairs = q_ref.shape[2] // 128
    width = tok.shape[1]
    bq, bo, bu, bd = (p.shape[0] for p in (pq, po, pu, pd))
    items = [(pq, fq, bq, i * (bq // 4), bq // 4, i % 2 == 0) for i in range(4)]
    items += [(po, fo, bo, i * (bo // 2), bo // 2, i == 0) for i in range(2)]
    items += [(pu, fu, bu, i * (bu // 2), bu // 2, i == 0) for i in range(2)]
    items += [(pd, fd, bd, i * (bd // 2), bd // 2, i == 0) for i in range(2)]
    gather = Gather(me, tensor, items, send_sem, recv_sem)
    loads = [
        pltpu.make_async_copy(src, dst, load_sem.at[i])
        for i, (src, dst) in enumerate(((wo_h, wo), (wup_h, wup), (wdown_h, wdown), (cot_h, cot)))
    ]
    s_own, s_proj = nb, nb + pairs
    s_other = s_proj + nb
    s_mlp = s_other + pairs
    s_dw = s_mlp + nb

    @pl.when(step == 0)
    def _():
        greet_gather(me, tensor)

    for at, todo in plan.items():

        @pl.when(step == at)
        def _():
            for i, s in todo:
                gather.stage(i, s)

    @pl.when(step == 0)
    def _():
        for c in loads:
            c.start()
        row = te[...]
        row = row * (1.0 / (1.0 + jnp.exp(-row)))
        sub = lax.broadcasted_iota(jnp.int32, row.shape, 0)
        pick = jnp.sum(jnp.where(sub == bucket[...] % 8, row, 0.0), axis=0, keepdims=True)
        cond_ref[...] = pick
        col = jnp.broadcast_to(pick, (8, pick.shape[1])).T[:, 0:1]
        for i in range(6):
            cs = slice(i * width, (i + 1) * width)
            mods_ref[i : i + 1, :] = (
                jnp.sum(wada[:, cs].astype(F32) * col, axis=0, keepdims=True) + bada[:, cs]
            )

    def block(first):
        return pl.ds(pl.multiple_of((step - first) * RB, RB), RB)

    @pl.when(step < s_own)
    def _():
        rows = block(0)
        x = tok[rows, :].astype(F32) + mask_column(mask, step, RB) * mvec[...]
        n, _ = normed(x)
        h = (n * gain1[...] * (1.0 + mods_ref[1:2, :]) + mods_ref[0:1, :]).astype(BF)
        h1_ref[rows, :] = h
        project(
            h, wq, cos.at[rows, :], sin.at[rows, :], q_ref.at[0, rows, :], k_ref.at[0, rows, :], v_ref.at[0, rows, :]
        )

    for half, first in ((0, s_own), (1, s_other)):

        @pl.when((step >= first) & (step < first + pairs))
        def _():
            pair = step - first
            at = pl.ds(pl.multiple_of(pair * 128, 128), 128)
            attend_pair(
                q_ref.at[half], k_ref.at[half], v_ref.at[half], at, o_ref.at[half], lse_ref, half * pairs + pair, oT, sbuf
            )

    @pl.when(step == s_proj)
    def _():
        for i in range(3):
            wxq_ref[i] = fq[i * width : (i + 1) * width, :].astype(BF)

    @pl.when((step >= s_proj) & (step < s_other))
    def _():
        rows = block(s_proj)
        project(
            h1_ref[rows, :], wxq_ref, cos.at[rows, :], sin.at[rows, :],
            q_ref.at[1, rows, :], k_ref.at[1, rows, :], v_ref.at[1, rows, :],
        )

    @pl.when(step == s_mlp)
    def _():
        wxo_ref[...] = fo[...].astype(BF)
        for c in loads:
            c.wait()
        gbup_ref[...] = jnp.zeros_like(gbup_ref)

    @pl.when((step >= s_mlp) & (step < s_dw))
    def _():
        rows = block(s_mlp)
        x = tok[rows, :].astype(F32) + mask_column(mask, step - s_mlp, RB) * mvec[...]
        attn = dot(o_ref[0, rows, :], wo[...]) + dot(o_ref[1, rows, :], wxo_ref[...])
        attn_ref[...] = attn
        n, _ = normed(x + mods_ref[2:3, :] * attn)
        h = (n * gain2[...] * (1.0 + mods_ref[4:5, :]) + mods_ref[3:4, :]).astype(BF)
        h2_ref[rows, :] = h
        act, slope = gelu_parts(dot(h, wup[...]) + bup[...])
        act = act.astype(BF)
        act_s[rows, :] = act
        feed_ref[...] = dot(act, wdown[...])
        gf = (mods_ref[5:6, :] * cot[rows, :].astype(F32)).astype(BF)
        gf_s[rows, :] = gf
        gp = (dot(gf, wdown[...], 1, 1) * slope).astype(BF)
        gp_s[rows, :] = gp
        gh_ref[...] = dot(gp, wup[...], 1, 1)
        gbup_ref[...] += jnp.sum(gp.astype(F32), axis=0, keepdims=True)

    @pl.when(step >= s_dw)
    def _():
        part = width // 2
        cs = pl.ds(pl.multiple_of((step - s_dw) * part, 128), part)
        store_blocks(du_ref, dot(h2_ref[:, cs], gp_s[...], 0, 0))
        store_blocks(dd_ref, dot(gf_s[:, cs], act_s[...], 0, 0))

    @pl.when(step == pl.num_programs(0) - 1)
    def _():
        for i in range(6, len(items)):
            gather.stage(i, 4)


FORWARD_PLAN = {
    0: [(i, 0) for i in range(10)],
    2: [(0, 1), (1, 1)],
    4: [(0, 2), (1, 2), (2, 1), (3, 1)],
    5: [(0, 3), (1, 3), (2, 2), (3, 2)],
    6: [(2, 3), (3, 3), (4, 1), (5, 1)],
    7: [(i, 4) for i in range(4)] + [(6, 1)],
    9: [(4, 2), (5, 2)],
    11: [(4, 3), (5, 3), (7, 1)],
    12: [(6, 2)],
    13: [(7, 2), (8, 1)],
    14: [(4, 4), (5, 4), (9, 1)],
    15: [(6, 3), (7, 3), (8, 2)],
    16: [(9, 2)],
    17: [(8, 3)],
    18: [(9, 3)],
}


def forward(dp, bucket, tokens, mask2, mvec, gain1, gain2, te, wada, bada, wq, cos, sin, bup, wo, wup, wdown, cot, pieces):
    rows, width = tokens.shape
    cols, ff = wq.shape[2], wup.shape[1]
    nb, pairs = rows // RB, cols // 128
    s_mlp = 2 * (nb + pairs)
    mblk = pl.BlockSpec((RB, width), lambda i: (jnp.clip(i - s_mlp, 0, nb - 1), 0))
    dblk = pl.BlockSpec((dp // 2, width // dp, ff), lambda i: (jnp.maximum(i - s_mlp - nb, 0), 0, 0))
    anys = pl.BlockSpec(memory_space=pl.ANY)
    one = lambda shape: pl.BlockSpec(shape, lambda i: (0,) * len(shape), pipeline_mode=pl.Buffered(1))
    act = (2, rows, cols)
    full = [(8 * p.shape[0], p.shape[1]) for p in pieces]
    vm = pltpu.VMEM
    return pl.pallas_call(
        functools.partial(forward_kernel, nb, FORWARD_PLAN),
        grid=(s_mlp + nb + 2,),
        in_specs=[
            one((1, 1)), one(tokens.shape), one(mask2.shape), one((1, width)), one((1, width)), one((1, width)),
            one(te.shape), one(wada.shape), one(bada.shape), one(wq.shape), one(cos.shape), one(sin.shape),
            one(bup.shape),
        ] + [anys] * 8,
        out_specs=[
            one((rows, width)), one(act), one(act), one(act), one((8, width)), one((1, te.shape[1])),
            one(act), one((2 * pairs, 2, rows)), one(wq.shape), one((cols, width)),
            mblk, one((rows, width)), mblk, mblk, one((1, ff)), dblk, dblk, anys, anys,
        ],
        out_shape=[
            sds((rows, width), BF), sds(act, BF), sds(act, BF), sds(act, BF), sds((8, width), F32),
            sds((1, te.shape[1]), F32), sds(act, BF), sds((2 * pairs, 2, rows), F32), sds(wq.shape, BF),
            sds((cols, width), BF), sds((rows, width), F32), sds((rows, width), BF), sds((rows, width), F32),
            sds((rows, width), F32), sds((1, ff), F32), sds((dp, width // dp, ff), F32),
            sds((dp, width // dp, ff), F32), sds(full[2], F32), sds(full[3], F32),
        ],
        scratch_shapes=[
            vm((128, rows), F32), vm((2, rows, 512), F32), vm(full[0], F32), vm(full[1], F32),
            vm(wo.shape, BF), vm(wup.shape, BF), vm(wdown.shape, BF), vm(cot.shape, BF),
            vm((rows, ff), BF), vm((rows, ff), BF), vm((rows, width), BF),
            pltpu.SemaphoreType.DMA((4,)), pltpu.SemaphoreType.DMA((80,)), pltpu.SemaphoreType.DMA((80,)),
        ],
        compiler_params=params(collective_id=2, has_side_effects=True),
        name="forward",
    )(bucket, tokens, mask2, mvec, gain1, gain2, te, wada, bada, wq, cos, sin, bup, wo, wup, wdown, cot, *pieces)


def attend_back_pair(q_ref, k_ref, v_ref, o_ref, do_ref, lse_ref, cosT, sinT, g_ref, at, gT):
    length = q_ref.shape[0]
    kk, vv = k_ref[...], v_ref[...]
    kT, qT, doT = kk.T, q_ref[...].T, do_ref[...].T
    oT = o_ref[...].T
    prod = doT.astype(F32) * oT.astype(F32)
    row = lax.broadcasted_iota(jnp.int32, (128, length), 0)
    half = HD // 2
    for h in range(2):
        hs = slice(h * HD, (h + 1) * HD)
        sel = (row < HD) == (h == 0)
        qm = jnp.where(sel, qT, jnp.zeros_like(qT))
        dm = jnp.where(sel, doT, jnp.zeros_like(doT))
        inner = jnp.sum(prod[hs, :], axis=0, keepdims=True)
        p = jnp.exp2(dot(kk, qm) * C2 - lse_ref[h : h + 1, :])
        ds = (p * (dot(vv, dm) - inner)).astype(BF)
        dv = dot(doT[hs, :], p.astype(BF), 1, 1)
        dk = dot(qT[hs, :], ds, 1, 1) * 0.125
        dq = dot(kT[hs, :], ds) * 0.125
        c, s = cosT[...], sinT[...]
        for i, d in ((0, dq), (1, dk)):
            a, b = d[:half, :], d[half:, :]
            gT[i, h * HD : h * HD + half, :] = a * c + b * s
            gT[i, h * HD + half : (h + 1) * HD, :] = b * c - a * s
        gT[2, hs, :] = dv
    for i in range(3):
        g_ref[i, :, at] = gT[i].T.astype(BF)


def gelu_parts(x):
    c0, c1 = 0.7978845608028654, 0.044715
    x2 = x * x
    t = jnp.tanh(x * (c0 + (c0 * c1) * x2))
    a = 0.5 + 0.5 * t
    d = a + (x * (0.5 - 0.5 * (t * t))) * (c0 + (3.0 * c0 * c1) * x2)
    return x * a, d


def mlp_other_kernel(
    dp, cut, tok, mask, mvec, mods, gain, attn_ref, h_ref, feed_ref, gh_ref, cot, wup, bup, wdown, bdown,
    mo, wo, wx, gbup, cond, du, dd,
    res_ref, gmid_ref, gm_ref, small, dw_ref, hu_out, hd_out,
    acc, keep_u, keep_d, load_sem, hu, hd, more_u, send_u, recv_u, more_d, send_d, recv_d,
):
    step, last = pl.program_id(0), pl.num_programs(0) - 1
    me, tensor = lax.axis_index("dp"), lax.axis_index("tensor")
    up = Reduce(dp, me, du, hu, more_u, send_u, recv_u)
    down = Reduce(dp, me, dd, hd, more_d, send_d, recv_d)

    def load(r, keep, k, m):
        return pltpu.make_async_copy(r.source.at[r.block(0, m, True)], keep.at[m], load_sem.at[k, m])

    @pl.when(step == 0)
    def _():
        barrier = pltpu.get_barrier_semaphore()
        for j in range(2):
            pl.semaphore_signal(barrier, inc=1, device_id={"dp": flipped(me, j)}, device_id_type=MESH)
        pl.semaphore_wait(barrier, 2)
        up.start(0)
        down.start(0)
        for k, (r, keep) in enumerate(((up, keep_u), (down, keep_d))):
            r.each(0, None, lambda m: load(r, keep, k, m).start())
        small[...] = jnp.zeros_like(small)

    @pl.when(step == 1)
    def _():
        up.each(0, None, lambda m: load(up, keep_u, 0, m).wait())
        up.add(0, kept=keep_u)
        up.start(1, (0, cut))

    @pl.when(step == 2)
    def _():
        down.each(0, None, lambda m: load(down, keep_d, 1, m).wait())
        down.add(0, kept=keep_d)

    x = tok[...].astype(F32) + mask_column(mask, step, tok.shape[0]) * mvec[...]
    attn = attn_ref[...]
    middle = x + mods[2:3, :] * attn
    n2, rs = normed(middle)
    act, slope = gelu_parts(dot(h_ref[...], wup[...]) + bup[...])
    feed = (feed_ref[...] + dot(act.astype(BF), wdown[...])) + bdown[...]
    g = cot[...].astype(F32)
    res_ref[...] = (middle + mods[5:6, :] * feed).astype(BF)
    gf = (mods[5:6, :] * g).astype(BF)
    gp = (dot(gf, wdown[...], 1, 1) * slope).astype(BF)
    gh = gh_ref[...] + dot(gp, wup[...], 1, 1)
    opened = 1.0 + mods[4:5, :]
    e = gh * (opened * gain[...])
    inner = jnp.mean(e * n2, axis=-1, keepdims=True)
    gmid = g + (e - jnp.mean(e, axis=-1, keepdims=True) - n2 * inner) * rs
    gmid_ref[...] = gmid
    ga = (mods[2:3, :] * gmid).astype(BF)
    gm_ref[0] = dot(ga, wo[...], 1, 1).astype(BF)
    gm_ref[1] = dot(ga, wx[...], 1, 1).astype(BF)
    col = lambda v: jnp.sum(v, axis=0, keepdims=True)
    small[0:1, :] += col(g * feed)
    small[1:2, :] += col(gf.astype(F32))
    small[2:3, :] += col(gh)
    small[3:4, :] += col(gh * n2)
    small[4:5, :] += col(gmid * attn)
    dw = dot(ga, mo[...], 0, 0)

    @pl.when(step == 0)
    def _():
        acc[...] = dw

    @pl.when(step > 0)
    def _():
        acc[...] += dw

    @pl.when(step == last)
    def _():
        width = gain.shape[1]
        small[5:6, :] = small[3:4, :] * opened
        small[3:4, :] = small[3:4, :] * gain[...]
        for i in range(gbup.shape[1] // width):
            small[8 + i : 9 + i, :] = gbup[:, i * width : (i + 1) * width]
        small[6:7, 0 : cond.shape[1]] = cond[...]
        store_blocks(dw_ref, acc[...])
        up.add(1, (0, cut))
        up.finish_send(0)
        down.finish_send(0)
        up.finish_send(1, (0, cut))
        stores = [
            pltpu.make_async_copy(src, dst, load_sem.at[k, 0]) for k, (src, dst) in enumerate(((hu, hu_out), (hd, hd_out)))
        ]
        for c in stores:
            c.start()
        for c in stores:
            c.wait()


def mlp_other(dp, cut, tokens, mask2, mvec, mods, gain, attn, h, feed, gh, cot, wup, bup, wdown, bdown, os, wo, wx, gbup, cond, du, dd):
    rows, width = tokens.shape
    ff, cols = wup.shape[1], wo.shape[0]
    part = width // dp
    blk = lambda c: pl.BlockSpec((RB, c), lambda i: (i, 0))
    one = lambda shape: pl.BlockSpec(shape, lambda i: (0,) * len(shape), pipeline_mode=pl.Buffered(1))
    anys = pl.BlockSpec(memory_space=pl.ANY)
    half = (dp // 2, part, ff)
    return pl.pallas_call(
        functools.partial(mlp_other_kernel, dp, cut),
        grid=(rows // RB,),
        in_specs=[
            blk(width), one(mask2.shape), one((1, width)), one(mods.shape), one((1, width)),
            blk(width), blk(width), blk(width), blk(width), blk(width),
            one(wup.shape), one((1, ff)), one(wdown.shape), one((1, width)),
            pl.BlockSpec((None, RB, cols), lambda i: (0, i, 0)), one(wo.shape), one(wx.shape), one(gbup.shape),
            one(cond.shape), anys, anys,
        ],
        out_specs=[
            blk(width), blk(width), pl.BlockSpec((2, RB, cols), lambda i: (0, i, 0)), one((16, width)),
            one((dp, part, cols)), anys, anys,
        ],
        out_shape=[
            sds((rows, width), BF), sds((rows, width), F32), sds((2, rows, cols), BF), sds((16, width), F32),
            sds((dp, part, cols), F32), sds(half, F32), sds(half, F32),
        ],
        scratch_shapes=[
            pltpu.VMEM((width, cols), F32), pltpu.VMEM(half, F32), pltpu.VMEM(half, F32),
            pltpu.SemaphoreType.DMA((2, dp // 2)), pltpu.VMEM(half, F32), pltpu.VMEM(half, F32),
            *reduce_scratch(dp, part, ff, False), *reduce_scratch(dp, part, ff, False),
        ],
        compiler_params=params(collective_id=3, has_side_effects=True),
        name="mlp_other",
    )(tokens, mask2, mvec, mods, gain, attn, h, feed, gh, cot, wup, bup, wdown, bdown, os, wo, wx, gbup, cond, du, dd)


def backward_kernel(
    dp, cut, nb, pairs, q_ref, k_ref, v_ref, o_ref, do_ref, lse_ref, cosT, sinT, h1, w, wx, tok, mask, mvec,
    mods, gain, gmid_ref, early_hbm, dw_hbm, hu_in, hd_in,
    gt_ref, early, late, up_ref, down_ref, out_ref, qkv_ref,
    gT, g, gx, dqkv, early_in, dw_out, late_s, own_sem, gsend, grecv, load_sem,
    hu, more_u, send_u, recv_u, hd, more_d, send_d, recv_d,
    ho, more_o, send_o, recv_o, hq, more_q, send_q, recv_q,
):
    step, last = pl.program_id(0), pl.num_programs(0) - 1
    me, tensor = lax.axis_index("dp"), lax.axis_index("tensor")
    up = Reduce(dp, me, None, hu, more_u, send_u, recv_u)
    down = Reduce(dp, me, None, hd, more_d, send_d, recv_d)
    out = Reduce(dp, me, dw_out, ho, more_o, send_o, recv_o)
    qkv = Reduce(dp, me, dqkv, hq, more_q, send_q, recv_q)
    hops = up.hops
    loads = [
        pltpu.make_async_copy(src, dst, load_sem.at[i]) for i, (src, dst) in enumerate(((dw_hbm, dw_out), (early_hbm, early_in), (hu_in, hu), (hd_in, hd)))
    ]
    s_dw, s_x, s_end = pairs, pairs + 1, 2 * pairs + 1

    def spread(src, dst, k, r):
        to = (me + r) % dp
        return pltpu.make_async_remote_copy(
            src_ref=src, dst_ref=dst.at[me], send_sem=gsend.at[k, r], recv_sem=grecv.at[k, r],
            device_id=(to, tensor), device_id_type=MESH,
        )

    def own(src, dst, k):
        return pltpu.make_async_copy(src, dst.at[me], own_sem.at[k])

    @pl.when(step == 0)
    def _():
        greet_all(dp, me, tensor)
        for c in loads:
            c.start()
        for c in loads:
            c.wait()
        out.start(0)
        up.start(1, (cut, up.count(1)))
        down.start(1)
        own(early_in, early, 0).start()

        @pl.loop(1, dp)
        def _(r):
            spread(early_in, early, 0, r).start()

    @pl.when(step == 1)
    def _():
        out.add(0)
        out.start(1)
        up.add(1, (cut, up.count(1)))
        up.start(2)

    @pl.when(step == s_dw)
    def _():
        up.add(2)
        up.start(3)

    @pl.when(step == s_x)
    def _():
        qkv.start(0)

    @pl.when(step == s_x + 1)
    def _():
        for j in range(3, hops):
            up.add(j)
            if j + 1 < hops:
                up.start(j + 1)
        up_ref[...] = hu[me // 2]
        qkv.add(0)
        qkv.start(1)
        down.add(1)
        down.start(2)
        out.add(1)
        out.start(2)

    @pl.when(step == s_end)
    def _():
        down.add(2)
        down.start(3)
        out.add(2)
        out.start(3)

    @pl.when(step == s_end + 2)
    def _():
        for r, dst in ((down, down_ref), (out, out_ref)):
            for j in range(3, hops):
                r.add(j)
                if j + 1 < hops:
                    r.start(j + 1)
            dst[...] = r.home[me // 2]

    @pl.when(step == last)
    def _():
        qkv.add(1)
        qkv.start(2)

    for first, dst in ((0, g), (s_x, gx)):

        @pl.when((step >= first) & (step < first + pairs))
        def _():
            at = pl.ds(pl.multiple_of((step - first) * 128, 128), 128)
            attend_back_pair(q_ref, k_ref, v_ref, o_ref, do_ref, lse_ref, cosT, sinT, dst, at, gT)

    @pl.when(step == s_dw)
    def _():
        cols = w.shape[2]
        for i in range(3):
            d = dot(h1[...], g[i], 0, 0)
            rows = dqkv.shape[1]
            if rows % 8 == 0:
                dqkv[:, :, i * cols : (i + 1) * cols] = d.reshape(dp, rows, cols)
            else:
                for b in range(dp):
                    dqkv[b, :, i * cols : (i + 1) * cols] = d[b * rows : (b + 1) * rows, :]
        late_s[...] = jnp.zeros_like(late_s)

    @pl.when(step >= s_end)
    def _():
        i = step - s_end
        rows = pl.ds(pl.multiple_of(i * RB, RB), RB)
        m = mask_column(mask, i, RB)
        n1, rs = normed(tok[...].astype(F32) + m * mvec[...])
        parts = [
            dot(d[0, rows, :], ww[0], 1, 1) + dot(d[1, rows, :], ww[1], 1, 1) + dot(d[2, rows, :], ww[2], 1, 1)
            for d, ww in ((g, w), (gx, wx))
        ]
        gh = parts[0] + parts[1]
        e = gh * ((1.0 + mods[1:2, :]) * gain[...])
        inner = jnp.mean(e * n1, axis=-1, keepdims=True)
        gs = gmid_ref[...] + (e - jnp.mean(e, axis=-1, keepdims=True) - n1 * inner) * rs
        gt_ref[...] = gs.astype(BF)
        col = lambda v: jnp.sum(v, axis=0, keepdims=True)
        late_s[0:1, :] += col(gh)
        late_s[1:2, :] += col(gh * n1)
        late_s[3:4, :] += col(m * gs)

    @pl.when(step == last)
    def _():
        late_s[2:3, :] = late_s[1:2, :] * (1.0 + mods[1:2, :])
        late_s[1:2, :] = late_s[1:2, :] * gain[...]
        own(late_s, late, 1).start()

        @pl.loop(1, dp)
        def _(r):
            spread(late_s, late, 1, r).start()

        for j in range(2, hops):
            qkv.add(j)
            if j + 1 < hops:
                qkv.start(j + 1)
        qkv_ref[...] = hq[me // 2]
        for j in range(hops):
            if j > 0:
                up.finish_send(j, (cut, up.count(1)) if j == 1 else None)
                down.finish_send(j)
            out.finish_send(j)
            qkv.finish_send(j)
        for k, (src, dst) in enumerate(((early_in, early), (late_s, late))):
            own(src, dst, k).wait()

            @pl.loop(1, dp)
            def _(r):
                spread(src, dst, k, r).wait()


def backward(dp, cut, qs, ks, vs, os, gm, lses, cosT, sinT, h1, w, wx, tokens, mask2, mvec, mods, gain, gmid, early, dw_out, hu, hd):
    rows, width = tokens.shape
    cols = w.shape[2]
    nb, pairs = rows // RB, cols // 128
    part, ff = hu.shape[1], hu.shape[2]
    s_end = 2 * pairs + 1
    one = lambda shape: pl.BlockSpec(shape, lambda i: (0,) * len(shape), pipeline_mode=pl.Buffered(1))
    pick = lambda i: jnp.minimum(i - (i > pairs).astype(jnp.int32), 2 * pairs - 1)
    pair = pl.BlockSpec((None, rows, 128), lambda i: (pick(i) // pairs, 0, pick(i) % pairs))
    blk = pl.BlockSpec((RB, width), lambda i: (jnp.maximum(i - s_end, 0), 0))
    anys = pl.BlockSpec(memory_space=pl.ANY)
    vm = pltpu.VMEM
    return pl.pallas_call(
        functools.partial(backward_kernel, dp, cut, nb, pairs),
        grid=(s_end + nb,),
        in_specs=[pair] * 5 + [
            pl.BlockSpec((None, 2, rows), lambda i: (pick(i), 0, 0)), one(cosT.shape), one(sinT.shape),
            one(h1.shape), one(w.shape), one(wx.shape), blk, one(mask2.shape), one((1, width)), one(mods.shape),
            one((1, width)), blk, anys, anys, anys, anys,
        ],
        out_specs=[
            blk, anys, anys, one((part, ff)), one((part, ff)),
            one((part, cols)), one((part, 3 * cols)),
        ],
        out_shape=[
            sds((rows, width), BF), sds((dp, *early.shape), F32), sds((dp, 8, width), F32), sds((part, ff), F32),
            sds((part, ff), F32), sds((part, cols), F32), sds((part, 3 * cols), F32),
        ],
        scratch_shapes=[
            vm((3, 128, rows), F32), vm((3, rows, cols), BF), vm((3, rows, cols), BF), vm((dp, part, 3 * cols), F32),
            vm(early.shape, F32), vm((dp, part, cols), F32),
            vm((8, width), F32), pltpu.SemaphoreType.DMA((2,)), pltpu.SemaphoreType.DMA((2, dp)),
            pltpu.SemaphoreType.DMA((2, dp)), pltpu.SemaphoreType.DMA((4,)),
            *reduce_scratch(dp, part, ff), *reduce_scratch(dp, part, ff), *reduce_scratch(dp, part, cols),
            *reduce_scratch(dp, part, 3 * cols),
        ],
        compiler_params=params(collective_id=4, has_side_effects=True),
        name="backward",
    )(qs, ks, vs, os, gm, lses, cosT, sinT, h1, w, wx, tokens, mask2, mvec, mods, gain, gmid, early, dw_out, hu, hd)


def rope_tables(length):
    half = HD // 2
    freq = 10000.0 ** (-(np.arange(half, dtype=np.float64) / half))
    angle = np.arange(length, dtype=np.float64)[:, None] * freq[None, :]
    return np.cos(angle).astype(np.float32), np.sin(angle).astype(np.float32)


def body(
    dp, tokens, cotangent, bucket, mask, time_embed, mask_vec, ln1_gain, w_qkv, w_out, ln2_gain,
    w_up, b_up, w_down, b_down, w_ada, b_ada,
):
    rows, width = tokens.shape
    cols, ff = w_out.shape[0], w_up.shape[1]
    me = lax.axis_index("dp").astype(jnp.int32)
    line = lambda v: v.reshape(1, -1)
    mvec, gain1, gain2, bdown, bup = map(line, (mask_vec, ln1_gain, ln2_gain, b_down, b_up))
    mask2 = mask.reshape(rows // 128, 128)
    c, s = rope_tables(rows)
    cos, sin = jnp.asarray(np.tile(c, (1, 4))), jnp.asarray(np.tile(np.concatenate([-s, s], 1), (1, 2)))
    cosT, sinT = jnp.asarray(np.ascontiguousarray(c.T)), jnp.asarray(np.ascontiguousarray(s.T))

    flat = w_qkv.reshape(3 * width, cols)

    def piece(w):
        n = w.shape[0] // 8
        return lax.optimization_barrier(lax.dynamic_slice_in_dim(w, (me % 8) * n, n, 0).astype(F32))

    bup_x = lax.ppermute(bup, "tensor", [(0, 1), (1, 0)])

    te_row = lax.dynamic_slice_in_dim(time_embed, (bucket[0] // 8) * 8, 8, 0)
    pieces = [piece(w) for w in (flat, w_out, w_up, w_down)]
    (h1, qs, ks, vs, mods, cond, os, lses, wx_qkv, wx_out, attn, h2, feed, gh2, gbup, du, dd, fu, fd) = forward(
        dp, bucket.reshape(1, 1), tokens, mask2, mvec, gain1, gain2, te_row, w_ada, line(b_ada), w_qkv, cos, sin,
        bup, w_out, w_up, w_down, cotangent, pieces,
    )
    wx_up, wx_down = fu.astype(BF), fd.astype(BF)
    cut = 3 * dp // 16
    result, gmid, gm, small, dw_out, hu, hd = mlp_other(
        dp, cut, tokens, mask2, mvec, mods, gain2, attn, h2, feed, gh2, cotangent, wx_up, bup_x, wx_down, bdown,
        os, w_out, wx_out, gbup, cond, du, dd,
    )
    grad_tokens, early, late, sum_up, sum_down, sum_out, sum_qkv = backward(
        dp, cut, qs, ks, vs, os, gm, lses, cosT, sinT, h1, w_qkv, wx_qkv, tokens, mask2, mvec, mods, gain1, gmid,
        small, dw_out, hu, hd,
    )

    def mine(x, n):
        return lax.dynamic_slice_in_dim(x, me * n, n, 0)

    n = width // dp
    early_sum, late_sum = jnp.sum(early, axis=0), jnp.sum(late, axis=0)
    sum_mask, sum_ln1 = mine(late_sum[3], n), mine(late_sum[2], n)
    sum_ln2, sum_bdown = mine(early_sum[5], n), mine(early_sum[1], n)
    sum_bup = mine(early_sum[8 : 8 + ff // width].reshape(ff), ff // dp)
    gmod = jnp.stack([late[:, 0], late[:, 1], early[:, 4], early[:, 2], early[:, 3], early[:, 0]], axis=1)
    gmod = lax.dynamic_slice_in_dim(gmod.reshape(dp, 6 * width), me * 6 * n, 6 * n, 1)
    sum_wada = lax.dot_general(
        early[:, 6, : cond.shape[1]], gmod, (((0,), (0,)), ((), ())), precision=lax.Precision.HIGHEST
    )
    sum_bada = jnp.sum(gmod, axis=0)
    return (
        result,
        grad_tokens,
        sum_mask,
        sum_ln1,
        sum_qkv.reshape(-1, 3, cols).transpose(1, 0, 2),
        sum_out.T,
        sum_ln2,
        sum_up,
        sum_bup,
        sum_down.T,
        sum_bdown,
        sum_wada,
        sum_bada,
    )


def solution(mesh):
    in_specs = (
        P("dp", None), P("dp", None), P("dp"), P("dp"), P(), P(), P(), P(None, None, "tensor"),
        P("tensor", None), P(), P(None, "tensor"), P("tensor"), P("tensor", None), P(), P(), P(),
    )
    out_specs = (
        P("dp", None), P("dp", None), P("dp"), P("dp"), P(None, "dp", "tensor"), P("tensor", "dp"),
        P("dp"), P("dp", "tensor"), P(("tensor", "dp")), P("tensor", "dp"), P("dp"), P(None, "dp"), P("dp"),
    )
    step = functools.partial(body, mesh.shape["dp"])
    return jax.shard_map(step, mesh=mesh, in_specs=in_specs, out_specs=out_specs, check_vma=False)
```

```python
import functools

import jax
import jax.numpy as jnp
import numpy as np
from jax import lax
from jax.experimental import pallas as pl
from jax.experimental.pallas import tpu as pltpu
from jax.sharding import PartitionSpec as P

HD = 64
EPS = 1e-05
LOG2E = 1.4426950408889634
C2 = 0.125 * LOG2E
BF = jnp.bfloat16
F32 = jnp.float32
AXES = ("dp", "tensor")
MESH = pl.DeviceIdType.MESH
RB = 256
VMEM_ALL = 67_000_000


def dot(a, b, ca=1, cb=0):
    return lax.dot_general(a, b, (((ca,), (cb,)), ((), ())), preferred_element_type=F32)


def sds(shape, dtype):
    return jax.ShapeDtypeStruct(shape, dtype)


def one(shape):
    return pl.BlockSpec(shape, lambda *_: (0,) * len(shape), pipeline_mode=pl.Buffered(1))


ANYS = pl.BlockSpec(memory_space=pl.ANY)


def line(ref):
    v = ref[...]
    return v.reshape(1, v.shape[0])


def params(**kw):
    return pltpu.CompilerParams(vmem_limit_bytes=VMEM_ALL, **kw)


def normed(x):
    mean = jnp.mean(x, axis=-1, keepdims=True)
    cent = x - mean
    var = jnp.mean(cent * cent, axis=-1, keepdims=True)
    rs = lax.rsqrt(var + EPS)
    return cent * rs, rs


FORWARD_PLAN = {
    3: [(0, 0)],
    4: [(1, 0), (2, 0)],
    5: [(0, 2), (0, 3), (3, 0), (4, 0)],
    6: [(1, 2), (1, 3), (2, 2), (2, 3), (5, 0)],
    7: [(0, 4), (3, 2), (3, 3), (4, 2), (6, 0), (7, 0), (1, 4), (4, 3)],
    8: [(2, 4), (3, 4), (4, 4), (5, 2), (5, 3), (6, 2), (8, 0), (6, 3), (7, 3)],
    9: [(5, 4), (6, 4), (7, 2), (9, 0)],
    10: [(8, 2), (8, 3), (10, 0), (7, 4)],
    11: [(9, 2), (9, 3), (11, 0)],
    12: [(8, 4)],
    13: [(10, 2)],
    14: [(9, 4), (10, 3)],
    15: [(11, 2)],
}
FORWARD_END = [(11, 3), (10, 4), (11, 4)]
MLP_PLAN = {
    0: [('S', 'u', 0, 7), ('S', 'd', 0, 7), ('S', 'u', 0, 3), ('S', 'd', 0, 3), ('S', 'u', 0, 5), ('S', 'd', 0, 5), ('S', 'u', 0, 6), ('S', 'd', 0, 6), ('S', 'u', 0, 1), ('S', 'd', 0, 1), ('S', 'u', 0, 2), ('S', 'd', 0, 2), ('S', 'u', 0, 4), ('S', 'd', 0, 4), ('S', 'u', 0, 0), ('S', 'd', 0, 0)],
    1: [('A', 'u', 0, 7), ('A', 'd', 0, 7), ('A', 'u', 0, 3), ('A', 'd', 0, 3), ('A', 'u', 0, 5), ('A', 'd', 0, 5), ('A', 'u', 0, 6), ('A', 'd', 0, 6), ('S', 'u', 1, 3), ('S', 'd', 1, 3), ('S', 'u', 1, 1), ('S', 'd', 1, 1)],
    2: [('A', 'u', 0, 1), ('A', 'd', 0, 1), ('A', 'u', 0, 2), ('A', 'd', 0, 2), ('A', 'u', 0, 4), ('A', 'd', 0, 4), ('A', 'u', 0, 0), ('A', 'd', 0, 0)],
    3: [('A', 'u', 1, 3), ('A', 'd', 1, 3)],
    4: [('A', 'u', 1, 1), ('A', 'd', 1, 1)],
}
BACK_PLAN = {
    (0, 0): [('S', 'o', 0, 7), ('S', 'o', 0, 3), ('S', 'o', 0, 5), ('S', 'o', 0, 6), ('S', 'o', 0, 1), ('S', 'o', 0, 2), ('S', 'o', 0, 4), ('S', 'o', 0, 0), ('S', 'u', 1, 2), ('S', 'd', 1, 2), ('S', 'u', 1, 0), ('S', 'd', 1, 0), ('S', 'u', 2, 1), ('S', 'd', 2, 1), ('S', 'u', 2, 0), ('S', 'd', 2, 0)],
    (0, 1): [('A', 'o', 0, 7), ('A', 'o', 0, 3), ('A', 'o', 0, 5), ('A', 'o', 0, 6), ('A', 'o', 0, 1), ('A', 'o', 0, 2), ('S', 'o', 1, 3), ('S', 'o', 1, 1), ('S', 'o', 1, 2), ('S', 'o', 1, 0)],
    (1, 0): [('A', 'o', 0, 4), ('A', 'o', 0, 0), ('S', 'q0', 0, 7), ('S', 'q0', 0, 3), ('S', 'q0', 0, 5), ('S', 'q0', 0, 6), ('S', 'q0', 0, 1), ('S', 'q0', 0, 2), ('S', 'q0', 0, 4), ('S', 'q0', 0, 0)],
    (1, 1): [('A', 'q0', 0, 7), ('A', 'q0', 0, 3), ('A', 'q0', 0, 5), ('A', 'q0', 0, 6), ('A', 'u', 1, 2), ('A', 'd', 1, 2), ('A', 'q0', 0, 1), ('A', 'q0', 0, 2), ('A', 'q0', 0, 4), ('S', 'q0', 1, 3), ('S', 'q0', 1, 1), ('S', 'q0', 1, 2), ('S', 'q0', 1, 0)],
    (2, 0): [('A', 'q0', 0, 0), ('S', 'q1', 0, 7), ('S', 'q1', 0, 3), ('S', 'q1', 0, 5), ('S', 'q1', 0, 6), ('S', 'q1', 0, 1), ('S', 'q1', 0, 2), ('S', 'q1', 0, 4), ('S', 'q1', 0, 0)],
    (2, 1): [('A', 'q1', 0, 7), ('A', 'q1', 0, 3), ('A', 'u', 1, 0), ('A', 'd', 1, 0), ('A', 'q1', 0, 5), ('A', 'q1', 0, 6), ('A', 'q1', 0, 1), ('A', 'q1', 0, 2), ('A', 'q1', 0, 4), ('S', 'q1', 1, 3), ('S', 'q1', 1, 1), ('S', 'q1', 1, 2), ('S', 'q1', 1, 0)],
    (3, 0): [('A', 'q1', 0, 0), ('S', 'q2', 0, 7), ('S', 'q2', 0, 3), ('S', 'q2', 0, 5), ('S', 'q2', 0, 6), ('S', 'q2', 0, 1), ('S', 'q2', 0, 2), ('S', 'q2', 0, 4), ('S', 'q2', 0, 0)],
    (3, 1): [('A', 'u', 2, 1), ('A', 'd', 2, 1), ('A', 'q2', 0, 7), ('A', 'q2', 0, 3), ('A', 'q2', 0, 5), ('A', 'q2', 0, 6), ('A', 'q2', 0, 1), ('A', 'q2', 0, 2), ('A', 'q2', 0, 4), ('S', 'q2', 1, 3), ('S', 'q2', 1, 1), ('S', 'q2', 1, 2), ('S', 'q2', 1, 0), ('S', 'u', 3, 0), ('S', 'd', 3, 0)],
    (4, 0): [('A', 'q2', 0, 0)],
    (4, 1): [('A', 'u', 2, 0), ('A', 'd', 2, 0)],
    (5, 0): [('A', 'o', 1, 3), ('S', 'o', 2, 1)],
    (5, 1): [('A', 'o', 1, 1), ('A', 'o', 1, 2), ('S', 'o', 2, 0)],
    (6, 0): [('A', 'o', 1, 0), ('A', 'q0', 1, 3), ('S', 'q0', 2, 1)],
    (7, 0): [('A', 'q0', 1, 1), ('S', 'q0', 2, 0)],
    (8, 0): [('A', 'u', 3, 0), ('A', 'q0', 1, 2)],
    (9, 0): [('A', 'q0', 1, 0)],
}
BACK_END = [('A', 'q1', 1, 3), ('A', 'q1', 1, 1), ('S', 'q1', 2, 1), ('S', 'q1', 2, 0), ('A', 'q1', 1, 2), ('A', 'o', 2, 1), ('S', 'o', 3, 0), ('A', 'q1', 1, 0), ('A', 'o', 2, 0), ('A', 'q2', 1, 3), ('S', 'q2', 2, 1), ('A', 'q0', 2, 1), ('S', 'q0', 3, 0), ('A', 'q2', 1, 1), ('S', 'q2', 2, 0), ('A', 'q0', 2, 0), ('A', 'd', 3, 0), ('A', 'q2', 1, 2), ('A', 'q1', 2, 1), ('S', 'q1', 3, 0), ('A', 'q2', 1, 0), ('A', 'q1', 2, 0), ('A', 'o', 3, 0), ('A', 'q2', 2, 1), ('S', 'q2', 3, 0), ('A', 'q0', 3, 0), ('A', 'q2', 2, 0), ('A', 'q1', 3, 0), ('A', 'q2', 3, 0)]


def mask_column(mask_ref, step, rows):
    m = mask_ref[...].astype(F32).T
    lane = lax.broadcasted_iota(jnp.int32, m.shape, 1)
    per = rows // 128
    parts = [
        jnp.sum(jnp.where(lane == step * per + j, m, 0.0), axis=1, keepdims=True) for j in range(per)
    ]
    return jnp.concatenate(parts, axis=0)


def flipped(me, bit):
    return me + (1 << bit) * (1 - 2 * ((me // (1 << bit)) % 2))


class Gather:
    ops = 8
    forwards = {0: (2, 3, 1), 2: (4, 5), 3: (6,), 4: (7,)}

    def __init__(self, me, tensor, items, send_sem, recv_sem):
        self.me, self.tensor, self.items, self.send_sem, self.recv_sem = me, tensor, items, send_sem, recv_sem

    def copy(self, i, op):
        src, dst, block, first, rows, yz = self.items[i]
        one, two = (1, 2) if yz else (2, 1)
        piece = self.me % 8
        if op in (4, 5, 7):
            piece = flipped(piece, one)
        if op in (6, 7):
            piece = flipped(piece, two)
        at = dst.at[pl.ds(pl.multiple_of(piece * block + first, 8), rows), :]
        if op == 0:
            device = {"tensor": 1 - self.tensor}
        else:
            bit = {1: 0, 2: one, 3: two, 4: two, 5: 0, 6: 0, 7: 0}[op]
            device = {"dp": flipped(self.me, bit)}
        k = i * self.ops + op
        return pltpu.make_async_remote_copy(
            src_ref=src.at[pl.ds(first, rows), :] if op == 0 else at,
            dst_ref=at,
            send_sem=self.send_sem.at[k],
            recv_sem=self.recv_sem.at[k],
            device_id=device,
            device_id_type=MESH,
        )

    def start(self, i):
        self.copy(i, 0).start()

    def after(self, i, op):
        self.copy(i, op).wait_recv()
        for other in self.forwards[op]:
            self.copy(i, other).start()

    def collect(self, i):
        for op in (1, 5, 6, 7):
            self.copy(i, op).wait_recv()

    def finish_send(self, i):
        for op in range(self.ops):
            self.copy(i, op).wait_send()


def greet_gather(me, tensor):
    barrier = pltpu.get_barrier_semaphore()
    pl.semaphore_signal(barrier, inc=1, device_id={"tensor": 1 - tensor}, device_id_type=MESH)
    for bit in range(3):
        pl.semaphore_signal(barrier, inc=1, device_id={"dp": flipped(me, bit)}, device_id_type=MESH)
    pl.semaphore_wait(barrier, 4)


class Reduce:
    def __init__(self, dp, me, swap, source, home, more, send_sem, recv_sem):
        self.dp, self.me, self.source, self.home, self.more = dp, me, source, home, more
        self.send_sem, self.recv_sem = send_sem, recv_sem
        self.hops = dp.bit_length() - 1
        self.order = list(range(self.hops))
        if swap:
            self.order[1], self.order[2] = 2, 1

    def block(self, j, m, keep):
        total = 0
        for i, bit in enumerate(self.order):
            mine = (self.me // (1 << bit)) % 2
            if i < j or (i == j and keep):
                total = total + mine * (1 << bit)
            elif i == j:
                total = total + (1 - mine) * (1 << bit)
            else:
                total = total + ((mine + m // (1 << (i - j - 1))) % 2) * (1 << bit)
        return total

    def count(self, j):
        return self.dp >> (j + 1)

    def base(self, j):
        return self.dp // 2 - (self.dp >> j)

    def copy(self, j, m):
        b = self.block(j, m, False)
        if j == 0:
            src, dst, k = self.source.at[b], self.home.at[b // 2], m
        else:
            at = self.base(j) + m
            src, dst, k = self.home.at[b // 2], self.more.at[at], self.dp // 2 + at
        return pltpu.make_async_remote_copy(
            src_ref=src,
            dst_ref=dst,
            send_sem=self.send_sem.at[k],
            recv_sem=self.recv_sem.at[k],
            device_id={"dp": flipped(self.me, self.order[j])},
            device_id_type=MESH,
        )

    def start(self, j, m):
        self.copy(j, m).start()

    def add(self, j, m, kept=None):
        self.copy(j, m).wait_recv()
        at = self.block(j, m, True) // 2
        if j > 0:
            ref, i = self.more, self.base(j) + m
        else:
            ref, i = (self.source, self.block(0, m, True)) if kept is None else (kept, m)
        rows = self.home.shape[1]
        if rows % 16 == 0:

            @pl.loop(0, rows // 16)
            def _(r):
                s = pl.ds(pl.multiple_of(r * 16, 16), 16)
                self.home[at, s, :] = self.home[at, s, :] + ref[i, s, :]
        else:
            self.home[at] = self.home[at] + ref[i]

    def finish_send(self, j, m):
        self.copy(j, m).wait_send()

    def every(self, j, do):
        n = self.count(j)
        if n > 8:

            @pl.loop(0, n)
            def _(m):
                do(m)
        else:
            for m in range(n):
                do(m)


def reduce_scratch(dp, rows, cols):
    return [
        pltpu.VMEM((dp // 2, rows, cols), F32),
        pltpu.VMEM((dp // 2 - 1, rows, cols), F32),
        pltpu.SemaphoreType.DMA((dp - 1,)),
        pltpu.SemaphoreType.DMA((dp - 1,)),
    ]


def store_blocks(out, value, at=slice(None)):
    rows = out.shape[1]
    n = value.shape[0] // rows
    if rows % 8 == 0:
        out[:, :, at] = value.reshape(n, rows, value.shape[1])
    else:
        for b in range(n):
            out[b, :, at] = value[b * rows : (b + 1) * rows, :]


def rope(x, cos, sin):
    lane = lax.broadcasted_iota(jnp.int32, x.shape, 1)
    other = jnp.where(lane % HD < HD // 2, pltpu.roll(x, 128 - HD // 2, 1), pltpu.roll(x, HD // 2, 1))
    return x * cos + other * sin


def project(y, width, cos, sin, q_ref, k_ref, v_ref):
    for c in range(0, width, 128):
        q_ref[:, c : c + 128] = rope(y[:, c : c + 128], cos, sin).astype(BF)
        k_ref[:, c : c + 128] = rope(y[:, width + c : width + c + 128], cos, sin).astype(BF)
    v_ref[...] = y[:, 2 * width :].astype(BF)


def attend_pair(q_ref, k_ref, v_ref, at, o_ref, lse_ref, pair, oT, sbuf):
    length = q_ref.shape[0]
    wide = sbuf.shape[2]
    kk = k_ref[:, at]
    qT, vT = q_ref[:, at].T, v_ref[:, at].T
    row = lax.broadcasted_iota(jnp.int32, (128, wide), 0)
    items = [(h, c) for h in range(2) for c in range(0, length, wide)]

    def scores(i):
        h, c = items[i]
        qq = qT[:, c : c + wide]
        s = dot(kk, jnp.where((row < HD) == (h == 0), qq, jnp.zeros_like(qq)))
        sbuf[i % 2] = s
        return jnp.max(s, axis=0, keepdims=True)

    top = scores(0)
    for i, (h, c) in enumerate(items):
        following = scores(i + 1) if i + 1 < len(items) else None
        p = jnp.exp2((sbuf[i % 2] - top) * C2)
        total = jnp.sum(p, axis=0, keepdims=True)
        oT[h * HD : (h + 1) * HD, c : c + wide] = dot(vT[h * HD : (h + 1) * HD, :], p.astype(BF)) * (1.0 / total)
        lse_ref[pl.ds(pair, 1), h : h + 1, c : c + wide] = (top * C2 + jnp.log2(total))[None]
        top = following
    o_ref[:, at] = oT[...].T.astype(BF)


def gelu_parts(x):
    c0, c1 = 0.7978845608028654, 0.044715
    x2 = x * x
    t = jnp.tanh(x * (c0 + (c0 * c1) * x2))
    a = 0.5 + 0.5 * t
    d = a + (x * (0.5 - 0.5 * (t * t))) * (c0 + (3.0 * c0 * c1) * x2)
    return x * a, d


def forward_kernel(
    nb, bucket, tok, mask, mvec, gain1, gain2, te, wada, bada, wq, cos, sin, bup,
    bup_h, wqf_h, wo_h, wup_h, wdown_h, cot_h,
    h1_ref, q_ref, k_ref, v_ref, mods_ref, cond_ref, o_ref, lse_ref, wxq_ref, wxo_ref,
    attn_ref, h2_ref, feed_ref, gh_ref, gbup_ref, du_ref, dd_ref, fu, fd, bupx,
    oT, sbuf, fq, fo, wo, wup, wdown, cot, act_s, gp_s, gf_s, lq, lo, lu, ld, pq, po, pu, pd,
    load_sem, send_sem, recv_sem, bup_sem,
):
    step = pl.program_id(0)
    me, tensor = lax.axis_index("dp"), lax.axis_index("tensor")
    cols = q_ref.shape[2]
    pairs = cols // 128
    width = tok.shape[1]
    items = []
    for p in range(pairs):
        n = pq.shape[1]
        items += [(pq.at[p], fq.at[p], n, i * (n // 2), n // 2, i == 0) for i in range(2)]
    for src, dst in ((po, fo), (pu, fu), (pd, fd)):
        n = src.shape[0]
        items += [(src, dst, n, i * (n // 2), n // 2, i == 0) for i in range(2)]
    gather = Gather(me, tensor, items, send_sem, recv_sem)
    pieces = []
    for i, (src, dst) in enumerate(((wqf_h, lq), (wo_h, lo), (wup_h, lu), (wdown_h, ld))):
        n = dst.shape[0]
        at = pl.ds(pl.multiple_of((me % 8) * n, 16), n)
        pieces.append(pltpu.make_async_copy(src.at[at, :], dst, load_sem.at[i]))
    loads = [
        pltpu.make_async_copy(src, dst, load_sem.at[4 + i])
        for i, (src, dst) in enumerate(((wo_h, wo), (wup_h, wup), (wdown_h, wdown), (cot_h, cot)))
    ]
    bias = pltpu.make_async_remote_copy(
        src_ref=bup_h, dst_ref=bupx, send_sem=bup_sem.at[0], recv_sem=bup_sem.at[1],
        device_id={"tensor": 1 - tensor}, device_id_type=MESH,
    )
    s_own, s_other = nb, nb + pairs
    s_mlp = s_other + pairs
    s_dw = s_mlp + nb

    @pl.when(step == 0)
    def _():
        for c in pieces:
            c.start()
        barrier = pltpu.get_barrier_semaphore()
        pl.semaphore_signal(barrier, inc=1, device_id={"tensor": 1 - tensor}, device_id_type=MESH)
        for bit in range(3):
            pl.semaphore_signal(barrier, inc=1, device_id={"dp": flipped(me, bit)}, device_id_type=MESH)
        for c in pieces:
            c.wait()
        for p in range(pairs):
            pq[p] = lq[:, p * 128 : (p + 1) * 128].astype(F32)
        for src, dst in ((lo, po), (lu, pu), (ld, pd)):
            dst[...] = src[...].astype(F32)
        pl.semaphore_wait(barrier, 4)
        for i in range(len(items)):
            gather.start(i)
        bias.start()
        for c in loads:
            c.start()

    for at, todo in FORWARD_PLAN.items():

        @pl.when(step == at)
        def _():
            for i, op in todo:
                gather.after(i, op)

    @pl.when(step == 0)
    def _():
        row = te[...]
        sub = lax.broadcasted_iota(jnp.int32, row.shape, 0)
        row = jnp.sum(jnp.where(sub == bucket[...], row, 0.0), axis=0, keepdims=True)
        row = row * (1.0 / (1.0 + jnp.exp(-row)))
        cond_ref[...] = row
        col = jnp.broadcast_to(row, (8, row.shape[1])).T[:, 0:1]
        bias_row = line(bada)
        for i in range(6):
            cs = slice(i * width, (i + 1) * width)
            mods_ref[i : i + 1, :] = jnp.sum(wada[:, cs].astype(F32) * col, axis=0, keepdims=True) + bias_row[:, cs]

    def block(first):
        return pl.ds(pl.multiple_of((step - first) * RB, RB), RB)

    @pl.when(step < s_own)
    def _():
        rows = block(0)
        x = tok[rows, :].astype(F32) + mask_column(mask, step, RB) * line(mvec)
        n, _ = normed(x)
        h = (n * (line(gain1) * (1.0 + mods_ref[1:2, :])) + mods_ref[0:1, :]).astype(BF)
        h1_ref[rows, :] = h
        y = jnp.concatenate([dot(h, wq[i]) for i in range(3)], axis=1)
        project(y, cols, cos[rows, :], sin[rows, :], q_ref.at[0, rows, :], k_ref.at[0, rows, :], v_ref.at[0, rows, :])

    def attend(half, pair):
        at = pl.ds(pl.multiple_of(pair * 128, 128), 128)
        attend_pair(
            q_ref.at[half], k_ref.at[half], v_ref.at[half], at, o_ref.at[half], lse_ref, half * pairs + pair, oT, sbuf
        )

    for p in range(pairs):

        @pl.when(step == s_other + p)
        def _():
            for i in (2 * p, 2 * p + 1):
                gather.collect(i)

    @pl.when((step >= s_other) & (step < s_mlp))
    def _():
        p = step - s_other
        at = pl.ds(pl.multiple_of(p * 128, 128), 128)
        for i in range(3):
            wxq_ref[i, :, at] = fq[p, i * width : (i + 1) * width, :].astype(BF)
        w = jnp.concatenate([wxq_ref[i, :, at] for i in range(3)], axis=1)
        for r in range(0, tok.shape[0], RB):
            rows = slice(r, r + RB)
            project(
                dot(h1_ref[rows, :], w), 128, cos[rows, :], sin[rows, :],
                q_ref.at[1, rows, at], k_ref.at[1, rows, at], v_ref.at[1, rows, at],
            )

    @pl.when((step >= s_own) & (step < s_mlp))
    def _():
        half = (step - s_own) // pairs
        attend(half, step - s_own - half * pairs)

    @pl.when(step == s_mlp)
    def _():
        for i in (2 * pairs, 2 * pairs + 1):
            gather.collect(i)
        wxo_ref[...] = fo[...].astype(BF)
        for c in loads:
            c.wait()
        gbup_ref[...] = jnp.zeros_like(gbup_ref)

    @pl.when((step >= s_mlp) & (step < s_dw))
    def _():
        rows = block(s_mlp)
        x = tok[rows, :].astype(F32) + mask_column(mask, step - s_mlp, RB) * line(mvec)
        attn = dot(o_ref[0, rows, :], wo[...]) + dot(o_ref[1, rows, :], wxo_ref[...])
        attn_ref[...] = attn
        n, _ = normed(x + mods_ref[2:3, :] * attn)
        h = (n * (line(gain2) * (1.0 + mods_ref[4:5, :])) + mods_ref[3:4, :]).astype(BF)
        h2_ref[rows, :] = h
        act, slope = gelu_parts(dot(h, wup[...]) + line(bup))
        act = act.astype(BF)
        act_s[rows, :] = act
        feed_ref[...] = dot(act, wdown[...])
        gf = (mods_ref[5:6, :] * cot[rows, :].astype(F32)).astype(BF)
        gf_s[rows, :] = gf
        gp = (dot(gf, wdown[...], 1, 1) * slope).astype(BF)
        gp_s[rows, :] = gp
        gh_ref[...] = dot(gp, wup[...], 1, 1)
        gbup_ref[...] += jnp.sum(gp.astype(F32), axis=0, keepdims=True)

    @pl.when(step >= s_dw)
    def _():
        part = width // 2
        cs = pl.ds(pl.multiple_of((step - s_dw) * part, 128), part)
        store_blocks(du_ref, dot(h2_ref[:, cs], gp_s[...], 0, 0))
        store_blocks(dd_ref, dot(gf_s[:, cs], act_s[...], 0, 0))

    @pl.when(step == pl.num_programs(0) - 1)
    def _():
        for i, op in FORWARD_END:
            gather.after(i, op)
        for i in range(2 * pairs + 2, len(items)):
            gather.collect(i)
        for i in range(len(items)):
            gather.finish_send(i)
        bias.wait()


def forward(dp, bucket, tokens, mask2, mvec, gain1, gain2, te, wada, bada, wq, cos, sin, bup, wo, wup, wdown, cot):
    rows, width = tokens.shape
    cols, ff = wq.shape[2], wup.shape[1]
    nb, pairs = rows // RB, cols // 128
    s_mlp = nb + 2 * pairs
    mblk = pl.BlockSpec((RB, width), lambda i: (jnp.clip(i - s_mlp, 0, nb - 1), 0))
    dblk = pl.BlockSpec((dp // 2, width // dp, ff), lambda i: (jnp.maximum(i - s_mlp - nb, 0), 0, 0))
    act = (2, rows, cols)
    wqf = wq.reshape(3 * width, cols)
    vm = pltpu.VMEM
    piece = lambda w: (w.shape[0] // 8, w.shape[1])
    n_items = 2 * pairs + 6
    return pl.pallas_call(
        functools.partial(forward_kernel, nb),
        grid=(s_mlp + nb + 2,),
        in_specs=[
            one(x.shape) for x in (bucket, tokens, mask2, mvec, gain1, gain2, te, wada, bada, wq, cos, sin, bup)
        ] + [ANYS] * 6,
        out_specs=[
            one((rows, width)), one(act), one(act), one(act), one((8, width)), one((1, te.shape[1])),
            one(act), one((2 * pairs, 2, rows)), one(wq.shape), one((cols, width)),
            mblk, one((rows, width)), mblk, mblk, one((1, ff)), dblk, dblk, ANYS, ANYS, ANYS,
        ],
        out_shape=[
            sds((rows, width), BF), sds(act, BF), sds(act, BF), sds(act, BF), sds((8, width), F32),
            sds((1, te.shape[1]), F32), sds(act, BF), sds((2 * pairs, 2, rows), F32), sds(wq.shape, BF),
            sds((cols, width), BF), sds((rows, width), F32), sds((rows, width), BF), sds((rows, width), F32),
            sds((rows, width), F32), sds((1, ff), F32), sds((dp, width // dp, ff), F32),
            sds((dp, width // dp, ff), F32), sds(wup.shape, F32), sds(wdown.shape, F32), sds(bup.shape, F32),
        ],
        scratch_shapes=[
            vm((128, rows), F32), vm((2, rows, 512), F32), vm((pairs, 3 * width, 128), F32), vm(wo.shape, F32),
            vm(wo.shape, BF), vm(wup.shape, BF), vm(wdown.shape, BF), vm(cot.shape, BF),
            vm((rows, ff), BF), vm((rows, ff), BF), vm((rows, width), BF),
            *[vm(piece(w), BF) for w in (wqf, wo, wup, wdown)],
            vm((pairs, piece(wqf)[0], 128), F32), *[vm(piece(w), F32) for w in (wo, wup, wdown)],
            pltpu.SemaphoreType.DMA((8,)), pltpu.SemaphoreType.DMA((8 * n_items,)),
            pltpu.SemaphoreType.DMA((8 * n_items,)), pltpu.SemaphoreType.DMA((2,)),
        ],
        compiler_params=params(collective_id=2, has_side_effects=True),
        name="forward",
    )(bucket, tokens, mask2, mvec, gain1, gain2, te, wada, bada, wq, cos, sin, bup, bup, wqf, wo, wup, wdown, cot)


def mlp_other_kernel(
    dp, tok, mask, mvec, mods, gain, attn_ref, h_ref, feed_ref, gh_ref, cot, bup, bdown,
    mo, wo, wx, gbup, cond, du, dd, fu, fd,
    res_ref, gmid_ref, gm_ref, small, dw_ref, hu_out, hd_out,
    acc, keep_u, keep_d, load_sem, stage_u, stage_d, wup, wdown, w_sem,
    hu, more_u, send_u, recv_u, hd, more_d, send_d, recv_d,
):
    step, last = pl.program_id(0), pl.num_programs(0) - 1
    me, tensor = lax.axis_index("dp"), lax.axis_index("tensor")
    weights = {
        "u": (Reduce(dp, me, False, du, hu, more_u, send_u, recv_u), keep_u),
        "d": (Reduce(dp, me, True, dd, hd, more_d, send_d, recv_d), keep_d),
    }

    def load(w, m):
        r, keep = weights[w]
        k = "ud".index(w)
        return pltpu.make_async_copy(r.source.at[r.block(0, m, True)], keep.at[m], load_sem.at[k, m])

    def act(kind, w, j, m):
        r, keep = weights[w]
        if kind == "S":
            r.start(j, m)
        elif j == 0:
            load(w, m).wait()
            r.add(j, m, keep)
        else:
            r.add(j, m)

    wloads = [
        pltpu.make_async_copy(src, dst, w_sem.at[i]) for i, (src, dst) in enumerate(((fu, stage_u), (fd, stage_d)))
    ]

    @pl.when(step == 0)
    def _():
        for c in wloads:
            c.start()
        barrier = pltpu.get_barrier_semaphore()
        for j in range(3):
            pl.semaphore_signal(barrier, inc=1, device_id={"dp": flipped(me, j)}, device_id_type=MESH)
        pl.semaphore_wait(barrier, 3)
        small[...] = jnp.zeros_like(small)

    if dp == 16:
        for at, todo in MLP_PLAN.items():

            @pl.when(step == min(at, 3))
            def _():
                if at == 0:
                    for w, (r, _keep) in weights.items():
                        r.every(0, lambda m: load(w, m).start())
                if at < 4:
                    for a in todo:
                        act(*a)
    else:

        @pl.when(step == 0)
        def _():
            for w, (r, _keep) in weights.items():
                r.every(0, lambda m: load(w, m).start())
                r.every(0, lambda m: r.start(0, m))

    @pl.when(step == 0)
    def _():
        for c, src, dst in zip(wloads, (stage_u, stage_d), (wup, wdown)):
            c.wait()
            dst[...] = src[...].astype(BF)

    x = tok[...].astype(F32) + mask_column(mask, step, tok.shape[0]) * line(mvec)
    attn = attn_ref[...]
    middle = x + mods[2:3, :] * attn
    n2, rs = normed(middle)
    ac, slope = gelu_parts(dot(h_ref[...], wup[...]) + line(bup))
    feed = (feed_ref[...] + dot(ac.astype(BF), wdown[...])) + line(bdown)
    g = cot[...].astype(F32)
    res_ref[...] = (middle + mods[5:6, :] * feed).astype(BF)
    gf = (mods[5:6, :] * g).astype(BF)
    gp = (dot(gf, wdown[...], 1, 1) * slope).astype(BF)
    gh = gh_ref[...] + dot(gp, wup[...], 1, 1)
    opened = 1.0 + mods[4:5, :]
    e = gh * (opened * line(gain))
    inner = jnp.mean(e * n2, axis=-1, keepdims=True)
    gmid = g + (e - jnp.mean(e, axis=-1, keepdims=True) - n2 * inner) * rs
    gmid_ref[...] = gmid
    ga = (mods[2:3, :] * gmid).astype(BF)
    gm_ref[0] = dot(ga, wo[...], 1, 1).astype(BF)
    gm_ref[1] = dot(ga, wx[...], 1, 1).astype(BF)
    col = lambda v: jnp.sum(v, axis=0, keepdims=True)
    small[0:1, :] += col(g * feed)
    small[1:2, :] += col(gf.astype(F32))
    small[2:3, :] += col(gh)
    small[3:4, :] += col(gh * n2)
    small[4:5, :] += col(gmid * attn)
    dw = dot(ga, mo[...], 0, 0)

    @pl.when(step == 0)
    def _():
        acc[...] = dw

    @pl.when(step > 0)
    def _():
        acc[...] += dw

    @pl.when(step == last)
    def _():
        width = mods.shape[1]
        small[5:6, :] = small[3:4, :] * opened
        small[3:4, :] = small[3:4, :] * line(gain)
        for i in range(gbup.shape[1] // width):
            small[8 + i : 9 + i, :] = gbup[:, i * width : (i + 1) * width]
        small[6:7, 0 : cond.shape[1]] = cond[...]
        store_blocks(dw_ref, acc[...])
        if dp == 16:
            for a in MLP_PLAN.get(4, []):
                act(*a)
            for todo in MLP_PLAN.values():
                for kind, w, j, m in todo:
                    if kind == "S":
                        weights[w][0].finish_send(j, m)
        else:
            for w, (r, keep) in weights.items():

                def one_block(m):
                    load(w, m).wait()
                    r.add(0, m, keep)
                    r.finish_send(0, m)

                r.every(0, one_block)
        stores = [
            pltpu.make_async_copy(src, dst, w_sem.at[k]) for k, (src, dst) in enumerate(((hu, hu_out), (hd, hd_out)))
        ]
        for c in stores:
            c.start()
        for c in stores:
            c.wait()


def mlp_other(dp, tokens, mask2, mvec, mods, gain, attn, h, feed, gh, cot, bup, bdown, os, wo, wx, gbup, cond, du, dd, fu, fd):
    rows, width = tokens.shape
    ff, cols = fu.shape[1], wo.shape[0]
    part = width // dp
    blk = lambda c: pl.BlockSpec((RB, c), lambda i: (i, 0))
    half = (dp // 2, part, ff)
    vm = pltpu.VMEM
    return pl.pallas_call(
        functools.partial(mlp_other_kernel, dp),
        grid=(rows // RB,),
        in_specs=[
            blk(width), one(mask2.shape), one(mvec.shape), one(mods.shape), one(gain.shape),
            blk(width), blk(width), blk(width), blk(width), blk(width), one(bup.shape), one(bdown.shape),
            pl.BlockSpec((None, RB, cols), lambda i: (0, i, 0)), one(wo.shape), one(wx.shape), one(gbup.shape),
            one(cond.shape), ANYS, ANYS, ANYS, ANYS,
        ],
        out_specs=[
            blk(width), blk(width), pl.BlockSpec((2, RB, cols), lambda i: (0, i, 0)), one((16, width)),
            one((dp, part, cols)), ANYS, ANYS,
        ],
        out_shape=[
            sds((rows, width), BF), sds((rows, width), F32), sds((2, rows, cols), BF), sds((16, width), F32),
            sds((dp, part, cols), F32), sds(half, F32), sds(half, F32),
        ],
        scratch_shapes=[
            vm((width, cols), F32), vm(half, F32), vm(half, F32), pltpu.SemaphoreType.DMA((2, dp // 2)),
            vm(fu.shape, F32), vm(fd.shape, F32), vm(fu.shape, BF), vm(fd.shape, BF), pltpu.SemaphoreType.DMA((2,)),
            *reduce_scratch(dp, part, ff), *reduce_scratch(dp, part, ff),
        ],
        compiler_params=params(collective_id=3, has_side_effects=True),
        name="mlp_other",
    )(tokens, mask2, mvec, mods, gain, attn, h, feed, gh, cot, bup, bdown, os, wo, wx, gbup, cond, du, dd, fu, fd)


def attend_back_pair(q_ref, k_ref, v_ref, o_ref, do_ref, lse_ref, cosT, sinT, g_ref, at, gT, between):
    length = q_ref.shape[0]
    kk, vv = k_ref[...], v_ref[...]
    kT, qT, doT = kk.T, q_ref[...].T, do_ref[...].T
    oT = o_ref[...].T
    prod = doT.astype(F32) * oT.astype(F32)
    row = lax.broadcasted_iota(jnp.int32, (128, length), 0)
    half = HD // 2
    for h in range(2):
        hs = slice(h * HD, (h + 1) * HD)
        sel = (row < HD) == (h == 0)
        qm = jnp.where(sel, qT, jnp.zeros_like(qT))
        dm = jnp.where(sel, doT, jnp.zeros_like(doT))
        inner = jnp.sum(prod[hs, :], axis=0, keepdims=True)
        p = jnp.exp2(dot(kk, qm) * C2 - lse_ref[h : h + 1, :])
        ds = (p * (dot(vv, dm) - inner)).astype(BF)
        dv = dot(doT[hs, :], p.astype(BF), 1, 1)
        dk = dot(qT[hs, :], ds, 1, 1) * 0.125
        dq = dot(kT[hs, :], ds) * 0.125
        c, s = cosT[...], sinT[...]
        for i, d in ((0, dq), (1, dk)):
            a, b = d[:half, :], d[half:, :]
            gT[i, h * HD : h * HD + half, :] = a * c + b * s
            gT[i, h * HD + half : (h + 1) * HD, :] = b * c - a * s
        gT[2, hs, :] = dv
        if h == 0:
            between()
    for i in range(3):
        g_ref[i, :, at] = gT[i].T.astype(BF)


def backward_kernel(
    dp, nb, pairs, q_ref, k_ref, v_ref, o_ref, do_ref, lse_ref, cosT, sinT, h1, w, wx, tok, mask, mvec,
    mods, gain, gmid_ref, small, dw_hbm, hu_in, hd_in,
    gt_ref, up_ref, down_ref, out_ref, qkv_ref, got_ref,
    gT, g, dw_out, dqs, late_s, pack, got, own_sem, gsend, grecv, load_sem, *scratch,
):
    step, last = pl.program_id(0), pl.num_programs(0) - 1
    me, tensor = lax.axis_index("dp"), lax.axis_index("tensor")
    names = ["u", "d", "o"] + [f"q{p}" for p in range(pairs)]
    sources = [None, None, dw_out] + [dqs.at[p] for p in range(pairs)]
    weights = {
        n: Reduce(dp, me, n == "d", src, *scratch[4 * i : 4 * i + 4]) for i, (n, src) in enumerate(zip(names, sources))
    }
    hops = weights["u"].hops
    width, cols = mods.shape[1], w.shape[2]
    loads = [
        pltpu.make_async_copy(src, dst, load_sem.at[i])
        for i, (src, dst) in enumerate(((dw_hbm, dw_out), (hu_in, weights["u"].home), (hd_in, weights["d"].home)))
    ]
    s_x, s_end = pairs, 2 * pairs

    def act(kind, n, j, m):
        if kind == "S":
            weights[n].start(j, m)
        else:
            weights[n].add(j, m)

    def point(at):
        if dp == 16 and at in BACK_PLAN:

            @pl.when(step == at[0])
            def _():
                for a in BACK_PLAN[at]:
                    act(*a)

    def spread(r):
        to = (me + r) % dp
        return pltpu.make_async_remote_copy(
            src_ref=pack.at[to], dst_ref=got.at[me], send_sem=gsend.at[r], recv_sem=grecv.at[r],
            device_id=(to, tensor), device_id_type=MESH,
        )

    @pl.when(step == 0)
    def _():
        for c in loads:
            c.start()
        barrier = pltpu.get_barrier_semaphore()

        @pl.loop(1, dp)
        def _(r):
            pl.semaphore_signal(barrier, inc=1, device_id=((me + r) % dp, tensor), device_id_type=MESH)

        pl.semaphore_wait(barrier, dp - 1)
        for c in loads:
            c.wait()
        late_s[...] = jnp.zeros_like(late_s)

    for i in range(2 * pairs + nb):
        point((i, 0))

    def between():
        for p in range(2 * pairs):
            point((p, 1))

    @pl.when(step < s_end)
    def _():
        half = step // pairs
        at = pl.ds(pl.multiple_of((step - half * pairs) * 128, 128), 128)
        attend_back_pair(q_ref, k_ref, v_ref, o_ref, do_ref, lse_ref, cosT, sinT, g.at[half], at, gT, between)

    @pl.when(step < s_x)
    def _():
        at = pl.ds(pl.multiple_of(step * 128, 128), 128)
        gp = jnp.concatenate([g[0, i, :, at] for i in range(3)], axis=1)
        store_blocks(dqs.at[step], dot(h1[...], gp, 0, 0))

    @pl.when(step >= s_end)
    def _():
        i = step - s_end
        rows = pl.ds(pl.multiple_of(i * RB, RB), RB)
        m = mask_column(mask, i, RB)
        n1, rs = normed(tok[...].astype(F32) + m * line(mvec))
        parts = [
            dot(d[0, rows, :], ww[0], 1, 1) + dot(d[1, rows, :], ww[1], 1, 1) + dot(d[2, rows, :], ww[2], 1, 1)
            for d, ww in ((g.at[0], w), (g.at[1], wx))
        ]
        gh = parts[0] + parts[1]
        e = gh * ((1.0 + mods[1:2, :]) * line(gain))
        inner = jnp.mean(e * n1, axis=-1, keepdims=True)
        gs = gmid_ref[...] + (e - jnp.mean(e, axis=-1, keepdims=True) - n1 * inner) * rs
        gt_ref[...] = gs.astype(BF)
        col = lambda v: jnp.sum(v, axis=0, keepdims=True)
        late_s[0:1, :] += col(gh)
        late_s[1:2, :] += col(gh * n1)
        late_s[3:4, :] += col(m * gs)

    @pl.when(step == last)
    def _():
        n = width // dp
        late_s[2:3, :] = late_s[1:2, :] * (1.0 + mods[1:2, :])
        late_s[1:2, :] = late_s[1:2, :] * line(gain)
        pack[...] = jnp.zeros_like(pack)
        summed = [late_s[3:4, :], late_s[2:3, :], small[5:6, :], small[1:2, :], small[8:9, :], small[9:10, :]]
        gmod = [late_s[0:1, :], late_s[1:2, :], small[4:5, :], small[2:3, :], small[3:4, :], small[0:1, :]]
        cond = small[6:7, 0:128]
        for d in range(dp):
            for i in range(4):
                pack[d, :, i * n : (i + 1) * n] = summed[i][:, d * n : (d + 1) * n]
            first = 2 * n * d
            row, off = 4 + first // width, first % width
            pack[d, :, 4 * n : 6 * n] = summed[row][:, off : off + 2 * n]
            done, need = 0, 6 * n
            while done < need:
                first = need * d + done
                row, off = first // width, first % width
                take = min(need - done, width - off)
                pack[d, :, PACK_MOD + done : PACK_MOD + done + take] = gmod[row][:, off : off + take]
                done += take
            pack[d, :, PACK_COND : PACK_COND + 128] = cond
        if dp == 16:
            for a in BACK_END[:2]:
                act(*a)
        own = pltpu.make_async_copy(pack.at[me], got.at[me], own_sem)
        own.start()

        @pl.loop(1, dp)
        def _(r):
            spread(r).start()

        if dp == 16:
            for a in BACK_END[2:]:
                act(*a)
            todo = [a for v in BACK_PLAN.values() for a in v] + BACK_END
            for kind, n, j, m in todo:
                if kind == "S":
                    weights[n].finish_send(j, m)
        else:
            for n, r in weights.items():
                for j in range(1 if n in "ud" else 0, hops):
                    r.every(j, lambda m: r.start(j, m))
                    r.every(j, lambda m: r.add(j, m))
                    r.every(j, lambda m: r.finish_send(j, m))
        up_ref[...] = weights["u"].home[me // 2]
        down_ref[...] = weights["d"].home[me // 2]
        out_ref[...] = weights["o"].home[me // 2]
        for p in range(pairs):
            qkv_ref[p] = weights[f"q{p}"].home[me // 2]
        own.wait()

        @pl.loop(1, dp)
        def _(r):
            spread(r).wait()

        got_ref[...] = got[...]


PACK_MOD, PACK_COND, PACK = 384, 768, 896


def backward(dp, qs, ks, vs, os, gm, lses, cosT, sinT, h1, w, wx, tokens, mask2, mvec, mods, gain, gmid, small, dw_out, hu, hd):
    rows, width = tokens.shape
    cols = w.shape[2]
    nb, pairs = rows // RB, cols // 128
    part, ff = hu.shape[1], hu.shape[2]
    s_end = 2 * pairs
    pick = lambda i: jnp.minimum(i, 2 * pairs - 1)
    pair = pl.BlockSpec((None, rows, 128), lambda i: (pick(i) // pairs, 0, pick(i) % pairs))
    blk = pl.BlockSpec((RB, width), lambda i: (jnp.maximum(i - s_end, 0), 0))
    vm = pltpu.VMEM
    return pl.pallas_call(
        functools.partial(backward_kernel, dp, nb, pairs),
        grid=(s_end + nb,),
        in_specs=[pair] * 5 + [
            pl.BlockSpec((None, 2, rows), lambda i: (pick(i), 0, 0)), one(cosT.shape), one(sinT.shape),
            one(h1.shape), one(w.shape), one(wx.shape), blk, one(mask2.shape), one(mvec.shape), one(mods.shape),
            one(gain.shape), blk, one(small.shape), ANYS, ANYS, ANYS,
        ],
        out_specs=[
            blk, one((part, ff)), one((part, ff)), one((part, cols)), one((pairs, part, 384)), one((dp, 1, PACK)),
        ],
        out_shape=[
            sds((rows, width), BF), sds((part, ff), F32), sds((part, ff), F32), sds((part, cols), F32),
            sds((pairs, part, 384), F32), sds((dp, 1, PACK), F32),
        ],
        scratch_shapes=[
            vm((3, 128, rows), F32), vm((2, 3, rows, cols), BF), vm((dp, part, cols), F32),
            vm((pairs, dp, part, 384), F32), vm((8, width), F32), vm((dp, 1, PACK), F32), vm((dp, 1, PACK), F32),
            pltpu.SemaphoreType.DMA, pltpu.SemaphoreType.DMA((dp,)), pltpu.SemaphoreType.DMA((dp,)),
            pltpu.SemaphoreType.DMA((3,)),
            *reduce_scratch(dp, part, ff), *reduce_scratch(dp, part, ff), *reduce_scratch(dp, part, cols),
            *[s for _ in range(pairs) for s in reduce_scratch(dp, part, 384)],
        ],
        compiler_params=params(collective_id=4, has_side_effects=True),
        name="backward",
    )(qs, ks, vs, os, gm, lses, cosT, sinT, h1, w, wx, tokens, mask2, mvec, mods, gain, gmid, small, dw_out, hu, hd)


def finish_kernel(got, up, down, out, qkv, mask, ln1, wqkv, wout, ln2, wup, bup, wdown, bdown, wada, bada):
    dp = got.shape[0]
    g = got[...].reshape(dp, got.shape[2])
    n = wup.shape[0]
    total = jnp.sum(g, axis=0, keepdims=True)
    for i, ref in enumerate((mask, ln1, ln2, bdown)):
        ref[...] = total[:, i * n : (i + 1) * n].reshape(n)
    bup[...] = total[:, 4 * n : 6 * n].reshape(2 * n)
    bada[...] = total[:, PACK_MOD : PACK_MOD + 6 * n].reshape(6 * n)
    wada[...] = lax.dot_general(
        g[:, PACK_COND : PACK_COND + wada.shape[0]], g[:, PACK_MOD : PACK_MOD + 6 * n], (((0,), (0,)), ((), ())),
        precision=lax.Precision.HIGHEST, preferred_element_type=F32,
    )
    wup[...] = up[...]
    wdown[...] = down[...].T
    wout[...] = out[...].T
    for p in range(qkv.shape[0]):
        for i in range(3):
            wqkv[i, :, p * 128 : (p + 1) * 128] = qkv[p, :, i * 128 : (i + 1) * 128]


def finish(got, up, down, out, qkv, tdim):
    n, ff = up.shape
    cols = out.shape[1]
    shapes = [(n,), (n,), (3, n, cols), (cols, n), (n,), (n, ff), (2 * n,), (ff, n), (n,), (tdim, 6 * n), (6 * n,)]
    ins = (got, up, down, out, qkv)
    return pl.pallas_call(
        finish_kernel,
        in_specs=[pl.BlockSpec(memory_space=pltpu.VMEM)] * len(ins),
        out_specs=[pl.BlockSpec(memory_space=pltpu.VMEM)] * len(shapes),
        out_shape=[sds(s, F32) for s in shapes],
        compiler_params=params(),
        name="finish",
    )(*ins)


def rope_tables(length):
    half = HD // 2
    freq = 10000.0 ** (-(np.arange(half, dtype=np.float64) / half))
    angle = np.arange(length, dtype=np.float64)[:, None] * freq[None, :]
    return np.cos(angle).astype(np.float32), np.sin(angle).astype(np.float32)


def body(
    dp, tokens, cotangent, bucket, mask, time_embed, mask_vec, ln1_gain, w_qkv, w_out, ln2_gain,
    w_up, b_up, w_down, b_down, w_ada, b_ada,
):
    rows, width = tokens.shape
    mask2 = mask.reshape(rows // 128, 128)
    c, s = rope_tables(rows)
    cos, sin = jnp.asarray(np.tile(c, (1, 4))), jnp.asarray(np.tile(np.concatenate([-s, s], 1), (1, 2)))
    cosT, sinT = jnp.asarray(np.ascontiguousarray(c.T)), jnp.asarray(np.ascontiguousarray(s.T))
    (h1, qs, ks, vs, mods, cond, os, lses, wx_qkv, wx_out, attn, h2, feed, gh2, gbup, du, dd, fu, fd, bup_x) = forward(
        dp, bucket.reshape(1, 1), tokens, mask2, mask_vec, ln1_gain, ln2_gain, time_embed, w_ada, b_ada, w_qkv,
        cos, sin, b_up, w_out, w_up, w_down, cotangent,
    )
    result, gmid, gm, small, dw_out, hu, hd = mlp_other(
        dp, tokens, mask2, mask_vec, mods, ln2_gain, attn, h2, feed, gh2, cotangent, bup_x, b_down,
        os, w_out, wx_out, gbup, cond, du, dd, fu, fd,
    )
    grad_tokens, sum_up, sum_down, sum_out, sum_qkv, got = backward(
        dp, qs, ks, vs, os, gm, lses, cosT, sinT, h1, w_qkv, wx_qkv, tokens, mask2, mask_vec, mods, ln1_gain, gmid,
        small, dw_out, hu, hd,
    )
    rest = finish(got, sum_up, sum_down, sum_out, sum_qkv, time_embed.shape[1])
    return (result, grad_tokens, *rest)


def solution(mesh):
    in_specs = (
        P("dp", None), P("dp", None), P("dp"), P("dp"), P(), P(), P(), P(None, None, "tensor"),
        P("tensor", None), P(), P(None, "tensor"), P("tensor"), P("tensor", None), P(), P(), P(),
    )
    out_specs = (
        P("dp", None), P("dp", None), P("dp"), P("dp"), P(None, "dp", "tensor"), P("tensor", "dp"),
        P("dp"), P("dp", "tensor"), P(("tensor", "dp")), P("tensor", "dp"), P("dp"), P(None, "dp"), P("dp"),
    )
    step = functools.partial(body, mesh.shape["dp"])
    return jax.shard_map(step, mesh=mesh, in_specs=in_specs, out_specs=out_specs, check_vma=False)
```

```python
import functools

import jax
import jax.numpy as jnp
import numpy as np
from jax import lax
from jax.experimental import pallas as pl
from jax.experimental.pallas import tpu as pltpu
from jax.sharding import PartitionSpec as P

HD = 64
EPS = 1e-05
LOG2E = 1.4426950408889634
C2 = 0.125 * LOG2E
BF = jnp.bfloat16
F32 = jnp.float32
AXES = ("dp", "tensor")
MESH = pl.DeviceIdType.MESH
RB = 256
VMEM_ALL = 67_000_000


def dot(a, b, ca=1, cb=0):
    return lax.dot_general(a, b, (((ca,), (cb,)), ((), ())), preferred_element_type=F32)


def sds(shape, dtype):
    return jax.ShapeDtypeStruct(shape, dtype)


def one(shape):
    return pl.BlockSpec(shape, lambda *_: (0,) * len(shape), pipeline_mode=pl.Buffered(1))


ANYS = pl.BlockSpec(memory_space=pl.ANY)


def line(ref):
    v = ref[...]
    return v.reshape(1, v.shape[0])


def params(**kw):
    return pltpu.CompilerParams(vmem_limit_bytes=VMEM_ALL, **kw)


def normed(x):
    mean = jnp.mean(x, axis=-1, keepdims=True)
    cent = x - mean
    var = jnp.mean(cent * cent, axis=-1, keepdims=True)
    rs = lax.rsqrt(var + EPS)
    return cent * rs, rs


FORWARD_PLAN = {
    3: [(0, 0), (1, 0)],
    4: [(2, 0)],
    5: [(0, 2), (0, 3), (3, 0), (4, 0)],
    6: [(1, 2), (1, 3), (2, 2), (2, 3), (5, 0), (6, 0)],
    7: [(0, 4), (3, 2), (3, 3), (4, 2), (7, 0), (4, 3), (1, 4)],
    8: [(2, 4), (3, 4), (5, 2), (5, 3), (6, 2), (6, 3), (8, 0), (4, 4), (7, 3)],
    9: [(5, 4), (6, 4), (7, 2), (9, 0)],
    10: [(7, 4), (8, 2), (8, 3), (10, 0)],
    11: [(9, 2), (9, 3), (11, 0)],
    12: [(8, 4), (12, 0)],
    13: [(10, 2)],
    14: [(9, 4), (11, 2), (13, 0)],
}
FORWARD_END = [(12, 2), (13, 2)]
MLP_PLAN = {
    (0, 0): [('S', 'u', 1, 3), ('S', 'd', 1, 3), ('S', 'u', 1, 1), ('S', 'd', 1, 1), ('S', 'u', 1, 2), ('S', 'd', 1, 2)],
    (1, 1): [('A', 'u', 1, 3), ('A', 'd', 1, 3)],
    (2, 1): [('A', 'u', 1, 1), ('A', 'd', 1, 1)],
}
MLP_END = [('A', 'u', 1, 2), ('A', 'd', 1, 2)]
BACK_PLAN = {
    (0, 0): [('S', 'o', 0, 7), ('S', 'o', 0, 3), ('S', 'o', 0, 5), ('S', 'o', 0, 6), ('S', 'o', 0, 1), ('S', 'o', 0, 2), ('S', 'o', 0, 4), ('S', 'o', 0, 0), ('S', 'u', 1, 0), ('S', 'd', 1, 0), ('S', 'u', 2, 1), ('S', 'd', 2, 1), ('S', 'u', 2, 0), ('S', 'd', 2, 0)],
    (0, 1): [('A', 'o', 0, 7), ('A', 'o', 0, 3), ('A', 'o', 0, 5), ('A', 'o', 0, 6), ('A', 'o', 0, 1), ('A', 'o', 0, 2), ('A', 'o', 0, 4), ('A', 'o', 0, 0), ('S', 'o', 1, 3), ('S', 'o', 1, 1), ('S', 'o', 1, 2), ('S', 'o', 1, 0)],
    (1, 0): [('S', 'q0', 0, 7), ('S', 'q0', 0, 3), ('S', 'q0', 0, 5), ('S', 'q0', 0, 6), ('S', 'q0', 0, 1), ('S', 'q0', 0, 2), ('S', 'q0', 0, 4), ('S', 'q0', 0, 0)],
    (1, 1): [('A', 'u', 1, 0), ('A', 'd', 1, 0), ('A', 'q0', 0, 7), ('A', 'q0', 0, 3), ('A', 'q0', 0, 5), ('A', 'q0', 0, 6), ('A', 'q0', 0, 1), ('A', 'q0', 0, 2), ('A', 'q0', 0, 4), ('A', 'q0', 0, 0), ('S', 'q0', 1, 3), ('S', 'q0', 1, 1), ('S', 'q0', 1, 2), ('S', 'q0', 1, 0)],
    (2, 0): [('S', 'q1', 0, 7), ('S', 'q1', 0, 3), ('S', 'q1', 0, 5), ('S', 'q1', 0, 6), ('S', 'q1', 0, 1), ('S', 'q1', 0, 2), ('S', 'q1', 0, 4), ('S', 'q1', 0, 0)],
    (2, 1): [('A', 'u', 2, 1), ('A', 'd', 2, 1), ('A', 'q1', 0, 7), ('A', 'q1', 0, 3), ('A', 'q1', 0, 5), ('A', 'q1', 0, 6), ('A', 'q1', 0, 1), ('A', 'q1', 0, 2), ('A', 'q1', 0, 4), ('A', 'q1', 0, 0), ('S', 'q1', 1, 3), ('S', 'q1', 1, 1), ('S', 'q1', 1, 2), ('S', 'q1', 1, 0), ('S', 'u', 3, 0), ('S', 'd', 3, 0)],
    (3, 0): [('A', 'u', 2, 0), ('A', 'd', 2, 0), ('S', 'q2', 0, 7), ('S', 'q2', 0, 3), ('S', 'q2', 0, 5), ('S', 'q2', 0, 6), ('S', 'q2', 0, 1), ('S', 'q2', 0, 2), ('S', 'q2', 0, 4), ('S', 'q2', 0, 0)],
    (3, 1): [('A', 'o', 1, 3), ('A', 'q2', 0, 7), ('A', 'q2', 0, 3), ('A', 'q2', 0, 5), ('A', 'q2', 0, 6), ('A', 'o', 1, 1), ('A', 'q2', 0, 1), ('A', 'q2', 0, 2), ('A', 'q2', 0, 4), ('A', 'q2', 0, 0), ('S', 'q2', 1, 3), ('S', 'q2', 1, 1), ('S', 'q2', 1, 2), ('S', 'q2', 1, 0), ('S', 'o', 2, 1), ('S', 'o', 2, 0)],
    (4, 0): [('A', 'o', 1, 2), ('A', 'o', 1, 0)],
    (4, 1): [('A', 'q0', 1, 3), ('S', 'q0', 2, 1)],
    (5, 0): [('A', 'q0', 1, 1), ('A', 'q0', 1, 2), ('S', 'q0', 2, 0)],
    (5, 1): [('A', 'u', 3, 0), ('A', 'q0', 1, 0), ('A', 'q1', 1, 3), ('S', 'q1', 2, 1)],
    (6, 0): [('A', 'q1', 1, 1), ('A', 'q1', 1, 2), ('S', 'q1', 2, 0)],
    (7, 0): [('A', 'q1', 1, 0), ('A', 'o', 2, 1), ('S', 'o', 3, 0)],
    (8, 0): [('A', 'q2', 1, 3), ('A', 'o', 2, 0), ('S', 'q2', 2, 1)],
    (9, 0): [('A', 'q2', 1, 1), ('A', 'q0', 2, 1), ('S', 'q2', 2, 0), ('S', 'q0', 3, 0)],
}
BACK_END = [('A', 'q2', 1, 2), ('A', 'q0', 2, 0), ('A', 'd', 3, 0), ('A', 'q2', 1, 0), ('A', 'q1', 2, 1), ('S', 'q1', 3, 0), ('A', 'q1', 2, 0), ('A', 'o', 3, 0), ('A', 'q2', 2, 1), ('S', 'q2', 3, 0), ('A', 'q0', 3, 0), ('A', 'q2', 2, 0), ('A', 'q1', 3, 0), ('A', 'q2', 3, 0)]


def mask_column(mask_ref, step, rows):
    m = mask_ref[...].astype(F32).T
    lane = lax.broadcasted_iota(jnp.int32, m.shape, 1)
    per = rows // 128
    parts = [
        jnp.sum(jnp.where(lane == step * per + j, m, 0.0), axis=1, keepdims=True) for j in range(per)
    ]
    return jnp.concatenate(parts, axis=0)


def flipped(me, bit):
    return me + (1 << bit) * (1 - 2 * ((me // (1 << bit)) % 2))


class Gather:
    ops = 8
    forwards = {0: (2, 3, 1), 2: (4, 5), 3: (6,), 4: (7,)}

    def __init__(self, me, tensor, items, send_sem, recv_sem):
        self.me, self.tensor, self.items, self.send_sem, self.recv_sem = me, tensor, items, send_sem, recv_sem

    def copy(self, i, op):
        src, dst, base, block, first, rows, yz, quarters = self.items[i]
        one, two = (1, 2) if yz else (2, 1)
        piece = self.me % 8
        if quarters:
            piece = self.me % 2 + 2 * ((self.me // (1 << one)) % 2)
            if op == 5:
                piece = flipped(piece, 1)
        else:
            if op in (4, 5, 7):
                piece = flipped(piece, one)
            if op in (6, 7):
                piece = flipped(piece, two)
        at = dst.at[pl.ds(pl.multiple_of(base + piece * block + first, 8), rows), :]
        if op == 0:
            device = {"tensor": 1 - self.tensor}
        else:
            bit = {1: 0, 2: one, 3: two, 4: two, 5: 0, 6: 0, 7: 0}[op]
            device = {"dp": flipped(self.me, bit)}
        k = i * self.ops + op
        return pltpu.make_async_remote_copy(
            src_ref=src.at[pl.ds(first, rows), :] if op == 0 else at,
            dst_ref=at,
            send_sem=self.send_sem.at[k],
            recv_sem=self.recv_sem.at[k],
            device_id=device,
            device_id_type=MESH,
        )

    def start(self, i):
        self.copy(i, 0).start()

    def after(self, i, op):
        self.copy(i, op).wait_recv()
        for other in self.forwards[op]:
            if not self.items[i][7] or other in (1, 2, 5):
                self.copy(i, other).start()

    def collect(self, i):
        for op in (1, 5) if self.items[i][7] else (1, 5, 6, 7):
            self.copy(i, op).wait_recv()

    def finish_send(self, i):
        for op in (0, 1, 2, 5) if self.items[i][7] else range(self.ops):
            self.copy(i, op).wait_send()


def greet_gather(me, tensor):
    barrier = pltpu.get_barrier_semaphore()
    pl.semaphore_signal(barrier, inc=1, device_id={"tensor": 1 - tensor}, device_id_type=MESH)
    for bit in range(3):
        pl.semaphore_signal(barrier, inc=1, device_id={"dp": flipped(me, bit)}, device_id_type=MESH)
    pl.semaphore_wait(barrier, 4)


class Reduce:
    def __init__(self, dp, me, swap, source, home, more, send_sem, recv_sem):
        self.dp, self.me, self.source, self.home, self.more = dp, me, source, home, more
        self.send_sem, self.recv_sem = send_sem, recv_sem
        self.hops = dp.bit_length() - 1
        self.order = list(range(self.hops))
        if swap:
            self.order[1], self.order[2] = 2, 1

    def block(self, j, m, keep):
        total = 0
        for i, bit in enumerate(self.order):
            mine = (self.me // (1 << bit)) % 2
            if i < j or (i == j and keep):
                total = total + mine * (1 << bit)
            elif i == j:
                total = total + (1 - mine) * (1 << bit)
            else:
                total = total + ((mine + m // (1 << (i - j - 1))) % 2) * (1 << bit)
        return total

    def count(self, j):
        return self.dp >> (j + 1)

    def base(self, j):
        return self.dp // 2 - (self.dp >> j)

    def copy(self, j, m):
        b = self.block(j, m, False)
        if j == 0:
            src, dst, k = self.source.at[b], self.home.at[b // 2], m
        else:
            at = self.base(j) + m
            src, dst, k = self.home.at[b // 2], self.more.at[at], self.dp // 2 + at
        return pltpu.make_async_remote_copy(
            src_ref=src,
            dst_ref=dst,
            send_sem=self.send_sem.at[k],
            recv_sem=self.recv_sem.at[k],
            device_id={"dp": flipped(self.me, self.order[j])},
            device_id_type=MESH,
        )

    def start(self, j, m):
        self.copy(j, m).start()

    def add(self, j, m, kept=None):
        self.copy(j, m).wait_recv()
        at = self.block(j, m, True) // 2
        if j > 0:
            ref, i = self.more, self.base(j) + m
        else:
            ref, i = (self.source, self.block(0, m, True)) if kept is None else (kept, m)
        self.home[at] = self.home[at] + ref[i]

    def finish_send(self, j, m):
        self.copy(j, m).wait_send()

    def every(self, j, do):
        n = self.count(j)
        if n > 8:

            @pl.loop(0, n)
            def _(m):
                do(m)
        else:
            for m in range(n):
                do(m)


def reduce_scratch(dp, rows, cols):
    return [
        pltpu.VMEM((dp // 2, rows, cols), F32),
        pltpu.VMEM((dp // 2 - 1, rows, cols), F32),
        pltpu.SemaphoreType.DMA((dp - 1,)),
        pltpu.SemaphoreType.DMA((dp - 1,)),
    ]


def store_blocks(out, value, at=slice(None)):
    rows = out.shape[1]
    n = value.shape[0] // rows
    if rows % 8 == 0:
        out[:, :, at] = value.reshape(n, rows, value.shape[1])
    else:
        for b in range(n):
            out[b, :, at] = value[b * rows : (b + 1) * rows, :]


def rope(x, cos, sin):
    lane = lax.broadcasted_iota(jnp.int32, x.shape, 1)
    other = jnp.where(lane % HD < HD // 2, pltpu.roll(x, 128 - HD // 2, 1), pltpu.roll(x, HD // 2, 1))
    return x * cos + other * sin


def project(y, width, cos, sin, q_ref, k_ref, v_ref):
    for c in range(0, width, 128):
        q_ref[:, c : c + 128] = rope(y[:, c : c + 128], cos, sin).astype(BF)
        k_ref[:, c : c + 128] = rope(y[:, width + c : width + c + 128], cos, sin).astype(BF)
    v_ref[...] = y[:, 2 * width :].astype(BF)


def attend_pair(q_ref, k_ref, v_ref, at, o_ref, lse_ref, pair, oT, sbuf):
    length = q_ref.shape[0]
    wide = sbuf.shape[2]
    kk = k_ref[:, at]
    qT, vT = q_ref[:, at].T, v_ref[:, at].T
    row = lax.broadcasted_iota(jnp.int32, (128, wide), 0)
    items = [(h, c) for h in range(2) for c in range(0, length, wide)]

    def scores(i):
        h, c = items[i]
        qq = qT[:, c : c + wide]
        s = dot(kk, jnp.where((row < HD) == (h == 0), qq, jnp.zeros_like(qq)))
        sbuf[i % 2] = s
        return jnp.max(s, axis=0, keepdims=True)

    top = scores(0)
    for i, (h, c) in enumerate(items):
        following = scores(i + 1) if i + 1 < len(items) else None
        p = jnp.exp2((sbuf[i % 2] - top) * C2)
        total = jnp.sum(p, axis=0, keepdims=True)
        oT[h * HD : (h + 1) * HD, c : c + wide] = dot(vT[h * HD : (h + 1) * HD, :], p.astype(BF)) * (1.0 / total)
        lse_ref[pl.ds(pair, 1), h : h + 1, c : c + wide] = (top * C2 + jnp.log2(total))[None]
        top = following
    o_ref[:, at] = oT[...].T.astype(BF)


def gelu_parts(x):
    c0, c1 = 0.7978845608028654, 0.044715
    x2 = x * x
    t = jnp.tanh(x * (c0 + (c0 * c1) * x2))
    a = 0.5 + 0.5 * t
    d = a + (x * (0.5 - 0.5 * (t * t))) * (c0 + (3.0 * c0 * c1) * x2)
    return x * a, d


def forward_kernel(
    nb, bucket, tok, mask, mvec, gain1, gain2, te, wada, bada, wq, cos, sin, bup,
    bup_h, wqf_h, wo_h, wup_h, wdown_h, cot_h,
    h1_ref, q_ref, k_ref, v_ref, mods_ref, cond_ref, o_ref, lse_ref, wxq_ref, wxo_ref,
    attn_ref, h2_ref, feed_ref, gh_ref, gbup_ref, fu, fd, bupx, ku, kd, ru, rd,
    oT, sbuf, fq, fo, wo, wup, wdown, cot, act_s, gp_s, gf_s, lq, lo, lu, ld, pq, po, pu, pd,
    du_s, dd_s, load_sem, send_sem, recv_sem, bup_sem, keep_sem, give_sem, take_sem,
):
    step = pl.program_id(0)
    me, tensor = lax.axis_index("dp"), lax.axis_index("tensor")
    cols = q_ref.shape[2]
    pairs = cols // 128
    width = tok.shape[1]
    items = []
    for p in range(pairs):
        n = pq.shape[1]
        items += [(pq.at[p], fq.at[p], 0, n, i * (n // 2), n // 2, i == 0, False) for i in range(2)]
    for src, dst in ((po, fo), (pu, fu)):
        n = src.shape[0]
        items += [(src, dst, 0, n, i * (n // 2), n // 2, i == 0, False) for i in range(2)]
    n = pd.shape[1]
    for s in range(2):
        items += [(pd.at[i], fd, i * 4 * n, n, s * (n // 2), n // 2, i == 0, True) for i in range(2)]
    gather = Gather(me, tensor, items, send_sem, recv_sem)
    pieces = []
    for i, (src, dst) in enumerate(((wqf_h, lq), (wo_h, lo), (wup_h, lu))):
        n = dst.shape[0]
        at = pl.ds(pl.multiple_of((me % 8) * n, 16), n)
        pieces.append(pltpu.make_async_copy(src.at[at, :], dst, load_sem.at[i]))
    for i in range(2):
        n = ld.shape[1]
        quarter = me % 2 + 2 * ((me // (2 << i)) % 2)
        at = pl.ds(pl.multiple_of((4 * i + quarter) * n, 16), n)
        pieces.append(pltpu.make_async_copy(wdown_h.at[at, :], ld.at[i], load_sem.at[3 + i]))
    loads = [
        pltpu.make_async_copy(src, dst, load_sem.at[5 + i])
        for i, (src, dst) in enumerate(((wo_h, wo), (wup_h, wup), (wdown_h, wdown), (cot_h, cot)))
    ]
    bias = pltpu.make_async_remote_copy(
        src_ref=bup_h, dst_ref=bupx, send_sem=bup_sem.at[0], recv_sem=bup_sem.at[1],
        device_id={"tensor": 1 - tensor}, device_id_type=MESH,
    )
    core = me % 2
    dp = du_s.shape[0]

    def parts(k, i):
        src, keep, take = ((du_s, ku, ru), (dd_s, kd, rd))[k]
        stay = pltpu.make_async_copy(src.at[2 * i + core], keep.at[i], keep_sem.at[k, i])
        give = pltpu.make_async_remote_copy(
            src_ref=src.at[2 * i + 1 - core], dst_ref=take.at[i], send_sem=give_sem.at[k, i],
            recv_sem=take_sem.at[k, i], device_id={"dp": flipped(me, 0)}, device_id_type=MESH,
        )
        return stay, give

    def split(first, last, do):
        @pl.loop(first, last)
        def _(i):
            for k in range(2):
                for c in parts(k, i):
                    do(c)

    s_own, s_other = nb, nb + pairs
    s_mlp = s_other + pairs
    s_dw = s_mlp + nb

    @pl.when(step == 0)
    def _():
        for c in pieces:
            c.start()
        barrier = pltpu.get_barrier_semaphore()
        pl.semaphore_signal(barrier, inc=1, device_id={"tensor": 1 - tensor}, device_id_type=MESH)
        for bit in range(3):
            pl.semaphore_signal(barrier, inc=1, device_id={"dp": flipped(me, bit)}, device_id_type=MESH)
        for c in pieces:
            c.wait()
        for p in range(pairs):
            pq[p] = lq[:, p * 128 : (p + 1) * 128].astype(F32)
        for src, dst in ((lo, po), (lu, pu), (ld, pd)):
            dst[...] = src[...].astype(F32)
        pl.semaphore_wait(barrier, 4)
        for i in range(len(items)):
            gather.start(i)
        bias.start()
        for c in loads:
            c.start()

    for at, todo in FORWARD_PLAN.items():

        @pl.when(step == at)
        def _():
            for i, op in todo:
                gather.after(i, op)

    @pl.when(step == s_dw + 1)
    def _():
        split(0, dp // 4, lambda c: c.start())

    @pl.when(step == 0)
    def _():
        row = te[...]
        sub = lax.broadcasted_iota(jnp.int32, row.shape, 0)
        row = jnp.sum(jnp.where(sub == bucket[...], row, 0.0), axis=0, keepdims=True)
        row = row * (1.0 / (1.0 + jnp.exp(-row)))
        cond_ref[...] = row
        col = jnp.broadcast_to(row, (8, row.shape[1])).T[:, 0:1]
        bias_row = line(bada)
        for i in range(6):
            cs = slice(i * width, (i + 1) * width)
            mods_ref[i : i + 1, :] = jnp.sum(wada[:, cs].astype(F32) * col, axis=0, keepdims=True) + bias_row[:, cs]

    def block(first):
        return pl.ds(pl.multiple_of((step - first) * RB, RB), RB)

    @pl.when(step < s_own)
    def _():
        rows = block(0)
        x = tok[rows, :].astype(F32) + mask_column(mask, step, RB) * line(mvec)
        n, _ = normed(x)
        h = (n * (line(gain1) * (1.0 + mods_ref[1:2, :])) + mods_ref[0:1, :]).astype(BF)
        h1_ref[rows, :] = h
        y = jnp.concatenate([dot(h, wq[i]) for i in range(3)], axis=1)
        project(y, cols, cos[rows, :], sin[rows, :], q_ref.at[0, rows, :], k_ref.at[0, rows, :], v_ref.at[0, rows, :])

    def attend(half, pair):
        at = pl.ds(pl.multiple_of(pair * 128, 128), 128)
        attend_pair(
            q_ref.at[half], k_ref.at[half], v_ref.at[half], at, o_ref.at[half], lse_ref, half * pairs + pair, oT, sbuf
        )

    for p in range(pairs):

        @pl.when(step == s_other + p)
        def _():
            for i in (2 * p, 2 * p + 1):
                gather.collect(i)

    @pl.when((step >= s_other) & (step < s_mlp))
    def _():
        p = step - s_other
        at = pl.ds(pl.multiple_of(p * 128, 128), 128)
        for i in range(3):
            wxq_ref[i, :, at] = fq[p, i * width : (i + 1) * width, :].astype(BF)
        w = jnp.concatenate([wxq_ref[i, :, at] for i in range(3)], axis=1)
        for r in range(0, tok.shape[0], RB):
            rows = slice(r, r + RB)
            project(
                dot(h1_ref[rows, :], w), 128, cos[rows, :], sin[rows, :],
                q_ref.at[1, rows, at], k_ref.at[1, rows, at], v_ref.at[1, rows, at],
            )

    @pl.when((step >= s_own) & (step < s_mlp))
    def _():
        half = (step - s_own) // pairs
        attend(half, step - s_own - half * pairs)

    @pl.when(step == s_mlp)
    def _():
        for i in (2 * pairs, 2 * pairs + 1):
            gather.collect(i)
        wxo_ref[...] = fo[...].astype(BF)
        for c in loads:
            c.wait()
        gbup_ref[...] = jnp.zeros_like(gbup_ref)

    @pl.when((step >= s_mlp) & (step < s_dw))
    def _():
        rows = block(s_mlp)
        x = tok[rows, :].astype(F32) + mask_column(mask, step - s_mlp, RB) * line(mvec)
        attn = dot(o_ref[0, rows, :], wo[...]) + dot(o_ref[1, rows, :], wxo_ref[...])
        attn_ref[...] = attn
        n, _ = normed(x + mods_ref[2:3, :] * attn)
        h = (n * (line(gain2) * (1.0 + mods_ref[4:5, :])) + mods_ref[3:4, :]).astype(BF)
        h2_ref[rows, :] = h
        act, slope = gelu_parts(dot(h, wup[...]) + line(bup))
        act = act.astype(BF)
        act_s[rows, :] = act
        feed_ref[...] = dot(act, wdown[...])
        gf = (mods_ref[5:6, :] * cot[rows, :].astype(F32)).astype(BF)
        gf_s[rows, :] = gf
        gp = (dot(gf, wdown[...], 1, 1) * slope).astype(BF)
        gp_s[rows, :] = gp
        gh_ref[...] = dot(gp, wup[...], 1, 1)
        gbup_ref[...] += jnp.sum(gp.astype(F32), axis=0, keepdims=True)

    @pl.when(step >= s_dw)
    def _():
        part = width // 2
        cs = pl.ds(pl.multiple_of((step - s_dw) * part, 128), part)
        blocks = pl.ds((step - s_dw) * (dp // 2), dp // 2)
        store_blocks(du_s.at[blocks], dot(h2_ref[:, cs], gp_s[...], 0, 0))
        store_blocks(dd_s.at[blocks], dot(gf_s[:, cs], act_s[...], 0, 0))

    @pl.when(step == pl.num_programs(0) - 1)
    def _():
        for i, op in FORWARD_END[:2]:
            gather.after(i, op)
        split(dp // 4, dp // 2, lambda c: c.start())
        for i, op in FORWARD_END[2:]:
            gather.after(i, op)
        for i in range(2 * pairs + 2, len(items)):
            gather.collect(i)
        for i in range(len(items)):
            gather.finish_send(i)
        bias.wait()
        split(0, dp // 2, lambda c: c.wait())


def forward(dp, bucket, tokens, mask2, mvec, gain1, gain2, te, wada, bada, wq, cos, sin, bup, wo, wup, wdown, cot):
    rows, width = tokens.shape
    cols, ff = wq.shape[2], wup.shape[1]
    nb, pairs = rows // RB, cols // 128
    s_mlp = nb + 2 * pairs
    mblk = pl.BlockSpec((RB, width), lambda i: (jnp.clip(i - s_mlp, 0, nb - 1), 0))
    grad = (dp, width // dp, ff)
    half = sds((dp // 2, *grad[1:]), F32)
    act = (2, rows, cols)
    wqf = wq.reshape(3 * width, cols)
    vm = pltpu.VMEM
    piece = lambda w: (w.shape[0] // 8, w.shape[1])
    n_items = 2 * pairs + 8
    return pl.pallas_call(
        functools.partial(forward_kernel, nb),
        grid=(s_mlp + nb + 2,),
        in_specs=[
            one(x.shape) for x in (bucket, tokens, mask2, mvec, gain1, gain2, te, wada, bada, wq, cos, sin, bup)
        ] + [ANYS] * 6,
        out_specs=[
            one((rows, width)), one(act), one(act), one(act), one((8, width)), one((1, te.shape[1])),
            one(act), one((2 * pairs, 2, rows)), one(wq.shape), one((cols, width)),
            mblk, one((rows, width)), mblk, mblk, one((1, ff)), *[ANYS] * 7,
        ],
        out_shape=[
            sds((rows, width), BF), sds(act, BF), sds(act, BF), sds(act, BF), sds((8, width), F32),
            sds((1, te.shape[1]), F32), sds(act, BF), sds((2 * pairs, 2, rows), F32), sds(wq.shape, BF),
            sds((cols, width), BF), sds((rows, width), F32), sds((rows, width), BF), sds((rows, width), F32),
            sds((rows, width), F32), sds((1, ff), F32), sds(wup.shape, F32), sds(wdown.shape, F32),
            sds(bup.shape, F32), half, half, half, half,
        ],
        scratch_shapes=[
            vm((128, rows), F32), vm((2, rows, 512), F32), vm((pairs, 3 * width, 128), F32), vm(wo.shape, F32),
            vm(wo.shape, BF), vm(wup.shape, BF), vm(wdown.shape, BF), vm(cot.shape, BF),
            vm((rows, ff), BF), vm((rows, ff), BF), vm((rows, width), BF),
            *[vm(piece(w), BF) for w in (wqf, wo, wup)], vm((2, *piece(wdown)), BF),
            vm((pairs, piece(wqf)[0], 128), F32), *[vm(piece(w), F32) for w in (wo, wup)],
            vm((2, *piece(wdown)), F32), vm(grad, F32), vm(grad, F32), pltpu.SemaphoreType.DMA((9,)), pltpu.SemaphoreType.DMA((8 * n_items,)),
            pltpu.SemaphoreType.DMA((8 * n_items,)), pltpu.SemaphoreType.DMA((2,)),
            *[pltpu.SemaphoreType.DMA((2, dp // 2))] * 3,
        ],
        compiler_params=params(collective_id=2, has_side_effects=True),
        name="forward",
    )(bucket, tokens, mask2, mvec, gain1, gain2, te, wada, bada, wq, cos, sin, bup, bup, wqf, wo, wup, wdown, cot)


def hidden(h, gf, wup, bup, wdown):
    wide = wup.shape[1] // 3
    feed = gh = None
    dots = lambda c: (dot(h, wup[:, c : c + wide]) + bup[:, c : c + wide], dot(gf, wdown[c : c + wide, :], 1, 1))
    ready = dots(0)
    for c in range(0, 3 * wide, wide):
        following = dots(c + wide) if c + wide < 3 * wide else None
        act, slope = gelu_parts(ready[0])
        gp = (ready[1] * slope).astype(BF)
        f = dot(act.astype(BF), wdown[c : c + wide, :])
        d = dot(gp, wup[:, c : c + wide], 1, 1)
        feed, gh = (f, d) if feed is None else (feed + f, gh + d)
        ready = following
    return feed, gh


def mlp_other_kernel(
    dp, tok, mask, mvec, mods, gain, attn_ref, h_ref, feed_ref, gh_ref, cot, bup, bdown,
    mo, wo, wx, gbup, cond, ku, kd, ru, rd, fu, fd,
    res_ref, gmid_ref, gm_ref, small, dw_ref, hu_out, hd_out,
    acc, keep_u, keep_d, load_sem, stage_u, stage_d, wup, wdown, w_sem,
    hu, more_u, send_u, recv_u, hd, more_d, send_d, recv_d,
):
    step, last = pl.program_id(0), pl.num_programs(0) - 1
    me, tensor = lax.axis_index("dp"), lax.axis_index("tensor")
    weights = {
        "u": Reduce(dp, me, False, None, hu, more_u, send_u, recv_u),
        "d": Reduce(dp, me, True, None, hd, more_d, send_d, recv_d),
    }

    def act(kind, w, j, m):
        if kind == "S":
            weights[w].start(j, m)
        else:
            weights[w].add(j, m)

    def point(at):
        if dp == 16 and at in MLP_PLAN:

            @pl.when(step == at[0])
            def _():
                for a in MLP_PLAN[at]:
                    act(*a)

    halves = [
        pltpu.make_async_copy(src, dst, load_sem.at[i])
        for i, (src, dst) in enumerate(((ru, hu), (ku, keep_u), (rd, hd), (kd, keep_d)))
    ]
    wloads = [
        pltpu.make_async_copy(src, dst, w_sem.at[i]) for i, (src, dst) in enumerate(((fu, stage_u), (fd, stage_d)))
    ]

    @pl.when(step == 0)
    def _():
        for c in halves + wloads:
            c.start()
        barrier = pltpu.get_barrier_semaphore()
        for j in range(1, 3):
            pl.semaphore_signal(barrier, inc=1, device_id={"dp": flipped(me, j)}, device_id_type=MESH)
        small[...] = jnp.zeros_like(small)
        pl.semaphore_wait(barrier, 2)
        for i, (home, keep) in enumerate(((hu, keep_u), (hd, keep_d))):
            halves[2 * i].wait()
            halves[2 * i + 1].wait()

            @pl.loop(0, dp // 2)
            def _(b):
                home[b] = home[b] + keep[b]

            if dp == 16:
                for a in MLP_PLAN[0, 0]:
                    if a[1] == "ud"[i]:
                        act(*a)
        for c, src, dst in zip(wloads, (stage_u, stage_d), (wup, wdown)):
            c.wait()
            dst[...] = src[...].astype(BF)

    for i in range(1, 4):
        point((i, 0))

    x = tok[...].astype(F32) + mask_column(mask, step, tok.shape[0]) * line(mvec)
    attn = attn_ref[...]
    middle = x + mods[2:3, :] * attn
    n2, rs = normed(middle)
    g = cot[...].astype(F32)
    gf = (mods[5:6, :] * g).astype(BF)
    feed, gh = hidden(h_ref[...], gf, wup, line(bup), wdown)
    feed = (feed_ref[...] + feed) + line(bdown)
    gh = gh_ref[...] + gh

    for i in range(4):
        point((i, 1))
    res_ref[...] = (middle + mods[5:6, :] * feed).astype(BF)
    opened = 1.0 + mods[4:5, :]
    e = gh * (opened * line(gain))
    inner = jnp.mean(e * n2, axis=-1, keepdims=True)
    gmid = g + (e - jnp.mean(e, axis=-1, keepdims=True) - n2 * inner) * rs
    gmid_ref[...] = gmid
    ga = (mods[2:3, :] * gmid).astype(BF)
    gm_ref[0] = dot(ga, wo[...], 1, 1).astype(BF)
    gm_ref[1] = dot(ga, wx[...], 1, 1).astype(BF)
    col = lambda v: jnp.sum(v, axis=0, keepdims=True)
    small[0:1, :] += col(g * feed)
    small[1:2, :] += col(gf.astype(F32))
    small[2:3, :] += col(gh)
    small[3:4, :] += col(gh * n2)
    small[4:5, :] += col(gmid * attn)
    dw = dot(ga, mo[...], 0, 0)

    @pl.when(step == 0)
    def _():
        acc[...] = dw

    @pl.when(step > 0)
    def _():
        acc[...] += dw

    @pl.when(step == last)
    def _():
        width = mods.shape[1]
        small[5:6, :] = small[3:4, :] * opened
        small[3:4, :] = small[3:4, :] * line(gain)
        for i in range(gbup.shape[1] // width):
            small[8 + i : 9 + i, :] = gbup[:, i * width : (i + 1) * width]
        small[6:7, 0 : cond.shape[1]] = cond[...]
        store_blocks(dw_ref, acc[...])
        if dp == 16:
            for a in MLP_END:
                act(*a)
            for todo in (*MLP_PLAN.values(), MLP_END):
                for kind, w, j, m in todo:
                    if kind == "S":
                        weights[w].finish_send(j, m)
        stores = [
            pltpu.make_async_copy(src, dst, w_sem.at[k]) for k, (src, dst) in enumerate(((hu, hu_out), (hd, hd_out)))
        ]
        for c in stores:
            c.start()
        for c in stores:
            c.wait()


def mlp_other(dp, tokens, mask2, mvec, mods, gain, attn, h, feed, gh, cot, bup, bdown, os, wo, wx, gbup, cond, ku, kd, ru, rd, fu, fd):
    rows, width = tokens.shape
    ff, cols = fu.shape[1], wo.shape[0]
    part = width // dp
    blk = lambda c: pl.BlockSpec((RB, c), lambda i: (i, 0))
    half = (dp // 2, part, ff)
    vm = pltpu.VMEM
    return pl.pallas_call(
        functools.partial(mlp_other_kernel, dp),
        grid=(rows // RB,),
        in_specs=[
            blk(width), one(mask2.shape), one(mvec.shape), one(mods.shape), one(gain.shape),
            blk(width), blk(width), blk(width), blk(width), blk(width), one(bup.shape), one(bdown.shape),
            pl.BlockSpec((None, RB, cols), lambda i: (0, i, 0)), one(wo.shape), one(wx.shape), one(gbup.shape),
            one(cond.shape), *[ANYS] * 6,
        ],
        out_specs=[
            blk(width), blk(width), pl.BlockSpec((2, RB, cols), lambda i: (0, i, 0)), one((16, width)),
            one((dp, part, cols)), ANYS, ANYS,
        ],
        out_shape=[
            sds((rows, width), BF), sds((rows, width), F32), sds((2, rows, cols), BF), sds((16, width), F32),
            sds((dp, part, cols), F32), sds(half, F32), sds(half, F32),
        ],
        scratch_shapes=[
            vm((width, cols), F32), vm(half, F32), vm(half, F32), pltpu.SemaphoreType.DMA((4,)),
            vm(fu.shape, F32), vm(fd.shape, F32), vm(fu.shape, BF), vm(fd.shape, BF), pltpu.SemaphoreType.DMA((2,)),
            *reduce_scratch(dp, part, ff), *reduce_scratch(dp, part, ff),
        ],
        compiler_params=params(collective_id=3, has_side_effects=True),
        name="mlp_other",
    )(tokens, mask2, mvec, mods, gain, attn, h, feed, gh, cot, bup, bdown, os, wo, wx, gbup, cond, ku, kd, ru, rd, fu, fd)


def attend_back_pair(q_ref, k_ref, v_ref, o_ref, do_ref, lse_ref, cosT, sinT, g_ref, at, gT, between):
    length = q_ref.shape[0]
    kk, vv = k_ref[...], v_ref[...]
    kT, qT, doT = kk.T, q_ref[...].T, do_ref[...].T
    oT = o_ref[...].T
    prod = doT.astype(F32) * oT.astype(F32)
    row = lax.broadcasted_iota(jnp.int32, (128, length), 0)
    half = HD // 2
    for h in range(2):
        hs = slice(h * HD, (h + 1) * HD)
        sel = (row < HD) == (h == 0)
        qm = jnp.where(sel, qT, jnp.zeros_like(qT))
        dm = jnp.where(sel, doT, jnp.zeros_like(doT))
        inner = jnp.sum(prod[hs, :], axis=0, keepdims=True)
        p = jnp.exp2(dot(kk, qm) * C2 - lse_ref[h : h + 1, :])
        ds = (p * (dot(vv, dm) - inner)).astype(BF)
        dv = dot(doT[hs, :], p.astype(BF), 1, 1)
        dk = dot(qT[hs, :], ds, 1, 1) * 0.125
        dq = dot(kT[hs, :], ds) * 0.125
        c, s = cosT[...], sinT[...]
        for i, d in ((0, dq), (1, dk)):
            a, b = d[:half, :], d[half:, :]
            gT[i, h * HD : h * HD + half, :] = a * c + b * s
            gT[i, h * HD + half : (h + 1) * HD, :] = b * c - a * s
        gT[2, hs, :] = dv
        if h == 0:
            between()
    for i in range(3):
        g_ref[i, :, at] = gT[i].T.astype(BF)


def backward_kernel(
    dp, nb, pairs, q_ref, k_ref, v_ref, o_ref, do_ref, lse_ref, cosT, sinT, h1_h, w_h, wx_h, tok, mask, mvec,
    mods, gain, gmid_ref, small, dw_hbm, hu_in, hd_in,
    gt_ref, up_ref, down_ref, out_ref, qkv_ref, got_ref,
    gT, g, h1, w, wx, dw_out, dqs, late_s, pack, got, own_sem, gsend, grecv, load_sem, *scratch,
):
    step, last = pl.program_id(0), pl.num_programs(0) - 1
    me, tensor = lax.axis_index("dp"), lax.axis_index("tensor")
    names = ["u", "d", "o"] + [f"q{p}" for p in range(pairs)]
    sources = [None, None, dw_out] + [dqs.at[p] for p in range(pairs)]
    weights = {
        n: Reduce(dp, me, n == "d", src, *scratch[4 * i : 4 * i + 4]) for i, (n, src) in enumerate(zip(names, sources))
    }
    hops = weights["u"].hops
    width, cols = mods.shape[1], w.shape[2]
    loads = [
        pltpu.make_async_copy(src, dst, load_sem.at[i])
        for i, (src, dst) in enumerate(((dw_hbm, dw_out), (hu_in, weights["u"].home), (hd_in, weights["d"].home)))
    ]
    later = [
        pltpu.make_async_copy(src, dst, load_sem.at[3 + i]) for i, (src, dst) in enumerate(((h1_h, h1), (w_h, w), (wx_h, wx)))
    ]
    s_x, s_end = pairs, 2 * pairs
    n = width // dp

    def act(kind, n, j, m):
        if kind == "S":
            weights[n].start(j, m)
        else:
            weights[n].add(j, m)

    def point(at):
        if dp == 16 and at in BACK_PLAN:

            @pl.when(step == at[0])
            def _():
                for a in BACK_PLAN[at]:
                    act(*a)

    def pack_rows(summed, gmod, cond):
        for d in range(dp):
            for i in range(4):
                if summed[i] is not None:
                    pack[d, :, i * n : (i + 1) * n] = summed[i][:, d * n : (d + 1) * n]
            row, off = 4 + 2 * n * d // width, 2 * n * d % width
            if summed[row] is not None:
                pack[d, :, 4 * n : 6 * n] = summed[row][:, off : off + 2 * n]
            done, need = 0, 6 * n
            while done < need:
                row, off = (need * d + done) // width, (need * d + done) % width
                take = min(need - done, width - off)
                if gmod[row] is not None:
                    pack[d, :, PACK_MOD + done : PACK_MOD + done + take] = gmod[row][:, off : off + take]
                done += take
            if cond is not None:
                pack[d, :, PACK_COND : PACK_COND + 128] = cond

    def spread(r):
        to = (me + r) % dp
        return pltpu.make_async_remote_copy(
            src_ref=pack.at[to], dst_ref=got.at[me], send_sem=gsend.at[r], recv_sem=grecv.at[r],
            device_id=(to, tensor), device_id_type=MESH,
        )

    @pl.when(step == 0)
    def _():
        for c in loads:
            c.start()
        barrier = pltpu.get_barrier_semaphore()

        @pl.loop(1, dp)
        def _(r):
            pl.semaphore_signal(barrier, inc=1, device_id=((me + r) % dp, tensor), device_id_type=MESH)

        pl.semaphore_wait(barrier, dp - 1)
        for c in loads:
            c.wait()
        for c in later:
            c.start()
        late_s[...] = jnp.zeros_like(late_s)
        pack[...] = jnp.zeros_like(pack)
        summed = [None, None, small[5:6, :], small[1:2, :], small[8:9, :], small[9:10, :]]
        gmod = [None, None, small[4:5, :], small[2:3, :], small[3:4, :], small[0:1, :]]
        pack_rows(summed, gmod, small[6:7, 0:128])

    for i in range(2 * pairs + nb):
        point((i, 0))

    def between():
        for p in range(2 * pairs):
            point((p, 1))

    @pl.when(step < s_end)
    def _():
        half = step // pairs
        at = pl.ds(pl.multiple_of((step - half * pairs) * 128, 128), 128)
        attend_back_pair(q_ref, k_ref, v_ref, o_ref, do_ref, lse_ref, cosT, sinT, g.at[half], at, gT, between)

    @pl.when(step == 0)
    def _():
        for c in later:
            c.wait()

    @pl.when(step < s_x)
    def _():
        at = pl.ds(pl.multiple_of(step * 128, 128), 128)
        gp = jnp.concatenate([g[0, i, :, at] for i in range(3)], axis=1)
        store_blocks(dqs.at[step], dot(h1[...], gp, 0, 0))

    @pl.when(step >= s_end)
    def _():
        i = step - s_end
        rows = pl.ds(pl.multiple_of(i * RB, RB), RB)
        m = mask_column(mask, i, RB)
        n1, rs = normed(tok[...].astype(F32) + m * line(mvec))
        parts = [
            dot(d[0, rows, :], ww[0], 1, 1) + dot(d[1, rows, :], ww[1], 1, 1) + dot(d[2, rows, :], ww[2], 1, 1)
            for d, ww in ((g.at[0], w), (g.at[1], wx))
        ]
        gh = parts[0] + parts[1]
        e = gh * ((1.0 + mods[1:2, :]) * line(gain))
        inner = jnp.mean(e * n1, axis=-1, keepdims=True)
        gs = gmid_ref[...] + (e - jnp.mean(e, axis=-1, keepdims=True) - n1 * inner) * rs
        gt_ref[...] = gs.astype(BF)
        col = lambda v: jnp.sum(v, axis=0, keepdims=True)
        late_s[0:1, :] += col(gh)
        late_s[1:2, :] += col(gh * n1)
        late_s[3:4, :] += col(m * gs)

    @pl.when(step == last)
    def _():
        late_s[2:3, :] = late_s[1:2, :] * (1.0 + mods[1:2, :])
        late_s[1:2, :] = late_s[1:2, :] * line(gain)
        none = [None] * 4
        pack_rows([late_s[3:4, :], late_s[2:3, :]] + none, [late_s[0:1, :], late_s[1:2, :]] + none, None)
        if dp == 16:
            for a in BACK_END[:2]:
                act(*a)
        own = pltpu.make_async_copy(pack.at[me], got.at[me], own_sem)
        own.start()

        @pl.loop(1, dp)
        def _(r):
            spread(r).start()

        if dp == 16:
            for a in BACK_END[2:]:
                act(*a)
            todo = [a for v in BACK_PLAN.values() for a in v] + BACK_END
            for kind, n, j, m in todo:
                if kind == "S":
                    weights[n].finish_send(j, m)
        else:
            for n, r in weights.items():
                for j in range(1 if n in "ud" else 0, hops):
                    r.every(j, lambda m: r.start(j, m))
                    r.every(j, lambda m: r.add(j, m))
                    r.every(j, lambda m: r.finish_send(j, m))
        up_ref[...] = weights["u"].home[me // 2]
        down_ref[...] = weights["d"].home[me // 2]
        out_ref[...] = weights["o"].home[me // 2]
        for p in range(pairs):
            qkv_ref[p] = weights[f"q{p}"].home[me // 2]
        own.wait()

        @pl.loop(1, dp)
        def _(r):
            spread(r).wait()

        got_ref[...] = got[...]


PACK_MOD, PACK_COND, PACK = 384, 768, 896


def backward(dp, qs, ks, vs, os, gm, lses, cosT, sinT, h1, w, wx, tokens, mask2, mvec, mods, gain, gmid, small, dw_out, hu, hd):
    rows, width = tokens.shape
    cols = w.shape[2]
    nb, pairs = rows // RB, cols // 128
    part, ff = hu.shape[1], hu.shape[2]
    s_end = 2 * pairs
    pick = lambda i: jnp.minimum(i, 2 * pairs - 1)
    pair = pl.BlockSpec((None, rows, 128), lambda i: (pick(i) // pairs, 0, pick(i) % pairs))
    blk = pl.BlockSpec((RB, width), lambda i: (jnp.maximum(i - s_end, 0), 0))
    vm = pltpu.VMEM
    return pl.pallas_call(
        functools.partial(backward_kernel, dp, nb, pairs),
        grid=(s_end + nb,),
        in_specs=[pair] * 5 + [
            pl.BlockSpec((None, 2, rows), lambda i: (pick(i), 0, 0)), one(cosT.shape), one(sinT.shape),
            ANYS, ANYS, ANYS, blk, one(mask2.shape), one(mvec.shape), one(mods.shape),
            one(gain.shape), blk, one(small.shape), ANYS, ANYS, ANYS,
        ],
        out_specs=[
            blk, one((part, ff)), one((part, ff)), one((part, cols)), one((pairs, part, 384)), one((dp, 1, PACK)),
        ],
        out_shape=[
            sds((rows, width), BF), sds((part, ff), F32), sds((part, ff), F32), sds((part, cols), F32),
            sds((pairs, part, 384), F32), sds((dp, 1, PACK), F32),
        ],
        scratch_shapes=[
            vm((3, 128, rows), F32), vm((2, 3, rows, cols), BF), vm(h1.shape, BF), vm(w.shape, BF), vm(wx.shape, BF),
            vm((dp, part, cols), F32),
            vm((pairs, dp, part, 384), F32), vm((8, width), F32), vm((dp, 1, PACK), F32), vm((dp, 1, PACK), F32),
            pltpu.SemaphoreType.DMA, pltpu.SemaphoreType.DMA((dp,)), pltpu.SemaphoreType.DMA((dp,)),
            pltpu.SemaphoreType.DMA((6,)),
            *reduce_scratch(dp, part, ff), *reduce_scratch(dp, part, ff), *reduce_scratch(dp, part, cols),
            *[s for _ in range(pairs) for s in reduce_scratch(dp, part, 384)],
        ],
        compiler_params=params(collective_id=4, has_side_effects=True),
        name="backward",
    )(qs, ks, vs, os, gm, lses, cosT, sinT, h1, w, wx, tokens, mask2, mvec, mods, gain, gmid, small, dw_out, hu, hd)


def finish_kernel(res_in, gt_in, got, up, down, out, qkv, res, gt, mask, ln1, wqkv, wout, ln2, wup, bup, wdown, bdown, wada, bada):
    res[...] = res_in[...]
    gt[...] = gt_in[...]

    @pl.when(pl.program_id(0) == 1)
    def _():
        finish_rest(got, up, down, out, qkv, mask, ln1, wqkv, wout, ln2, wup, bup, wdown, bdown, wada, bada)


def finish_rest(got, up, down, out, qkv, mask, ln1, wqkv, wout, ln2, wup, bup, wdown, bdown, wada, bada):
    dp = got.shape[0]
    g = got[...].reshape(dp, got.shape[2])
    n = wup.shape[0]
    total = jnp.sum(g, axis=0, keepdims=True)
    for i, ref in enumerate((mask, ln1, ln2, bdown)):
        ref[...] = total[:, i * n : (i + 1) * n].reshape(n)
    bup[...] = total[:, 4 * n : 6 * n].reshape(2 * n)
    bada[...] = total[:, PACK_MOD : PACK_MOD + 6 * n].reshape(6 * n)
    wada[...] = lax.dot_general(
        g[:, PACK_MOD : PACK_MOD + 6 * n], g[:, PACK_COND : PACK_COND + wada.shape[1]], (((0,), (0,)), ((), ())),
        precision=lax.Precision.HIGHEST, preferred_element_type=F32,
    )
    wup[...] = up[...]
    wdown[...] = down[...]
    wout[...] = out[...]
    for p in range(qkv.shape[0]):
        for i in range(3):
            wqkv[i, :, p * 128 : (p + 1) * 128] = qkv[p, :, i * 128 : (i + 1) * 128]


def finish(result, grad_tokens, got, up, down, out, qkv, tdim):
    n, ff = up.shape
    cols = out.shape[1]
    shapes = [(n,), (n,), (3, n, cols), (n, cols), (n,), (n, ff), (2 * n,), (n, ff), (n,), (6 * n, tdim), (6 * n,)]
    ins = (got, up, down, out, qkv)
    blk = pl.BlockSpec((result.shape[0] // 2, result.shape[1]), lambda i: (i, 0))
    return pl.pallas_call(
        finish_kernel,
        grid=(2,),
        in_specs=[blk, blk] + [one(x.shape) for x in ins],
        out_specs=[blk, blk] + [one(s) for s in shapes],
        out_shape=[sds(result.shape, BF)] * 2 + [sds(s, F32) for s in shapes],
        compiler_params=params(),
        name="finish",
    )(result, grad_tokens, *ins)


def rope_tables(length):
    half = HD // 2
    freq = 10000.0 ** (-(np.arange(half, dtype=np.float64) / half))
    angle = np.arange(length, dtype=np.float64)[:, None] * freq[None, :]
    return np.cos(angle).astype(np.float32), np.sin(angle).astype(np.float32)


def body(
    dp, tokens, cotangent, bucket, mask, time_embed, mask_vec, ln1_gain, w_qkv, w_out, ln2_gain,
    w_up, b_up, w_down, b_down, w_ada, b_ada,
):
    rows, width = tokens.shape
    mask2 = mask.reshape(rows // 128, 128)
    c, s = rope_tables(rows)
    cos, sin = jnp.asarray(np.tile(c, (1, 4))), jnp.asarray(np.tile(np.concatenate([-s, s], 1), (1, 2)))
    cosT, sinT = jnp.asarray(np.ascontiguousarray(c.T)), jnp.asarray(np.ascontiguousarray(s.T))
    (h1, qs, ks, vs, mods, cond, os, lses, wx_qkv, wx_out, attn, h2, feed, gh2, gbup, fu, fd, bup_x, ku, kd, ru, rd) = forward(
        dp, bucket.reshape(1, 1), tokens, mask2, mask_vec, ln1_gain, ln2_gain, time_embed, w_ada, b_ada, w_qkv,
        cos, sin, b_up, w_out, w_up, w_down, cotangent,
    )
    result, gmid, gm, small, dw_out, hu, hd = mlp_other(
        dp, tokens, mask2, mask_vec, mods, ln2_gain, attn, h2, feed, gh2, cotangent, bup_x, b_down,
        os, w_out, wx_out, gbup, cond, ku, kd, ru, rd, fu, fd,
    )
    grad_tokens, sum_up, sum_down, sum_out, sum_qkv, got = backward(
        dp, qs, ks, vs, os, gm, lses, cosT, sinT, h1, w_qkv, wx_qkv, tokens, mask2, mask_vec, mods, ln1_gain, gmid,
        small, dw_out, hu, hd,
    )
    out = finish(result, grad_tokens, got, sum_up, sum_down, sum_out, sum_qkv, time_embed.shape[1])
    return tuple(x.T if i in (5, 9, 11) else x for i, x in enumerate(out))


def solution(mesh):
    in_specs = (
        P("dp", None), P("dp", None), P("dp"), P("dp"), P(), P(), P(), P(None, None, "tensor"),
        P("tensor", None), P(), P(None, "tensor"), P("tensor"), P("tensor", None), P(), P(), P(),
    )
    out_specs = (
        P("dp", None), P("dp", None), P("dp"), P("dp"), P(None, "dp", "tensor"), P("tensor", "dp"),
        P("dp"), P("dp", "tensor"), P(("tensor", "dp")), P("tensor", "dp"), P("dp"), P(None, "dp"), P("dp"),
    )
    step = functools.partial(body, mesh.shape["dp"])
    return jax.shard_map(step, mesh=mesh, in_specs=in_specs, out_specs=out_specs, check_vma=False)
```

```python
import functools

import jax
import jax.numpy as jnp
import numpy as np
from jax import lax
from jax.experimental import pallas as pl
from jax.experimental.pallas import tpu as pltpu
from jax.sharding import PartitionSpec as P

HD = 64
EPS = 1e-05
LOG2E = 1.4426950408889634
C2 = 0.125 * LOG2E
BF = jnp.bfloat16
F32 = jnp.float32
AXES = ("dp", "tensor")
MESH = pl.DeviceIdType.MESH
RB = 256
VMEM_ALL = 67_000_000


def dot(a, b, ca=1, cb=0):
    return lax.dot_general(a, b, (((ca,), (cb,)), ((), ())), preferred_element_type=F32)


def sds(shape, dtype):
    return jax.ShapeDtypeStruct(shape, dtype)


def one(shape):
    return pl.BlockSpec(shape, lambda *_: (0,) * len(shape), pipeline_mode=pl.Buffered(1))


ANYS = pl.BlockSpec(memory_space=pl.ANY)


def line(ref):
    v = ref[...]
    return v.reshape(1, v.shape[0])


def params(**kw):
    return pltpu.CompilerParams(vmem_limit_bytes=VMEM_ALL, **kw)


def normed(x):
    mean = jnp.mean(x, axis=-1, keepdims=True)
    cent = x - mean
    var = jnp.mean(cent * cent, axis=-1, keepdims=True)
    rs = lax.rsqrt(var + EPS)
    return cent * rs, rs


HOP_BITS = {'u': [1, 3, 2], 'd': [2, 1, 3], 'o': [2, 1, 3], 'q0': [1, 3, 2], 'q1': [1, 3, 2], 'q2': [2, 1, 3]}
FORWARD_PLAN = {
    3: [(0, 0)],
    4: [(1, 0), (2, 0)],
    5: [(0, 2), (0, 3), (3, 0), (4, 0)],
    6: [(1, 2), (1, 3), (5, 0), (6, 0)],
    7: [(0, 4), (2, 2), (2, 3), (3, 3), (7, 0), (3, 2), (4, 2), (4, 3), (1, 4)],
    8: [(2, 4), (5, 2), (5, 3), (6, 2), (6, 3), (7, 3), (8, 0), (7, 2), (3, 4), (4, 4)],
    9: [(5, 4), (6, 4), (9, 0)],
    10: [(7, 4), (8, 2), (8, 3), (10, 0)],
    11: [(9, 2), (9, 3), (11, 0)],
    12: [(8, 4), (12, 0)],
    13: [(10, 2), (13, 0)],
    14: [(9, 4), (11, 2)],
}
FORWARD_END = [(12, 2), (13, 2)]
MLP_PLAN = {
    (0, 0): [('S', 'u', 1, 3), ('S', 'd', 1, 3), ('S', 'u', 1, 1), ('S', 'd', 1, 1), ('S', 'u', 1, 2), ('S', 'd', 1, 2)],
    (1, 1): [('A', 'u', 1, 3), ('A', 'd', 1, 3)],
    (2, 1): [('A', 'u', 1, 1), ('A', 'd', 1, 1)],
}
MLP_END = [('A', 'u', 1, 2), ('A', 'd', 1, 2)]
BACK_PLAN = {
    (0, 0): [('S', 'o', 0, 7), ('S', 'o', 0, 3), ('S', 'o', 0, 5), ('S', 'o', 0, 6), ('S', 'o', 0, 1), ('S', 'o', 0, 2), ('S', 'o', 0, 4), ('S', 'o', 0, 0), ('S', 'u', 1, 0), ('S', 'd', 1, 0), ('S', 'u', 2, 1), ('S', 'd', 2, 1), ('S', 'u', 2, 0), ('S', 'd', 2, 0)],
    (0, 1): [('A', 'o', 0, 7), ('A', 'o', 0, 3), ('A', 'o', 0, 5), ('A', 'o', 0, 6), ('A', 'o', 0, 1), ('A', 'o', 0, 2), ('A', 'o', 0, 4), ('A', 'o', 0, 0), ('S', 'o', 1, 3), ('S', 'o', 1, 1), ('S', 'o', 1, 2), ('S', 'o', 1, 0)],
    (1, 0): [('S', 'q0', 0, 7), ('S', 'q0', 0, 3), ('S', 'q0', 0, 5), ('S', 'q0', 0, 6), ('S', 'q0', 0, 1), ('S', 'q0', 0, 2), ('S', 'q0', 0, 4), ('S', 'q0', 0, 0)],
    (1, 1): [('A', 'u', 1, 0), ('A', 'd', 1, 0), ('A', 'q0', 0, 7), ('A', 'q0', 0, 3), ('A', 'q0', 0, 5), ('A', 'q0', 0, 6), ('A', 'q0', 0, 1), ('A', 'q0', 0, 2), ('A', 'q0', 0, 4), ('A', 'q0', 0, 0), ('S', 'q0', 1, 3), ('S', 'q0', 1, 1), ('S', 'q0', 1, 2), ('S', 'q0', 1, 0)],
    (2, 0): [('S', 'q1', 0, 7), ('S', 'q1', 0, 3), ('S', 'q1', 0, 5), ('S', 'q1', 0, 6), ('S', 'q1', 0, 1), ('S', 'q1', 0, 2), ('S', 'q1', 0, 4), ('S', 'q1', 0, 0)],
    (2, 1): [('A', 'd', 2, 1), ('A', 'u', 2, 1), ('A', 'q1', 0, 7), ('A', 'q1', 0, 3), ('A', 'q1', 0, 5), ('A', 'q1', 0, 6), ('A', 'q1', 0, 1), ('A', 'q1', 0, 2), ('A', 'q1', 0, 4), ('A', 'q1', 0, 0), ('S', 'q1', 1, 3), ('S', 'q1', 1, 1), ('S', 'q1', 1, 2), ('S', 'q1', 1, 0), ('S', 'u', 3, 0), ('S', 'd', 3, 0)],
    (3, 0): [('A', 'd', 2, 0), ('S', 'q2', 0, 7), ('S', 'q2', 0, 3), ('S', 'q2', 0, 5), ('S', 'q2', 0, 6), ('S', 'q2', 0, 1), ('S', 'q2', 0, 2), ('S', 'q2', 0, 4), ('S', 'q2', 0, 0)],
    (3, 1): [('A', 'q0', 1, 3), ('A', 'o', 1, 3), ('A', 'q2', 0, 7), ('A', 'q2', 0, 3), ('A', 'q2', 0, 5), ('A', 'q2', 0, 6), ('A', 'q2', 0, 1), ('A', 'q0', 1, 1), ('A', 'o', 1, 1), ('A', 'q2', 0, 2), ('A', 'q2', 0, 4), ('A', 'q2', 0, 0), ('S', 'q2', 1, 3), ('S', 'q2', 1, 1), ('S', 'q2', 1, 2), ('S', 'q2', 1, 0), ('S', 'o', 2, 1), ('S', 'q0', 2, 1), ('S', 'o', 2, 0), ('S', 'q0', 2, 0)],
    (4, 0): [('A', 'q0', 1, 2), ('A', 'o', 1, 2), ('A', 'q0', 1, 0), ('A', 'o', 1, 0)],
    (4, 1): [('A', 'u', 2, 0), ('A', 'q1', 1, 3), ('S', 'q1', 2, 1)],
    (5, 0): [('A', 'q1', 1, 1), ('A', 'q1', 1, 2), ('S', 'q1', 2, 0)],
    (5, 1): [('A', 'q1', 1, 0), ('A', 'u', 3, 0), ('A', 'o', 2, 1), ('S', 'o', 3, 0)],
    (6, 0): [('A', 'o', 2, 0)],
    (7, 0): [('A', 'd', 3, 0)],
    (8, 0): [('A', 'q2', 1, 3), ('S', 'q2', 2, 1)],
    (9, 0): [('A', 'q2', 1, 1), ('A', 'q0', 2, 1), ('A', 'q2', 1, 2), ('S', 'q2', 2, 0), ('S', 'q0', 3, 0)],
}
BACK_END = [('A', 'q2', 1, 0), ('A', 'q2', 2, 1), ('S', 'q2', 3, 0), ('A', 'q0', 2, 0), ('A', 'q2', 2, 0), ('A', 'q1', 2, 1), ('S', 'q1', 3, 0), ('A', 'q1', 2, 0), ('A', 'q0', 3, 0), ('A', 'o', 3, 0), ('A', 'q1', 3, 0), ('A', 'q2', 3, 0)]


def mask_column(mask_ref, step, rows):
    m = mask_ref[...].astype(F32).T
    lane = lax.broadcasted_iota(jnp.int32, m.shape, 1)
    per = rows // 128
    parts = [
        jnp.sum(jnp.where(lane == step * per + j, m, 0.0), axis=1, keepdims=True) for j in range(per)
    ]
    return jnp.concatenate(parts, axis=0)


def flipped(me, bit):
    return me + (1 << bit) * (1 - 2 * ((me // (1 << bit)) % 2))


class Gather:
    ops = 8
    forwards = {0: (2, 3, 1), 2: (4, 5), 3: (6,), 4: (7,)}

    def __init__(self, me, tensor, items, send_sem, recv_sem):
        self.me, self.tensor, self.items, self.send_sem, self.recv_sem = me, tensor, items, send_sem, recv_sem

    def copy(self, i, op):
        src, dst, base, block, first, rows, yz, quarters = self.items[i]
        one, two = (1, 2) if yz else (2, 1)
        piece = self.me % 8
        if quarters:
            piece = self.me % 2 + 2 * ((self.me // (1 << one)) % 2)
            if op == 5:
                piece = flipped(piece, 1)
        else:
            if op in (4, 5, 7):
                piece = flipped(piece, one)
            if op in (6, 7):
                piece = flipped(piece, two)
        at = dst.at[pl.ds(pl.multiple_of(base + piece * block + first, 8), rows), :]
        if op == 0:
            device = {"tensor": 1 - self.tensor}
        else:
            bit = {1: 0, 2: one, 3: two, 4: two, 5: 0, 6: 0, 7: 0}[op]
            device = {"dp": flipped(self.me, bit)}
        k = i * self.ops + op
        return pltpu.make_async_remote_copy(
            src_ref=src.at[pl.ds(first, rows), :] if op == 0 else at,
            dst_ref=at,
            send_sem=self.send_sem.at[k],
            recv_sem=self.recv_sem.at[k],
            device_id=device,
            device_id_type=MESH,
        )

    def start(self, i):
        self.copy(i, 0).start()

    def after(self, i, op):
        self.copy(i, op).wait_recv()
        for other in self.forwards[op]:
            if not self.items[i][7] or other in (1, 2, 5):
                self.copy(i, other).start()

    def collect(self, i):
        for op in (1, 5) if self.items[i][7] else (1, 5, 6, 7):
            self.copy(i, op).wait_recv()

    def finish_send(self, i):
        for op in (0, 1, 2, 5) if self.items[i][7] else range(self.ops):
            self.copy(i, op).wait_send()


def greet_gather(me, tensor):
    barrier = pltpu.get_barrier_semaphore()
    pl.semaphore_signal(barrier, inc=1, device_id={"tensor": 1 - tensor}, device_id_type=MESH)
    for bit in range(3):
        pl.semaphore_signal(barrier, inc=1, device_id={"dp": flipped(me, bit)}, device_id_type=MESH)
    pl.semaphore_wait(barrier, 4)


class Reduce:
    def __init__(self, dp, me, name, source, home, more, send_sem, recv_sem):
        self.dp, self.me, self.source, self.home, self.more = dp, me, source, home, more
        self.send_sem, self.recv_sem = send_sem, recv_sem
        self.hops = dp.bit_length() - 1
        self.order = list(range(self.hops))
        if self.hops >= 4:
            self.order[1:4] = HOP_BITS[name]

    def block(self, j, m, keep):
        total = 0
        for i, bit in enumerate(self.order):
            mine = (self.me // (1 << bit)) % 2
            if i < j or (i == j and keep):
                total = total + mine * (1 << bit)
            elif i == j:
                total = total + (1 - mine) * (1 << bit)
            else:
                total = total + ((mine + m // (1 << (i - j - 1))) % 2) * (1 << bit)
        return total

    def count(self, j):
        return self.dp >> (j + 1)

    def base(self, j):
        return self.dp // 2 - (self.dp >> j)

    def copy(self, j, m):
        b = self.block(j, m, False)
        if j == 0:
            src, dst, k = self.source.at[b], self.home.at[b // 2], m
        else:
            at = self.base(j) + m
            src, dst, k = self.home.at[b // 2], self.more.at[at], self.dp // 2 + at
        return pltpu.make_async_remote_copy(
            src_ref=src,
            dst_ref=dst,
            send_sem=self.send_sem.at[k],
            recv_sem=self.recv_sem.at[k],
            device_id={"dp": flipped(self.me, self.order[j])},
            device_id_type=MESH,
        )

    def start(self, j, m):
        self.copy(j, m).start()

    def add(self, j, m, kept=None):
        self.copy(j, m).wait_recv()
        at = self.block(j, m, True) // 2
        if j > 0:
            ref, i = self.more, self.base(j) + m
        else:
            ref, i = (self.source, self.block(0, m, True)) if kept is None else (kept, m)
        self.home[at] = self.home[at] + ref[i]

    def finish_send(self, j, m):
        self.copy(j, m).wait_send()

    def every(self, j, do):
        n = self.count(j)
        if n > 8:

            @pl.loop(0, n)
            def _(m):
                do(m)
        else:
            for m in range(n):
                do(m)


def reduce_scratch(dp, rows, cols):
    return [
        pltpu.VMEM((dp // 2, rows, cols), F32),
        pltpu.VMEM((dp // 2 - 1, rows, cols), F32),
        pltpu.SemaphoreType.DMA((dp - 1,)),
        pltpu.SemaphoreType.DMA((dp - 1,)),
    ]


def store_blocks(out, value, at=slice(None)):
    rows = out.shape[1]
    n = value.shape[0] // rows
    if rows % 8 == 0:
        out[:, :, at] = value.reshape(n, rows, value.shape[1])
    else:
        for b in range(n):
            out[b, :, at] = value[b * rows : (b + 1) * rows, :]


def rope(x, cos, sin):
    lane = lax.broadcasted_iota(jnp.int32, x.shape, 1)
    other = jnp.where(lane % HD < HD // 2, pltpu.roll(x, 128 - HD // 2, 1), pltpu.roll(x, HD // 2, 1))
    return x * cos + other * sin


def project(y, width, cos, sin, q_ref, k_ref, v_ref):
    for c in range(0, width, 128):
        q_ref[:, c : c + 128] = rope(y[:, c : c + 128], cos, sin).astype(BF)
        k_ref[:, c : c + 128] = rope(y[:, width + c : width + c + 128], cos, sin).astype(BF)
    v_ref[...] = y[:, 2 * width :].astype(BF)


def attend_pair(q_ref, k_ref, v_ref, at, o_ref, lse_ref, pair, oT, sbuf):
    length = q_ref.shape[0]
    wide = sbuf.shape[2]
    kk = k_ref[:, at]
    qT, vT = q_ref[:, at].T, v_ref[:, at].T
    row = lax.broadcasted_iota(jnp.int32, (128, wide), 0)
    items = [(h, c) for h in range(2) for c in range(0, length, wide)]

    def scores(i):
        h, c = items[i]
        qq = qT[:, c : c + wide]
        s = dot(kk, jnp.where((row < HD) == (h == 0), qq, jnp.zeros_like(qq)))
        sbuf[i % 2] = s
        return jnp.max(s, axis=0, keepdims=True)

    top = scores(0)
    for i, (h, c) in enumerate(items):
        following = scores(i + 1) if i + 1 < len(items) else None
        p = jnp.exp2((sbuf[i % 2] - top) * C2)
        total = jnp.sum(p, axis=0, keepdims=True)
        oT[h * HD : (h + 1) * HD, c : c + wide] = dot(vT[h * HD : (h + 1) * HD, :], p.astype(BF)) * (1.0 / total)
        lse_ref[pl.ds(pair, 1), h : h + 1, c : c + wide] = (top * C2 + jnp.log2(total))[None]
        top = following
    o_ref[:, at] = oT[...].T.astype(BF)


def gelu_parts(x):
    c0, c1 = 0.7978845608028654, 0.044715
    x2 = x * x
    t = jnp.tanh(x * (c0 + (c0 * c1) * x2))
    a = 0.5 + 0.5 * t
    d = a + (x * (0.5 - 0.5 * (t * t))) * (c0 + (3.0 * c0 * c1) * x2)
    return x * a, d


def forward_kernel(
    nb, bucket, mask, mvec, gain1, gain2, bada, bup,
    tok_h, te_h, wada_h, wq_h, cos_h, sin_h, bup_h, wqf_h, wo_h, wup_h, wdown_h, cot_h,
    h1_ref, q_ref, k_ref, v_ref, mods_ref, cond_ref, o_ref, lse_ref, wxq_ref, wxo_ref,
    attn_ref, h2_ref, feed_ref, gh_ref, gbup_ref, fu, fd, bupx, ku, kd, ru, rd,
    oT, sbuf, fq, fo, wo, wup, wdown, cot, act_s, gp_s, gf_s, lq, lo, lu, ld, pq, po, pu, pd,
    du_s, dd_s, tok, te, wada, wq, cos, sin, first_sem, load_sem, send_sem, recv_sem, bup_sem, keep_sem, give_sem, take_sem,
):
    step = pl.program_id(0)
    me, tensor = lax.axis_index("dp"), lax.axis_index("tensor")
    cols = q_ref.shape[2]
    pairs = cols // 128
    width = tok.shape[1]
    items = []
    for p in range(pairs):
        n = pq.shape[1]
        items += [(pq.at[p], fq.at[p], 0, n, i * (n // 2), n // 2, i == 0, False) for i in range(2)]
    for src, dst in ((po, fo), (pu, fu)):
        n = src.shape[0]
        items += [(src, dst, 0, n, i * (n // 2), n // 2, i == 0, False) for i in range(2)]
    n = pd.shape[1]
    for s in range(2):
        items += [(pd.at[i], fd, i * 4 * n, n, s * (n // 2), n // 2, i == 0, True) for i in range(2)]
    gather = Gather(me, tensor, items, send_sem, recv_sem)
    pieces = []
    for i, (src, dst) in enumerate(((wqf_h, lq), (wo_h, lo), (wup_h, lu))):
        n = dst.shape[0]
        at = pl.ds(pl.multiple_of((me % 8) * n, 16), n)
        pieces.append(pltpu.make_async_copy(src.at[at, :], dst, load_sem.at[i]))
    for i in range(2):
        n = ld.shape[1]
        quarter = me % 2 + 2 * ((me // (2 << i)) % 2)
        at = pl.ds(pl.multiple_of((4 * i + quarter) * n, 16), n)
        pieces.append(pltpu.make_async_copy(wdown_h.at[at, :], ld.at[i], load_sem.at[3 + i]))
    loads = [
        pltpu.make_async_copy(src, dst, load_sem.at[5 + i])
        for i, (src, dst) in enumerate(((wo_h, wo), (wup_h, wup), (wdown_h, wdown), (cot_h, cot)))
    ]
    early = [
        pltpu.make_async_copy(src, dst, first_sem.at[i])
        for i, (src, dst) in enumerate(
            ((te_h, te), (wada_h, wada), (tok_h, tok), (wq_h, wq), (cos_h, cos), (sin_h, sin))
        )
    ]
    bias = pltpu.make_async_remote_copy(
        src_ref=bup_h, dst_ref=bupx, send_sem=bup_sem.at[0], recv_sem=bup_sem.at[1],
        device_id={"tensor": 1 - tensor}, device_id_type=MESH,
    )
    core = me % 2
    dp = du_s.shape[0]

    def parts(k, i):
        src, keep, take = ((du_s, ku, ru), (dd_s, kd, rd))[k]
        stay = pltpu.make_async_copy(src.at[2 * i + core], keep.at[i], keep_sem.at[k, i])
        give = pltpu.make_async_remote_copy(
            src_ref=src.at[2 * i + 1 - core], dst_ref=take.at[i], send_sem=give_sem.at[k, i],
            recv_sem=take_sem.at[k, i], device_id={"dp": flipped(me, 0)}, device_id_type=MESH,
        )
        return stay, give

    def split(first, last, do):
        @pl.loop(first, last)
        def _(i):
            for k in range(2):
                for c in parts(k, i):
                    do(c)

    s_own, s_other = nb, nb + pairs
    s_mlp = s_other + pairs
    s_dw = s_mlp + nb

    @pl.when(step == 0)
    def _():
        for c in pieces + early:
            c.start()
        barrier = pltpu.get_barrier_semaphore()
        pl.semaphore_signal(barrier, inc=1, device_id={"tensor": 1 - tensor}, device_id_type=MESH)
        for bit in range(3):
            pl.semaphore_signal(barrier, inc=1, device_id={"dp": flipped(me, bit)}, device_id_type=MESH)
        pieces[0].wait()
        for p in range(pairs):
            pq[p] = lq[:, p * 128 : (p + 1) * 128].astype(F32)
        pl.semaphore_wait(barrier, 4)
        for i in range(2 * pairs):
            gather.start(i)
        for c in pieces[1:]:
            c.wait()
        for src, dst in ((lo, po), (lu, pu), (ld, pd)):
            dst[...] = src[...].astype(F32)
        for c in early:
            c.wait()
        for i in range(2 * pairs, len(items)):
            gather.start(i)
        bias.start()
        for c in loads:
            c.start()

    for at, todo in FORWARD_PLAN.items():

        @pl.when(step == at)
        def _():
            for i, op in todo:
                gather.after(i, op)

    @pl.when(step == s_dw + 1)
    def _():
        split(0, dp // 4, lambda c: c.start())

    @pl.when(step == 0)
    def _():
        row = te[...]
        sub = lax.broadcasted_iota(jnp.int32, row.shape, 0)
        row = jnp.sum(jnp.where(sub == bucket[...], row, 0.0), axis=0, keepdims=True)
        row = row * (1.0 / (1.0 + jnp.exp(-row)))
        cond_ref[...] = row
        col = jnp.broadcast_to(row, (8, row.shape[1])).T[:, 0:1]
        bias_row = line(bada)
        for i in range(6):
            cs = slice(i * width, (i + 1) * width)
            mods_ref[i : i + 1, :] = jnp.sum(wada[:, cs].astype(F32) * col, axis=0, keepdims=True) + bias_row[:, cs]

    def block(first):
        return pl.ds(pl.multiple_of((step - first) * RB, RB), RB)

    @pl.when(step < s_own)
    def _():
        rows = block(0)
        x = tok[rows, :].astype(F32) + mask_column(mask, step, RB) * line(mvec)
        n, _ = normed(x)
        h = (n * (line(gain1) * (1.0 + mods_ref[1:2, :])) + mods_ref[0:1, :]).astype(BF)
        h1_ref[rows, :] = h
        y = jnp.concatenate([dot(h, wq[i]) for i in range(3)], axis=1)
        project(y, cols, cos[rows, :], sin[rows, :], q_ref.at[0, rows, :], k_ref.at[0, rows, :], v_ref.at[0, rows, :])

    def attend(half, pair):
        at = pl.ds(pl.multiple_of(pair * 128, 128), 128)
        attend_pair(
            q_ref.at[half], k_ref.at[half], v_ref.at[half], at, o_ref.at[half], lse_ref, half * pairs + pair, oT, sbuf
        )

    for p in range(pairs):

        @pl.when(step == s_other + p)
        def _():
            for i in (2 * p, 2 * p + 1):
                gather.collect(i)

    @pl.when((step >= s_other) & (step < s_mlp))
    def _():
        p = step - s_other
        at = pl.ds(pl.multiple_of(p * 128, 128), 128)
        for i in range(3):
            wxq_ref[i, :, at] = fq[p, i * width : (i + 1) * width, :].astype(BF)
        w = jnp.concatenate([wxq_ref[i, :, at] for i in range(3)], axis=1)
        for r in range(0, tok.shape[0], RB):
            rows = slice(r, r + RB)
            project(
                dot(h1_ref[rows, :], w), 128, cos[rows, :], sin[rows, :],
                q_ref.at[1, rows, at], k_ref.at[1, rows, at], v_ref.at[1, rows, at],
            )

    @pl.when((step >= s_own) & (step < s_mlp))
    def _():
        half = (step - s_own) // pairs
        attend(half, step - s_own - half * pairs)

    @pl.when(step == s_mlp)
    def _():
        for i in (2 * pairs, 2 * pairs + 1):
            gather.collect(i)
        wxo_ref[...] = fo[...].astype(BF)
        for c in loads:
            c.wait()
        gbup_ref[...] = jnp.zeros_like(gbup_ref)

    @pl.when((step >= s_mlp) & (step < s_dw))
    def _():
        rows = block(s_mlp)
        x = tok[rows, :].astype(F32) + mask_column(mask, step - s_mlp, RB) * line(mvec)
        attn = dot(o_ref[0, rows, :], wo[...]) + dot(o_ref[1, rows, :], wxo_ref[...])
        attn_ref[...] = attn
        n, _ = normed(x + mods_ref[2:3, :] * attn)
        h = (n * (line(gain2) * (1.0 + mods_ref[4:5, :])) + mods_ref[3:4, :]).astype(BF)
        h2_ref[rows, :] = h
        act, slope = gelu_parts(dot(h, wup[...]) + line(bup))
        act = act.astype(BF)
        act_s[rows, :] = act
        feed_ref[...] = dot(act, wdown[...])
        gf = (mods_ref[5:6, :] * cot[rows, :].astype(F32)).astype(BF)
        gf_s[rows, :] = gf
        gp = (dot(gf, wdown[...], 1, 1) * slope).astype(BF)
        gp_s[rows, :] = gp
        gh_ref[...] = dot(gp, wup[...], 1, 1)
        gbup_ref[...] += jnp.sum(gp.astype(F32), axis=0, keepdims=True)

    @pl.when(step >= s_dw)
    def _():
        part = width // 2
        cs = pl.ds(pl.multiple_of((step - s_dw) * part, 128), part)
        blocks = pl.ds((step - s_dw) * (dp // 2), dp // 2)
        store_blocks(du_s.at[blocks], dot(h2_ref[:, cs], gp_s[...], 0, 0))
        store_blocks(dd_s.at[blocks], dot(gf_s[:, cs], act_s[...], 0, 0))

    @pl.when(step == pl.num_programs(0) - 1)
    def _():
        for i, op in FORWARD_END[:2]:
            gather.after(i, op)
        split(dp // 4, dp // 2, lambda c: c.start())
        for i, op in FORWARD_END[2:]:
            gather.after(i, op)
        for i in range(2 * pairs + 2, len(items)):
            gather.collect(i)
        for i in range(len(items)):
            gather.finish_send(i)
        bias.wait()
        split(0, dp // 2, lambda c: c.wait())


def forward(dp, bucket, tokens, mask2, mvec, gain1, gain2, te, wada, bada, wq, cos, sin, bup, wo, wup, wdown, cot):
    rows, width = tokens.shape
    cols, ff = wq.shape[2], wup.shape[1]
    nb, pairs = rows // RB, cols // 128
    s_mlp = nb + 2 * pairs
    mblk = pl.BlockSpec((RB, width), lambda i: (jnp.clip(i - s_mlp, 0, nb - 1), 0))
    grad = (dp, width // dp, ff)
    half = sds((dp // 2, *grad[1:]), F32)
    act = (2, rows, cols)
    wqf = wq.reshape(3 * width, cols)
    vm = pltpu.VMEM
    piece = lambda w: (w.shape[0] // 8, w.shape[1])
    n_items = 2 * pairs + 8
    return pl.pallas_call(
        functools.partial(forward_kernel, nb),
        grid=(s_mlp + nb + 2,),
        in_specs=[
            one(x.shape) for x in (bucket, mask2, mvec, gain1, gain2, bada, bup)
        ] + [ANYS] * 12,
        out_specs=[
            one((rows, width)), one(act), one(act), one(act), one((8, width)), one((1, te.shape[1])),
            one(act), one((2 * pairs, 2, rows)), one(wq.shape), one((cols, width)),
            mblk, one((rows, width)), mblk, mblk, one((1, ff)), *[ANYS] * 7,
        ],
        out_shape=[
            sds((rows, width), BF), sds(act, BF), sds(act, BF), sds(act, BF), sds((8, width), F32),
            sds((1, te.shape[1]), F32), sds(act, BF), sds((2 * pairs, 2, rows), F32), sds(wq.shape, BF),
            sds((cols, width), BF), sds((rows, width), F32), sds((rows, width), BF), sds((rows, width), F32),
            sds((rows, width), F32), sds((1, ff), F32), sds(wup.shape, F32), sds(wdown.shape, F32),
            sds(bup.shape, F32), half, half, half, half,
        ],
        scratch_shapes=[
            vm((128, rows), F32), vm((2, rows, 512), F32), vm((pairs, 3 * width, 128), F32), vm(wo.shape, F32),
            vm(wo.shape, BF), vm(wup.shape, BF), vm(wdown.shape, BF), vm(cot.shape, BF),
            vm((rows, ff), BF), vm((rows, ff), BF), vm((rows, width), BF),
            *[vm(piece(w), BF) for w in (wqf, wo, wup)], vm((2, *piece(wdown)), BF),
            vm((pairs, piece(wqf)[0], 128), F32), *[vm(piece(w), F32) for w in (wo, wup)],
            vm((2, *piece(wdown)), F32), vm(grad, F32), vm(grad, F32),
            *[vm(x.shape, x.dtype) for x in (tokens, te, wada, wq, cos, sin)],
            pltpu.SemaphoreType.DMA((6,)), pltpu.SemaphoreType.DMA((9,)), pltpu.SemaphoreType.DMA((8 * n_items,)),
            pltpu.SemaphoreType.DMA((8 * n_items,)), pltpu.SemaphoreType.DMA((2,)),
            *[pltpu.SemaphoreType.DMA((2, dp // 2))] * 3,
        ],
        compiler_params=params(collective_id=2, has_side_effects=True),
        name="forward",
    )(
        bucket, mask2, mvec, gain1, gain2, bada, bup, tokens, te, wada, wq, cos, sin, bup, wqf, wo, wup, wdown, cot
    )


def hidden(h, gf, wup, bup, wdown):
    wide = wup.shape[1] // 3
    feed = gh = None
    dots = lambda c: (dot(h, wup[:, c : c + wide]) + bup[:, c : c + wide], dot(gf, wdown[c : c + wide, :], 1, 1))
    ready = dots(0)
    for c in range(0, 3 * wide, wide):
        following = dots(c + wide) if c + wide < 3 * wide else None
        act, slope = gelu_parts(ready[0])
        gp = (ready[1] * slope).astype(BF)
        f = dot(act.astype(BF), wdown[c : c + wide, :])
        d = dot(gp, wup[:, c : c + wide], 1, 1)
        feed, gh = (f, d) if feed is None else (feed + f, gh + d)
        ready = following
    return feed, gh


def mlp_other_kernel(
    dp, tok, mask, mvec, mods, gain, attn_ref, h_ref, feed_ref, gh_ref, cot, bup, bdown,
    mo, wo, wx, gbup, cond, ku, kd, ru, rd, fu, fd,
    res_ref, gmid_ref, gm_ref, small, dw_ref, hu_out, hd_out,
    acc, keep_u, keep_d, load_sem, stage_u, stage_d, wup, wdown, w_sem,
    hu, more_u, send_u, recv_u, hd, more_d, send_d, recv_d,
):
    step, last = pl.program_id(0), pl.num_programs(0) - 1
    me, tensor = lax.axis_index("dp"), lax.axis_index("tensor")
    weights = {
        "u": Reduce(dp, me, "u", None, hu, more_u, send_u, recv_u),
        "d": Reduce(dp, me, "d", None, hd, more_d, send_d, recv_d),
    }

    def act(kind, w, j, m):
        if kind == "S":
            weights[w].start(j, m)
        else:
            weights[w].add(j, m)

    def point(at):
        if dp == 16 and at in MLP_PLAN:

            @pl.when(step == at[0])
            def _():
                for a in MLP_PLAN[at]:
                    act(*a)

    halves = [
        pltpu.make_async_copy(src, dst, load_sem.at[i])
        for i, (src, dst) in enumerate(((ru, hu), (ku, keep_u), (rd, hd), (kd, keep_d)))
    ]
    wloads = [
        pltpu.make_async_copy(src, dst, w_sem.at[i]) for i, (src, dst) in enumerate(((fu, stage_u), (fd, stage_d)))
    ]

    @pl.when(step == 0)
    def _():
        for c in halves + wloads:
            c.start()
        barrier = pltpu.get_barrier_semaphore()
        for j in range(1, 4):
            pl.semaphore_signal(barrier, inc=1, device_id={"dp": flipped(me, j)}, device_id_type=MESH)
        small[...] = jnp.zeros_like(small)
        pl.semaphore_wait(barrier, 3)
        for i, (home, keep) in enumerate(((hu, keep_u), (hd, keep_d))):
            halves[2 * i].wait()
            halves[2 * i + 1].wait()

            @pl.loop(0, dp // 2)
            def _(b):
                home[b] = home[b] + keep[b]

            if dp == 16:
                for a in MLP_PLAN[0, 0]:
                    if a[1] == "ud"[i]:
                        act(*a)
        for c, src, dst in zip(wloads, (stage_u, stage_d), (wup, wdown)):
            c.wait()
            dst[...] = src[...].astype(BF)

    for i in range(1, 4):
        point((i, 0))

    x = tok[...].astype(F32) + mask_column(mask, step, tok.shape[0]) * line(mvec)
    attn = attn_ref[...]
    middle = x + mods[2:3, :] * attn
    n2, rs = normed(middle)
    g = cot[...].astype(F32)
    gf = (mods[5:6, :] * g).astype(BF)
    feed, gh = hidden(h_ref[...], gf, wup, line(bup), wdown)
    feed = (feed_ref[...] + feed) + line(bdown)
    gh = gh_ref[...] + gh

    for i in range(4):
        point((i, 1))
    res_ref[...] = (middle + mods[5:6, :] * feed).astype(BF)
    opened = 1.0 + mods[4:5, :]
    e = gh * (opened * line(gain))
    inner = jnp.mean(e * n2, axis=-1, keepdims=True)
    gmid = g + (e - jnp.mean(e, axis=-1, keepdims=True) - n2 * inner) * rs
    gmid_ref[...] = gmid
    ga = (mods[2:3, :] * gmid).astype(BF)
    gm_ref[0] = dot(ga, wo[...], 1, 1).astype(BF)
    gm_ref[1] = dot(ga, wx[...], 1, 1).astype(BF)
    col = lambda v: jnp.sum(v, axis=0, keepdims=True)
    small[0:1, :] += col(g * feed)
    small[1:2, :] += col(gf.astype(F32))
    small[2:3, :] += col(gh)
    small[3:4, :] += col(gh * n2)
    small[4:5, :] += col(gmid * attn)
    dw = dot(ga, mo[...], 0, 0)

    @pl.when(step == 0)
    def _():
        acc[...] = dw

    @pl.when(step > 0)
    def _():
        acc[...] += dw

    @pl.when(step == last)
    def _():
        width = mods.shape[1]
        small[5:6, :] = small[3:4, :] * opened
        small[3:4, :] = small[3:4, :] * line(gain)
        for i in range(gbup.shape[1] // width):
            small[8 + i : 9 + i, :] = gbup[:, i * width : (i + 1) * width]
        small[6:7, 0 : cond.shape[1]] = cond[...]
        store_blocks(dw_ref, acc[...])
        if dp == 16:
            for a in MLP_END:
                act(*a)
            for todo in (*MLP_PLAN.values(), MLP_END):
                for kind, w, j, m in todo:
                    if kind == "S":
                        weights[w].finish_send(j, m)
        stores = [
            pltpu.make_async_copy(src, dst, w_sem.at[k]) for k, (src, dst) in enumerate(((hu, hu_out), (hd, hd_out)))
        ]
        for c in stores:
            c.start()
        for c in stores:
            c.wait()


def mlp_other(dp, tokens, mask2, mvec, mods, gain, attn, h, feed, gh, cot, bup, bdown, os, wo, wx, gbup, cond, ku, kd, ru, rd, fu, fd):
    rows, width = tokens.shape
    ff, cols = fu.shape[1], wo.shape[0]
    part = width // dp
    blk = lambda c: pl.BlockSpec((RB, c), lambda i: (i, 0))
    half = (dp // 2, part, ff)
    vm = pltpu.VMEM
    return pl.pallas_call(
        functools.partial(mlp_other_kernel, dp),
        grid=(rows // RB,),
        in_specs=[
            blk(width), one(mask2.shape), one(mvec.shape), one(mods.shape), one(gain.shape),
            blk(width), blk(width), blk(width), blk(width), blk(width), one(bup.shape), one(bdown.shape),
            pl.BlockSpec((None, RB, cols), lambda i: (0, i, 0)), one(wo.shape), one(wx.shape), one(gbup.shape),
            one(cond.shape), *[ANYS] * 6,
        ],
        out_specs=[
            blk(width), blk(width), pl.BlockSpec((2, RB, cols), lambda i: (0, i, 0)), one((16, width)),
            one((dp, part, cols)), ANYS, ANYS,
        ],
        out_shape=[
            sds((rows, width), BF), sds((rows, width), F32), sds((2, rows, cols), BF), sds((16, width), F32),
            sds((dp, part, cols), F32), sds(half, F32), sds(half, F32),
        ],
        scratch_shapes=[
            vm((width, cols), F32), vm(half, F32), vm(half, F32), pltpu.SemaphoreType.DMA((4,)),
            vm(fu.shape, F32), vm(fd.shape, F32), vm(fu.shape, BF), vm(fd.shape, BF), pltpu.SemaphoreType.DMA((2,)),
            *reduce_scratch(dp, part, ff), *reduce_scratch(dp, part, ff),
        ],
        compiler_params=params(collective_id=3, has_side_effects=True),
        name="mlp_other",
    )(tokens, mask2, mvec, mods, gain, attn, h, feed, gh, cot, bup, bdown, os, wo, wx, gbup, cond, ku, kd, ru, rd, fu, fd)


def attend_back_pair(q_ref, k_ref, v_ref, o_ref, do_ref, lse_ref, cosT, sinT, g_ref, at, gT, between):
    length = q_ref.shape[0]
    kk, vv = k_ref[...], v_ref[...]
    kT, qT, doT = kk.T, q_ref[...].T, do_ref[...].T
    oT = o_ref[...].T
    prod = doT.astype(F32) * oT.astype(F32)
    row = lax.broadcasted_iota(jnp.int32, (128, length), 0)
    half = HD // 2
    for h in range(2):
        hs = slice(h * HD, (h + 1) * HD)
        sel = (row < HD) == (h == 0)
        qm = jnp.where(sel, qT, jnp.zeros_like(qT))
        dm = jnp.where(sel, doT, jnp.zeros_like(doT))
        inner = jnp.sum(prod[hs, :], axis=0, keepdims=True)
        p = jnp.exp2(dot(kk, qm) * C2 - lse_ref[h : h + 1, :])
        ds = (p * (dot(vv, dm) - inner)).astype(BF)
        dv = dot(doT[hs, :], p.astype(BF), 1, 1)
        dk = dot(qT[hs, :], ds, 1, 1) * 0.125
        dq = dot(kT[hs, :], ds) * 0.125
        c, s = cosT[...], sinT[...]
        for i, d in ((0, dq), (1, dk)):
            a, b = d[:half, :], d[half:, :]
            gT[i, h * HD : h * HD + half, :] = a * c + b * s
            gT[i, h * HD + half : (h + 1) * HD, :] = b * c - a * s
        gT[2, hs, :] = dv
        if h == 0:
            between()
    for i in range(3):
        g_ref[i, :, at] = gT[i].T.astype(BF)


def backward_kernel(
    dp, nb, pairs, q_ref, k_ref, v_ref, o_ref, do_ref, lse_ref, cosT, sinT, h1_h, w_h, wx_h, tok, mask, mvec,
    mods, gain, gmid_ref, small, dw_hbm, hu_in, hd_in,
    gt_ref, up_ref, down_ref, out_ref, qkv_ref, got_ref,
    gT, g, h1, w, wx, dw_out, dqs, late_s, pack, got, own_sem, gsend, grecv, load_sem, *scratch,
):
    step, last = pl.program_id(0), pl.num_programs(0) - 1
    me, tensor = lax.axis_index("dp"), lax.axis_index("tensor")
    names = ["u", "d", "o"] + [f"q{p}" for p in range(pairs)]
    sources = [None, None, dw_out] + [dqs.at[p] for p in range(pairs)]
    weights = {
        n: Reduce(dp, me, n, src, *scratch[4 * i : 4 * i + 4]) for i, (n, src) in enumerate(zip(names, sources))
    }
    hops = weights["u"].hops
    width, cols = mods.shape[1], w.shape[2]
    loads = [
        pltpu.make_async_copy(src, dst, load_sem.at[i])
        for i, (src, dst) in enumerate(((dw_hbm, dw_out), (hu_in, weights["u"].home), (hd_in, weights["d"].home)))
    ]
    later = [
        pltpu.make_async_copy(src, dst, load_sem.at[3 + i]) for i, (src, dst) in enumerate(((h1_h, h1), (w_h, w), (wx_h, wx)))
    ]
    s_x, s_end = pairs, 2 * pairs
    n = width // dp

    def act(kind, n, j, m):
        if kind == "S":
            weights[n].start(j, m)
        else:
            weights[n].add(j, m)

    def point(at):
        if dp == 16 and at in BACK_PLAN:

            @pl.when(step == at[0])
            def _():
                for a in BACK_PLAN[at]:
                    act(*a)

    def pack_rows(summed, gmod, cond):
        for d in range(dp):
            for i in range(4):
                if summed[i] is not None:
                    pack[d, :, i * n : (i + 1) * n] = summed[i][:, d * n : (d + 1) * n]
            row, off = 4 + 2 * n * d // width, 2 * n * d % width
            if summed[row] is not None:
                pack[d, :, 4 * n : 6 * n] = summed[row][:, off : off + 2 * n]
            done, need = 0, 6 * n
            while done < need:
                row, off = (need * d + done) // width, (need * d + done) % width
                take = min(need - done, width - off)
                if gmod[row] is not None:
                    pack[d, :, PACK_MOD + done : PACK_MOD + done + take] = gmod[row][:, off : off + take]
                done += take
            if cond is not None:
                pack[d, :, PACK_COND : PACK_COND + 128] = cond

    def spread(r):
        to = (me + r) % dp
        return pltpu.make_async_remote_copy(
            src_ref=pack.at[to], dst_ref=got.at[me], send_sem=gsend.at[r], recv_sem=grecv.at[r],
            device_id=(to, tensor), device_id_type=MESH,
        )

    @pl.when(step == 0)
    def _():
        for c in loads:
            c.start()
        barrier = pltpu.get_barrier_semaphore()

        @pl.loop(1, dp)
        def _(r):
            pl.semaphore_signal(barrier, inc=1, device_id=((me + r) % dp, tensor), device_id_type=MESH)

        pl.semaphore_wait(barrier, dp - 1)
        for c in loads:
            c.wait()
        for c in later:
            c.start()
        late_s[...] = jnp.zeros_like(late_s)
        pack[...] = jnp.zeros_like(pack)
        summed = [None, None, small[5:6, :], small[1:2, :], small[8:9, :], small[9:10, :]]
        gmod = [None, None, small[4:5, :], small[2:3, :], small[3:4, :], small[0:1, :]]
        pack_rows(summed, gmod, small[6:7, 0:128])

    for i in range(2 * pairs + nb):
        point((i, 0))

    def between():
        for p in range(2 * pairs):
            point((p, 1))

    @pl.when(step < s_end)
    def _():
        half = step // pairs
        at = pl.ds(pl.multiple_of((step - half * pairs) * 128, 128), 128)
        attend_back_pair(q_ref, k_ref, v_ref, o_ref, do_ref, lse_ref, cosT, sinT, g.at[half], at, gT, between)

    @pl.when(step == 0)
    def _():
        for c in later:
            c.wait()

    @pl.when(step < s_x)
    def _():
        at = pl.ds(pl.multiple_of(step * 128, 128), 128)
        gp = jnp.concatenate([g[0, i, :, at] for i in range(3)], axis=1)
        store_blocks(dqs.at[step], dot(h1[...], gp, 0, 0))

    @pl.when(step >= s_end)
    def _():
        i = step - s_end
        rows = pl.ds(pl.multiple_of(i * RB, RB), RB)
        m = mask_column(mask, i, RB)
        n1, rs = normed(tok[...].astype(F32) + m * line(mvec))
        parts = [
            dot(d[0, rows, :], ww[0], 1, 1) + dot(d[1, rows, :], ww[1], 1, 1) + dot(d[2, rows, :], ww[2], 1, 1)
            for d, ww in ((g.at[0], w), (g.at[1], wx))
        ]
        gh = parts[0] + parts[1]
        e = gh * ((1.0 + mods[1:2, :]) * line(gain))
        inner = jnp.mean(e * n1, axis=-1, keepdims=True)
        gs = gmid_ref[...] + (e - jnp.mean(e, axis=-1, keepdims=True) - n1 * inner) * rs
        gt_ref[...] = gs.astype(BF)
        col = lambda v: jnp.sum(v, axis=0, keepdims=True)
        late_s[0:1, :] += col(gh)
        late_s[1:2, :] += col(gh * n1)
        late_s[3:4, :] += col(m * gs)

    @pl.when(step == last)
    def _():
        late_s[2:3, :] = late_s[1:2, :] * (1.0 + mods[1:2, :])
        late_s[1:2, :] = late_s[1:2, :] * line(gain)
        none = [None] * 4
        pack_rows([late_s[3:4, :], late_s[2:3, :]] + none, [late_s[0:1, :], late_s[1:2, :]] + none, None)
        if dp == 16:
            for a in BACK_END[:2]:
                act(*a)
        own = pltpu.make_async_copy(pack.at[me], got.at[me], own_sem)
        own.start()

        @pl.loop(1, dp)
        def _(r):
            spread(r).start()

        if dp == 16:
            for a in BACK_END[2:]:
                act(*a)
            todo = [a for v in BACK_PLAN.values() for a in v] + BACK_END
            for kind, n, j, m in todo:
                if kind == "S":
                    weights[n].finish_send(j, m)
        else:
            for n, r in weights.items():
                for j in range(1 if n in "ud" else 0, hops):
                    r.every(j, lambda m: r.start(j, m))
                    r.every(j, lambda m: r.add(j, m))
                    r.every(j, lambda m: r.finish_send(j, m))
        up_ref[...] = weights["u"].home[me // 2]
        down_ref[...] = weights["d"].home[me // 2]
        out_ref[...] = weights["o"].home[me // 2]
        for p in range(pairs):
            qkv_ref[p] = weights[f"q{p}"].home[me // 2]
        own.wait()

        @pl.loop(1, dp)
        def _(r):
            spread(r).wait()

        got_ref[...] = got[...]


PACK_MOD, PACK_COND, PACK = 384, 768, 896


def backward(dp, qs, ks, vs, os, gm, lses, cosT, sinT, h1, w, wx, tokens, mask2, mvec, mods, gain, gmid, small, dw_out, hu, hd):
    rows, width = tokens.shape
    cols = w.shape[2]
    nb, pairs = rows // RB, cols // 128
    part, ff = hu.shape[1], hu.shape[2]
    s_end = 2 * pairs
    pick = lambda i: jnp.minimum(i, 2 * pairs - 1)
    pair = pl.BlockSpec((None, rows, 128), lambda i: (pick(i) // pairs, 0, pick(i) % pairs))
    blk = pl.BlockSpec((RB, width), lambda i: (jnp.maximum(i - s_end, 0), 0))
    vm = pltpu.VMEM
    return pl.pallas_call(
        functools.partial(backward_kernel, dp, nb, pairs),
        grid=(s_end + nb,),
        in_specs=[pair] * 5 + [
            pl.BlockSpec((None, 2, rows), lambda i: (pick(i), 0, 0)), one(cosT.shape), one(sinT.shape),
            ANYS, ANYS, ANYS, blk, one(mask2.shape), one(mvec.shape), one(mods.shape),
            one(gain.shape), blk, one(small.shape), ANYS, ANYS, ANYS,
        ],
        out_specs=[
            blk, one((part, ff)), one((part, ff)), one((part, cols)), one((pairs, part, 384)), one((dp, 1, PACK)),
        ],
        out_shape=[
            sds((rows, width), BF), sds((part, ff), F32), sds((part, ff), F32), sds((part, cols), F32),
            sds((pairs, part, 384), F32), sds((dp, 1, PACK), F32),
        ],
        scratch_shapes=[
            vm((3, 128, rows), F32), vm((2, 3, rows, cols), BF), vm(h1.shape, BF), vm(w.shape, BF), vm(wx.shape, BF),
            vm((dp, part, cols), F32),
            vm((pairs, dp, part, 384), F32), vm((8, width), F32), vm((dp, 1, PACK), F32), vm((dp, 1, PACK), F32),
            pltpu.SemaphoreType.DMA, pltpu.SemaphoreType.DMA((dp,)), pltpu.SemaphoreType.DMA((dp,)),
            pltpu.SemaphoreType.DMA((6,)),
            *reduce_scratch(dp, part, ff), *reduce_scratch(dp, part, ff), *reduce_scratch(dp, part, cols),
            *[s for _ in range(pairs) for s in reduce_scratch(dp, part, 384)],
        ],
        compiler_params=params(collective_id=4, has_side_effects=True),
        name="backward",
    )(qs, ks, vs, os, gm, lses, cosT, sinT, h1, w, wx, tokens, mask2, mvec, mods, gain, gmid, small, dw_out, hu, hd)


def finish_kernel(res_in, gt_in, got, up, down, out, qkv, res, gt, mask, ln1, wqkv, wout, ln2, wup, bup, wdown, bdown, wada, bada):
    res[...] = res_in[...]
    gt[...] = gt_in[...]

    @pl.when(pl.program_id(0) == 1)
    def _():
        finish_rest(got, up, down, out, qkv, mask, ln1, wqkv, wout, ln2, wup, bup, wdown, bdown, wada, bada)


def finish_rest(got, up, down, out, qkv, mask, ln1, wqkv, wout, ln2, wup, bup, wdown, bdown, wada, bada):
    dp = got.shape[0]
    g = got[...].reshape(dp, got.shape[2])
    n = wup.shape[0]
    total = jnp.sum(g, axis=0, keepdims=True)
    for i, ref in enumerate((mask, ln1, ln2, bdown)):
        ref[...] = total[:, i * n : (i + 1) * n].reshape(n)
    bup[...] = total[:, 4 * n : 6 * n].reshape(2 * n)
    bada[...] = total[:, PACK_MOD : PACK_MOD + 6 * n].reshape(6 * n)
    wada[...] = lax.dot_general(
        g[:, PACK_MOD : PACK_MOD + 6 * n], g[:, PACK_COND : PACK_COND + wada.shape[1]], (((0,), (0,)), ((), ())),
        precision=lax.Precision.HIGHEST, preferred_element_type=F32,
    )
    wup[...] = up[...]
    wdown[...] = down[...]
    wout[...] = out[...]
    for p in range(qkv.shape[0]):
        for i in range(3):
            wqkv[i, :, p * 128 : (p + 1) * 128] = qkv[p, :, i * 128 : (i + 1) * 128]


def finish(result, grad_tokens, got, up, down, out, qkv, tdim):
    n, ff = up.shape
    cols = out.shape[1]
    shapes = [(n,), (n,), (3, n, cols), (n, cols), (n,), (n, ff), (2 * n,), (n, ff), (n,), (6 * n, tdim), (6 * n,)]
    ins = (got, up, down, out, qkv)
    blk = pl.BlockSpec((result.shape[0] // 2, result.shape[1]), lambda i: (i, 0))
    return pl.pallas_call(
        finish_kernel,
        grid=(2,),
        in_specs=[blk, blk] + [one(x.shape) for x in ins],
        out_specs=[blk, blk] + [one(s) for s in shapes],
        out_shape=[sds(result.shape, BF)] * 2 + [sds(s, F32) for s in shapes],
        compiler_params=params(),
        name="finish",
    )(result, grad_tokens, *ins)


def rope_tables(length):
    half = HD // 2
    freq = 10000.0 ** (-(np.arange(half, dtype=np.float64) / half))
    angle = np.arange(length, dtype=np.float64)[:, None] * freq[None, :]
    return np.cos(angle).astype(np.float32), np.sin(angle).astype(np.float32)


def body(
    dp, tokens, cotangent, bucket, mask, time_embed, mask_vec, ln1_gain, w_qkv, w_out, ln2_gain,
    w_up, b_up, w_down, b_down, w_ada, b_ada,
):
    rows, width = tokens.shape
    mask2 = mask.reshape(rows // 128, 128)
    c, s = rope_tables(rows)
    cos, sin = jnp.asarray(np.tile(c, (1, 4))), jnp.asarray(np.tile(np.concatenate([-s, s], 1), (1, 2)))
    cosT, sinT = jnp.asarray(np.ascontiguousarray(c.T)), jnp.asarray(np.ascontiguousarray(s.T))
    (h1, qs, ks, vs, mods, cond, os, lses, wx_qkv, wx_out, attn, h2, feed, gh2, gbup, fu, fd, bup_x, ku, kd, ru, rd) = forward(
        dp, bucket.reshape(1, 1), tokens, mask2, mask_vec, ln1_gain, ln2_gain, time_embed, w_ada, b_ada, w_qkv,
        cos, sin, b_up, w_out, w_up, w_down, cotangent,
    )
    result, gmid, gm, small, dw_out, hu, hd = mlp_other(
        dp, tokens, mask2, mask_vec, mods, ln2_gain, attn, h2, feed, gh2, cotangent, bup_x, b_down,
        os, w_out, wx_out, gbup, cond, ku, kd, ru, rd, fu, fd,
    )
    grad_tokens, sum_up, sum_down, sum_out, sum_qkv, got = backward(
        dp, qs, ks, vs, os, gm, lses, cosT, sinT, h1, w_qkv, wx_qkv, tokens, mask2, mask_vec, mods, ln1_gain, gmid,
        small, dw_out, hu, hd,
    )
    out = finish(result, grad_tokens, got, sum_up, sum_down, sum_out, sum_qkv, time_embed.shape[1])
    return tuple(x.T if i in (5, 9, 11) else x for i, x in enumerate(out))


def solution(mesh):
    in_specs = (
        P("dp", None), P("dp", None), P("dp"), P("dp"), P(), P(), P(), P(None, None, "tensor"),
        P("tensor", None), P(), P(None, "tensor"), P("tensor"), P("tensor", None), P(), P(), P(),
    )
    out_specs = (
        P("dp", None), P("dp", None), P("dp"), P("dp"), P(None, "dp", "tensor"), P("tensor", "dp"),
        P("dp"), P("dp", "tensor"), P(("tensor", "dp")), P("tensor", "dp"), P("dp"), P(None, "dp"), P("dp"),
    )
    step = functools.partial(body, mesh.shape["dp"])
    return jax.shard_map(step, mesh=mesh, in_specs=in_specs, out_specs=out_specs, check_vma=False)
```

```python
import functools

import jax
import jax.numpy as jnp
import numpy as np
from jax import lax
from jax.experimental import pallas as pl
from jax.experimental.pallas import tpu as pltpu
from jax.sharding import PartitionSpec as P

HD = 64
EPS = 1e-05
LOG2E = 1.4426950408889634
C2 = 0.125 * LOG2E
BF = jnp.bfloat16
F32 = jnp.float32
AXES = ("dp", "tensor")
MESH = pl.DeviceIdType.MESH
RB = 256
VMEM_ALL = 67_000_000


def dot(a, b, ca=1, cb=0):
    return lax.dot_general(a, b, (((ca,), (cb,)), ((), ())), preferred_element_type=F32)


def sds(shape, dtype):
    return jax.ShapeDtypeStruct(shape, dtype)


def one(shape):
    return pl.BlockSpec(shape, lambda *_: (0,) * len(shape), pipeline_mode=pl.Buffered(1))


ANYS = pl.BlockSpec(memory_space=pl.ANY)


def line(ref):
    v = ref[...]
    return v.reshape(1, v.shape[0])


def params(**kw):
    return pltpu.CompilerParams(vmem_limit_bytes=VMEM_ALL, **kw)


def normed(x):
    mean = jnp.mean(x, axis=-1, keepdims=True)
    cent = x - mean
    var = jnp.mean(cent * cent, axis=-1, keepdims=True)
    rs = lax.rsqrt(var + EPS)
    return cent * rs, rs


HOP_BITS = {'u': [1, 3, 2], 'd': [2, 1, 3], 'o': [2, 1, 3], 'q0': [1, 3, 2], 'q1': [1, 3, 2], 'q2': [2, 1, 3]}
FORWARD_PLAN = {
    3: [(0, 0)],
    4: [(1, 0), (2, 0)],
    5: [(0, 2), (0, 3), (3, 0), (4, 0)],
    6: [(1, 2), (1, 3), (5, 0), (6, 0)],
    7: [(0, 4), (2, 2), (2, 3), (3, 3), (7, 0), (3, 2), (4, 2), (4, 3), (1, 4)],
    8: [(2, 4), (5, 2), (5, 3), (6, 2), (6, 3), (7, 3), (8, 0), (7, 2), (3, 4), (4, 4)],
    9: [(5, 4), (6, 4), (9, 0)],
    10: [(7, 4), (8, 2), (8, 3), (10, 0)],
    11: [(9, 2), (9, 3), (11, 0)],
    12: [(8, 4), (12, 0)],
    13: [(10, 2), (13, 0)],
    14: [(9, 4), (11, 2)],
}
FORWARD_END = [(12, 2), (13, 2)]
MLP_PLAN = {
    (0, 0): [('S', 'u', 1, 3), ('S', 'd', 1, 3), ('S', 'u', 1, 1), ('S', 'd', 1, 1), ('S', 'u', 1, 2), ('S', 'd', 1, 2)],
    (1, 1): [('A', 'u', 1, 3), ('A', 'd', 1, 3)],
    (2, 1): [('A', 'u', 1, 1), ('A', 'd', 1, 1)],
}
MLP_END = [('A', 'u', 1, 2), ('A', 'd', 1, 2)]
BACK_PLAN = {
    (0, 0): [('S', 'o', 0, 7), ('S', 'o', 0, 3), ('S', 'o', 0, 5), ('S', 'o', 0, 6), ('S', 'o', 0, 1), ('S', 'o', 0, 2), ('S', 'o', 0, 4), ('S', 'o', 0, 0), ('S', 'u', 1, 0), ('S', 'd', 1, 0), ('S', 'u', 2, 1), ('S', 'd', 2, 1), ('S', 'u', 2, 0), ('S', 'd', 2, 0)],
    (0, 1): [('A', 'o', 0, 7), ('A', 'o', 0, 3), ('A', 'o', 0, 5), ('A', 'o', 0, 6), ('A', 'o', 0, 1), ('A', 'o', 0, 2), ('A', 'o', 0, 4), ('A', 'o', 0, 0), ('S', 'o', 1, 3), ('S', 'o', 1, 1), ('S', 'o', 1, 2), ('S', 'o', 1, 0)],
    (1, 0): [('S', 'q0', 0, 7), ('S', 'q0', 0, 3), ('S', 'q0', 0, 5), ('S', 'q0', 0, 6), ('S', 'q0', 0, 1), ('S', 'q0', 0, 2), ('S', 'q0', 0, 4), ('S', 'q0', 0, 0)],
    (1, 1): [('A', 'u', 1, 0), ('A', 'd', 1, 0), ('A', 'q0', 0, 7), ('A', 'q0', 0, 3), ('A', 'q0', 0, 5), ('A', 'q0', 0, 6), ('A', 'q0', 0, 1), ('A', 'q0', 0, 2), ('A', 'q0', 0, 4), ('A', 'q0', 0, 0), ('S', 'q0', 1, 3), ('S', 'q0', 1, 1), ('S', 'q0', 1, 2), ('S', 'q0', 1, 0)],
    (2, 0): [('S', 'q1', 0, 7), ('S', 'q1', 0, 3), ('S', 'q1', 0, 5), ('S', 'q1', 0, 6), ('S', 'q1', 0, 1), ('S', 'q1', 0, 2), ('S', 'q1', 0, 4), ('S', 'q1', 0, 0)],
    (2, 1): [('A', 'd', 2, 1), ('A', 'u', 2, 1), ('A', 'q1', 0, 7), ('A', 'q1', 0, 3), ('A', 'q1', 0, 5), ('A', 'q1', 0, 6), ('A', 'q1', 0, 1), ('A', 'q1', 0, 2), ('A', 'q1', 0, 4), ('A', 'q1', 0, 0), ('S', 'q1', 1, 3), ('S', 'q1', 1, 1), ('S', 'q1', 1, 2), ('S', 'q1', 1, 0), ('S', 'u', 3, 0), ('S', 'd', 3, 0)],
    (3, 0): [('A', 'd', 2, 0), ('S', 'q2', 0, 7), ('S', 'q2', 0, 3), ('S', 'q2', 0, 5), ('S', 'q2', 0, 6), ('S', 'q2', 0, 1), ('S', 'q2', 0, 2), ('S', 'q2', 0, 4), ('S', 'q2', 0, 0)],
    (3, 1): [('A', 'q0', 1, 3), ('A', 'o', 1, 3), ('A', 'q2', 0, 7), ('A', 'q2', 0, 3), ('A', 'q2', 0, 5), ('A', 'q2', 0, 6), ('A', 'q2', 0, 1), ('A', 'q0', 1, 1), ('A', 'o', 1, 1), ('A', 'q2', 0, 2), ('A', 'q2', 0, 4), ('A', 'q2', 0, 0), ('S', 'q2', 1, 3), ('S', 'q2', 1, 1), ('S', 'q2', 1, 2), ('S', 'q2', 1, 0), ('S', 'o', 2, 1), ('S', 'q0', 2, 1), ('S', 'o', 2, 0), ('S', 'q0', 2, 0)],
    (4, 0): [('A', 'q0', 1, 2), ('A', 'o', 1, 2), ('A', 'q0', 1, 0), ('A', 'o', 1, 0)],
    (4, 1): [('A', 'u', 2, 0), ('A', 'q1', 1, 3), ('S', 'q1', 2, 1)],
    (5, 0): [('A', 'q1', 1, 1), ('A', 'q1', 1, 2), ('S', 'q1', 2, 0)],
    (5, 1): [('A', 'q1', 1, 0), ('A', 'u', 3, 0), ('A', 'o', 2, 1), ('S', 'o', 3, 0)],
    (6, 0): [('A', 'o', 2, 0)],
    (7, 0): [('A', 'd', 3, 0)],
    (8, 0): [('A', 'q2', 1, 3), ('S', 'q2', 2, 1)],
    (9, 0): [('A', 'q2', 1, 1), ('A', 'q0', 2, 1), ('A', 'q2', 1, 2), ('S', 'q2', 2, 0), ('S', 'q0', 3, 0)],
}
BACK_END = [('A', 'q2', 1, 0), ('A', 'q2', 2, 1), ('S', 'q2', 3, 0), ('A', 'q0', 2, 0), ('A', 'q2', 2, 0), ('A', 'q1', 2, 1), ('S', 'q1', 3, 0), ('A', 'q1', 2, 0), ('A', 'q0', 3, 0), ('A', 'o', 3, 0), ('A', 'q1', 3, 0), ('A', 'q2', 3, 0)]


def mask_column(mask_ref, step, rows):
    m = mask_ref[...].astype(F32).T
    lane = lax.broadcasted_iota(jnp.int32, m.shape, 1)
    per = rows // 128
    parts = [
        jnp.sum(jnp.where(lane == step * per + j, m, 0.0), axis=1, keepdims=True) for j in range(per)
    ]
    return jnp.concatenate(parts, axis=0)


def flipped(me, bit):
    return me + (1 << bit) * (1 - 2 * ((me // (1 << bit)) % 2))


class Gather:
    ops = 8
    forwards = {0: (2, 3, 1), 2: (4, 5), 3: (6,), 4: (7,)}

    def __init__(self, me, tensor, items, send_sem, recv_sem):
        self.me, self.tensor, self.items, self.send_sem, self.recv_sem = me, tensor, items, send_sem, recv_sem

    def copy(self, i, op):
        src, dst, base, block, first, rows, yz, quarters = self.items[i]
        one, two = (1, 2) if yz else (2, 1)
        piece = self.me % 8
        if quarters:
            piece = self.me % 2 + 2 * ((self.me // (1 << one)) % 2)
            if op == 5:
                piece = flipped(piece, 1)
        else:
            if op in (4, 5, 7):
                piece = flipped(piece, one)
            if op in (6, 7):
                piece = flipped(piece, two)
        at = dst.at[pl.ds(pl.multiple_of(base + piece * block + first, 8), rows), :]
        if op == 0:
            device = {"tensor": 1 - self.tensor}
        else:
            bit = {1: 0, 2: one, 3: two, 4: two, 5: 0, 6: 0, 7: 0}[op]
            device = {"dp": flipped(self.me, bit)}
        k = i * self.ops + op
        return pltpu.make_async_remote_copy(
            src_ref=src.at[pl.ds(first, rows), :] if op == 0 else at,
            dst_ref=at,
            send_sem=self.send_sem.at[k],
            recv_sem=self.recv_sem.at[k],
            device_id=device,
            device_id_type=MESH,
        )

    def start(self, i):
        self.copy(i, 0).start()

    def after(self, i, op):
        self.copy(i, op).wait_recv()
        for other in self.forwards[op]:
            if not self.items[i][7] or other in (1, 2, 5):
                self.copy(i, other).start()

    def collect(self, i):
        for op in (1, 5) if self.items[i][7] else (1, 5, 6, 7):
            self.copy(i, op).wait_recv()

    def finish_send(self, i):
        for op in (0, 1, 2, 5) if self.items[i][7] else range(self.ops):
            self.copy(i, op).wait_send()


def greet_gather(me, tensor):
    barrier = pltpu.get_barrier_semaphore()
    pl.semaphore_signal(barrier, inc=1, device_id={"tensor": 1 - tensor}, device_id_type=MESH)
    for bit in range(3):
        pl.semaphore_signal(barrier, inc=1, device_id={"dp": flipped(me, bit)}, device_id_type=MESH)
    pl.semaphore_wait(barrier, 4)


class Reduce:
    def __init__(self, dp, me, name, source, home, more, send_sem, recv_sem):
        self.dp, self.me, self.source, self.home, self.more = dp, me, source, home, more
        self.send_sem, self.recv_sem = send_sem, recv_sem
        self.hops = dp.bit_length() - 1
        self.order = list(range(self.hops))
        if self.hops >= 4:
            self.order[1:4] = HOP_BITS[name]

    def block(self, j, m, keep):
        total = 0
        for i, bit in enumerate(self.order):
            mine = (self.me // (1 << bit)) % 2
            if i < j or (i == j and keep):
                total = total + mine * (1 << bit)
            elif i == j:
                total = total + (1 - mine) * (1 << bit)
            else:
                total = total + ((mine + m // (1 << (i - j - 1))) % 2) * (1 << bit)
        return total

    def count(self, j):
        return self.dp >> (j + 1)

    def base(self, j):
        return self.dp // 2 - (self.dp >> j)

    def copy(self, j, m):
        b = self.block(j, m, False)
        if j == 0:
            src, dst, k = self.source.at[b], self.home.at[b // 2], m
        else:
            at = self.base(j) + m
            src, dst, k = self.home.at[b // 2], self.more.at[at], self.dp // 2 + at
        return pltpu.make_async_remote_copy(
            src_ref=src,
            dst_ref=dst,
            send_sem=self.send_sem.at[k],
            recv_sem=self.recv_sem.at[k],
            device_id={"dp": flipped(self.me, self.order[j])},
            device_id_type=MESH,
        )

    def start(self, j, m):
        self.copy(j, m).start()

    def add(self, j, m, kept=None):
        self.copy(j, m).wait_recv()
        at = self.block(j, m, True) // 2
        if j > 0:
            ref, i = self.more, self.base(j) + m
        else:
            ref, i = (self.source, self.block(0, m, True)) if kept is None else (kept, m)
        self.home[at] = self.home[at] + ref[i]

    def finish_send(self, j, m):
        self.copy(j, m).wait_send()

    def every(self, j, do):
        n = self.count(j)
        if n > 8:

            @pl.loop(0, n)
            def _(m):
                do(m)
        else:
            for m in range(n):
                do(m)


def reduce_scratch(dp, rows, cols):
    return [
        pltpu.VMEM((dp // 2, rows, cols), F32),
        pltpu.VMEM((dp // 2 - 1, rows, cols), F32),
        pltpu.SemaphoreType.DMA((dp - 1,)),
        pltpu.SemaphoreType.DMA((dp - 1,)),
    ]


def store_blocks(out, value, at=slice(None)):
    rows = out.shape[1]
    n = value.shape[0] // rows
    if rows % 8 == 0:
        out[:, :, at] = value.reshape(n, rows, value.shape[1])
    else:
        for b in range(n):
            out[b, :, at] = value[b * rows : (b + 1) * rows, :]


def rope(x, cos, sin):
    lane = lax.broadcasted_iota(jnp.int32, x.shape, 1)
    other = jnp.where(lane % HD < HD // 2, pltpu.roll(x, 128 - HD // 2, 1), pltpu.roll(x, HD // 2, 1))
    return x * cos + other * sin


def project(y, width, cos, sin, q_ref, k_ref, v_ref):
    for c in range(0, width, 128):
        q_ref[:, c : c + 128] = rope(y[:, c : c + 128], cos, sin).astype(BF)
        k_ref[:, c : c + 128] = rope(y[:, width + c : width + c + 128], cos, sin).astype(BF)
    v_ref[...] = y[:, 2 * width :].astype(BF)


def attend_pair(q_ref, k_ref, v_ref, at, o_ref, lse_ref, pair, oT, sbuf):
    length = q_ref.shape[0]
    wide = sbuf.shape[2]
    kk = k_ref[:, at]
    qT, vT = q_ref[:, at].T, v_ref[:, at].T
    row = lax.broadcasted_iota(jnp.int32, (128, wide), 0)
    items = [(h, c) for h in range(2) for c in range(0, length, wide)]

    def scores(i):
        h, c = items[i]
        qq = qT[:, c : c + wide]
        s = dot(kk, jnp.where((row < HD) == (h == 0), qq, jnp.zeros_like(qq)))
        sbuf[i % 2] = s
        return jnp.max(s, axis=0, keepdims=True)

    top = scores(0)
    for i, (h, c) in enumerate(items):
        following = scores(i + 1) if i + 1 < len(items) else None
        p = jnp.exp2((sbuf[i % 2] - top) * C2)
        total = jnp.sum(p, axis=0, keepdims=True)
        oT[h * HD : (h + 1) * HD, c : c + wide] = dot(vT[h * HD : (h + 1) * HD, :], p.astype(BF)) * (1.0 / total)
        lse_ref[pl.ds(pair, 1), h : h + 1, c : c + wide] = (top * C2 + jnp.log2(total))[None]
        top = following
    o_ref[:, at] = oT[...].T.astype(BF)


def gelu_parts(x):
    c0, c1 = 0.7978845608028654, 0.044715
    x2 = x * x
    t = jnp.tanh(x * (c0 + (c0 * c1) * x2))
    a = 0.5 + 0.5 * t
    d = a + (x * (0.5 - 0.5 * (t * t))) * (c0 + (3.0 * c0 * c1) * x2)
    return x * a, d


def forward_kernel(
    nb, bucket, mask, mvec, gain1, gain2, bada, bup, cosT, sinT,
    tok_h, te_h, wada_h, wq_h, bup_h, wqf_h, wo_h, wup_h, wdown_h, cot_h,
    h1_ref, q_ref, k_ref, v_ref, mods_ref, cond_ref, o_ref, lse_ref, wxq_ref, wxo_ref,
    attn_ref, h2_ref, feed_ref, gh_ref, gbup_ref, fu, fd, bupx, ku, kd, ru, rd,
    oT, sbuf, fq, fo, wo, wup, wdown, cot, act_s, gp_s, gf_s, lq, lo, lu, ld, pq, po, pu, pd,
    du_s, dd_s, tok, te, wada, wq, cos, sin, first_sem, load_sem, send_sem, recv_sem, bup_sem, keep_sem, give_sem, take_sem,
):
    step = pl.program_id(0)
    me, tensor = lax.axis_index("dp"), lax.axis_index("tensor")
    cols = q_ref.shape[2]
    pairs = cols // 128
    width = tok.shape[1]
    items = []
    for p in range(pairs):
        n = pq.shape[1]
        items += [(pq.at[p], fq.at[p], 0, n, i * (n // 2), n // 2, i == 0, False) for i in range(2)]
    for src, dst in ((po, fo), (pu, fu)):
        n = src.shape[0]
        items += [(src, dst, 0, n, i * (n // 2), n // 2, i == 0, False) for i in range(2)]
    n = pd.shape[1]
    for s in range(2):
        items += [(pd.at[i], fd, i * 4 * n, n, s * (n // 2), n // 2, i == 0, True) for i in range(2)]
    gather = Gather(me, tensor, items, send_sem, recv_sem)
    pieces = []
    for i, (src, dst) in enumerate(((wqf_h, lq), (wo_h, lo), (wup_h, lu))):
        n = dst.shape[0]
        at = pl.ds(pl.multiple_of((me % 8) * n, 16), n)
        pieces.append(pltpu.make_async_copy(src.at[at, :], dst, load_sem.at[i]))
    for i in range(2):
        n = ld.shape[1]
        quarter = me % 2 + 2 * ((me // (2 << i)) % 2)
        at = pl.ds(pl.multiple_of((4 * i + quarter) * n, 16), n)
        pieces.append(pltpu.make_async_copy(wdown_h.at[at, :], ld.at[i], load_sem.at[3 + i]))
    loads = [
        pltpu.make_async_copy(src, dst, load_sem.at[5 + i])
        for i, (src, dst) in enumerate(((wo_h, wo), (wup_h, wup), (wdown_h, wdown), (cot_h, cot)))
    ]
    early = [
        pltpu.make_async_copy(src, dst, first_sem.at[i])
        for i, (src, dst) in enumerate(
            ((te_h, te), (wada_h, wada), (tok_h, tok), (wq_h, wq))
        )
    ]
    bias = pltpu.make_async_remote_copy(
        src_ref=bup_h, dst_ref=bupx, send_sem=bup_sem.at[0], recv_sem=bup_sem.at[1],
        device_id={"tensor": 1 - tensor}, device_id_type=MESH,
    )
    core = me % 2
    dp = du_s.shape[0]

    def parts(k, i):
        src, keep, take = ((du_s, ku, ru), (dd_s, kd, rd))[k]
        stay = pltpu.make_async_copy(src.at[2 * i + core], keep.at[i], keep_sem.at[k, i])
        give = pltpu.make_async_remote_copy(
            src_ref=src.at[2 * i + 1 - core], dst_ref=take.at[i], send_sem=give_sem.at[k, i],
            recv_sem=take_sem.at[k, i], device_id={"dp": flipped(me, 0)}, device_id_type=MESH,
        )
        return stay, give

    def split(first, last, do):
        @pl.loop(first, last)
        def _(i):
            for k in range(2):
                for c in parts(k, i):
                    do(c)

    s_own, s_other = nb, nb + pairs
    s_mlp = s_other + pairs
    s_dw = s_mlp + nb

    @pl.when(step == 0)
    def _():
        for c in pieces + early:
            c.start()
        barrier = pltpu.get_barrier_semaphore()
        pl.semaphore_signal(barrier, inc=1, device_id={"tensor": 1 - tensor}, device_id_type=MESH)
        for bit in range(3):
            pl.semaphore_signal(barrier, inc=1, device_id={"dp": flipped(me, bit)}, device_id_type=MESH)
        pieces[0].wait()
        for p in range(pairs):
            pq[p] = lq[:, p * 128 : (p + 1) * 128].astype(F32)
        pl.semaphore_wait(barrier, 4)
        for i in range(2 * pairs):
            gather.start(i)
        for c in pieces[1:]:
            c.wait()
        for src, dst in ((lo, po), (lu, pu), (ld, pd)):
            dst[...] = src[...].astype(F32)
        for i in range(2 * pairs, len(items)):
            gather.start(i)
        bias.start()
        c, s = cosT[...].T, sinT[...].T
        cos[...] = jnp.concatenate([c] * 4, axis=1)
        sin[...] = jnp.concatenate([-s, s] * 2, axis=1)
        for c in early:
            c.wait()
        for c in loads:
            c.start()

    for at, todo in FORWARD_PLAN.items():

        @pl.when(step == at)
        def _():
            for i, op in todo:
                gather.after(i, op)

    @pl.when(step == s_dw + 1)
    def _():
        split(0, dp // 4, lambda c: c.start())

    @pl.when(step == 0)
    def _():
        row = te[...]
        sub = lax.broadcasted_iota(jnp.int32, row.shape, 0)
        row = jnp.sum(jnp.where(sub == bucket[...], row, 0.0), axis=0, keepdims=True)
        row = row * (1.0 / (1.0 + jnp.exp(-row)))
        cond_ref[...] = row
        col = jnp.broadcast_to(row, (8, row.shape[1])).T[:, 0:1]
        bias_row = line(bada)
        for i in range(6):
            cs = slice(i * width, (i + 1) * width)
            mods_ref[i : i + 1, :] = jnp.sum(wada[:, cs].astype(F32) * col, axis=0, keepdims=True) + bias_row[:, cs]

    def block(first):
        return pl.ds(pl.multiple_of((step - first) * RB, RB), RB)

    @pl.when(step < s_own)
    def _():
        rows = block(0)
        x = tok[rows, :].astype(F32) + mask_column(mask, step, RB) * line(mvec)
        n, _ = normed(x)
        h = (n * (line(gain1) * (1.0 + mods_ref[1:2, :])) + mods_ref[0:1, :]).astype(BF)
        h1_ref[rows, :] = h
        y = jnp.concatenate([dot(h, wq[i]) for i in range(3)], axis=1)
        project(y, cols, cos[rows, :], sin[rows, :], q_ref.at[0, rows, :], k_ref.at[0, rows, :], v_ref.at[0, rows, :])

    def attend(half, pair):
        at = pl.ds(pl.multiple_of(pair * 128, 128), 128)
        attend_pair(
            q_ref.at[half], k_ref.at[half], v_ref.at[half], at, o_ref.at[half], lse_ref, half * pairs + pair, oT, sbuf
        )

    for p in range(pairs):

        @pl.when(step == s_other + p)
        def _():
            for i in (2 * p, 2 * p + 1):
                gather.collect(i)

    @pl.when((step >= s_other) & (step < s_mlp))
    def _():
        p = step - s_other
        at = pl.ds(pl.multiple_of(p * 128, 128), 128)
        for i in range(3):
            wxq_ref[i, :, at] = fq[p, i * width : (i + 1) * width, :].astype(BF)
        w = jnp.concatenate([wxq_ref[i, :, at] for i in range(3)], axis=1)
        for r in range(0, tok.shape[0], RB):
            rows = slice(r, r + RB)
            project(
                dot(h1_ref[rows, :], w), 128, cos[rows, :], sin[rows, :],
                q_ref.at[1, rows, at], k_ref.at[1, rows, at], v_ref.at[1, rows, at],
            )

    @pl.when((step >= s_own) & (step < s_mlp))
    def _():
        half = (step - s_own) // pairs
        attend(half, step - s_own - half * pairs)

    @pl.when(step == s_mlp)
    def _():
        for i in (2 * pairs, 2 * pairs + 1):
            gather.collect(i)
        wxo_ref[...] = fo[...].astype(BF)
        for c in loads:
            c.wait()
        gbup_ref[...] = jnp.zeros_like(gbup_ref)

    @pl.when((step >= s_mlp) & (step < s_dw))
    def _():
        rows = block(s_mlp)
        x = tok[rows, :].astype(F32) + mask_column(mask, step - s_mlp, RB) * line(mvec)
        attn = dot(o_ref[0, rows, :], wo[...]) + dot(o_ref[1, rows, :], wxo_ref[...])
        attn_ref[...] = attn
        n, _ = normed(x + mods_ref[2:3, :] * attn)
        h = (n * (line(gain2) * (1.0 + mods_ref[4:5, :])) + mods_ref[3:4, :]).astype(BF)
        h2_ref[rows, :] = h
        act, slope = gelu_parts(dot(h, wup[...]) + line(bup))
        act = act.astype(BF)
        act_s[rows, :] = act
        feed_ref[...] = dot(act, wdown[...])
        gf = (mods_ref[5:6, :] * cot[rows, :].astype(F32)).astype(BF)
        gf_s[rows, :] = gf
        gp = (dot(gf, wdown[...], 1, 1) * slope).astype(BF)
        gp_s[rows, :] = gp
        gh_ref[...] = dot(gp, wup[...], 1, 1)
        gbup_ref[...] += jnp.sum(gp.astype(F32), axis=0, keepdims=True)

    @pl.when(step >= s_dw)
    def _():
        part = width // 2
        cs = pl.ds(pl.multiple_of((step - s_dw) * part, 128), part)
        blocks = pl.ds((step - s_dw) * (dp // 2), dp // 2)
        store_blocks(du_s.at[blocks], dot(h2_ref[:, cs], gp_s[...], 0, 0))
        store_blocks(dd_s.at[blocks], dot(gf_s[:, cs], act_s[...], 0, 0))

    @pl.when(step == pl.num_programs(0) - 1)
    def _():
        for i, op in FORWARD_END[:2]:
            gather.after(i, op)
        split(dp // 4, dp // 2, lambda c: c.start())
        for i, op in FORWARD_END[2:]:
            gather.after(i, op)
        for i in range(2 * pairs + 2, len(items)):
            gather.collect(i)
        for i in range(len(items)):
            gather.finish_send(i)
        bias.wait()
        split(0, dp // 2, lambda c: c.wait())


def forward(dp, bucket, tokens, mask2, mvec, gain1, gain2, te, wada, bada, wq, cosT, sinT, bup, wo, wup, wdown, cot):
    rows, width = tokens.shape
    cols, ff = wq.shape[2], wup.shape[1]
    nb, pairs = rows // RB, cols // 128
    s_mlp = nb + 2 * pairs
    mblk = pl.BlockSpec((RB, width), lambda i: (jnp.clip(i - s_mlp, 0, nb - 1), 0))
    grad = (dp, width // dp, ff)
    half = sds((dp // 2, *grad[1:]), F32)
    act = (2, rows, cols)
    wqf = wq.reshape(3 * width, cols)
    vm = pltpu.VMEM
    piece = lambda w: (w.shape[0] // 8, w.shape[1])
    n_items = 2 * pairs + 8
    return pl.pallas_call(
        functools.partial(forward_kernel, nb),
        grid=(s_mlp + nb + 2,),
        in_specs=[
            one(x.shape) for x in (bucket, mask2, mvec, gain1, gain2, bada, bup, cosT, sinT)
        ] + [ANYS] * 10,
        out_specs=[
            one((rows, width)), one(act), one(act), one(act), one((8, width)), one((1, te.shape[1])),
            one(act), one((2 * pairs, 2, rows)), one(wq.shape), one((cols, width)),
            mblk, one((rows, width)), mblk, mblk, one((1, ff)), *[ANYS] * 7,
        ],
        out_shape=[
            sds((rows, width), BF), sds(act, BF), sds(act, BF), sds(act, BF), sds((8, width), F32),
            sds((1, te.shape[1]), F32), sds(act, BF), sds((2 * pairs, 2, rows), F32), sds(wq.shape, BF),
            sds((cols, width), BF), sds((rows, width), F32), sds((rows, width), BF), sds((rows, width), F32),
            sds((rows, width), F32), sds((1, ff), F32), sds(wup.shape, F32), sds(wdown.shape, F32),
            sds(bup.shape, F32), half, half, half, half,
        ],
        scratch_shapes=[
            vm((128, rows), F32), vm((2, rows, 512), F32), vm((pairs, 3 * width, 128), F32), vm(wo.shape, F32),
            vm(wo.shape, BF), vm(wup.shape, BF), vm(wdown.shape, BF), vm(cot.shape, BF),
            vm((rows, ff), BF), vm((rows, ff), BF), vm((rows, width), BF),
            *[vm(piece(w), BF) for w in (wqf, wo, wup)], vm((2, *piece(wdown)), BF),
            vm((pairs, piece(wqf)[0], 128), F32), *[vm(piece(w), F32) for w in (wo, wup)],
            vm((2, *piece(wdown)), F32), vm(grad, F32), vm(grad, F32),
            *[vm(x.shape, x.dtype) for x in (tokens, te, wada, wq)], vm((rows, 128), F32), vm((rows, 128), F32),
            pltpu.SemaphoreType.DMA((4,)), pltpu.SemaphoreType.DMA((9,)), pltpu.SemaphoreType.DMA((8 * n_items,)),
            pltpu.SemaphoreType.DMA((8 * n_items,)), pltpu.SemaphoreType.DMA((2,)),
            *[pltpu.SemaphoreType.DMA((2, dp // 2))] * 3,
        ],
        compiler_params=params(collective_id=2, has_side_effects=True),
        name="forward",
    )(
        bucket, mask2, mvec, gain1, gain2, bada, bup, cosT, sinT, tokens, te, wada, wq, bup, wqf, wo, wup, wdown, cot
    )


def hidden(h, gf, wup, bup, wdown):
    wide = wup.shape[1] // 3
    feed = gh = None
    dots = lambda c: (dot(h, wup[:, c : c + wide]) + bup[:, c : c + wide], dot(gf, wdown[c : c + wide, :], 1, 1))
    ready = dots(0)
    for c in range(0, 3 * wide, wide):
        following = dots(c + wide) if c + wide < 3 * wide else None
        act, slope = gelu_parts(ready[0])
        gp = (ready[1] * slope).astype(BF)
        f = dot(act.astype(BF), wdown[c : c + wide, :])
        d = dot(gp, wup[:, c : c + wide], 1, 1)
        feed, gh = (f, d) if feed is None else (feed + f, gh + d)
        ready = following
    return feed, gh


def mlp_other_kernel(
    dp, tok, mask, mvec, mods, gain, attn_ref, h_ref, feed_ref, gh_ref, cot, bup, bdown,
    mo, wo, wx, gbup, cond, ku, kd, ru, rd, fu, fd,
    res_ref, gmid_ref, gm_ref, small, dw_ref, hu_out, hd_out,
    acc, keep_u, keep_d, load_sem, stage_u, stage_d, wup, wdown, w_sem,
    hu, more_u, send_u, recv_u, hd, more_d, send_d, recv_d,
):
    step, last = pl.program_id(0), pl.num_programs(0) - 1
    me, tensor = lax.axis_index("dp"), lax.axis_index("tensor")
    weights = {
        "u": Reduce(dp, me, "u", None, hu, more_u, send_u, recv_u),
        "d": Reduce(dp, me, "d", None, hd, more_d, send_d, recv_d),
    }

    def act(kind, w, j, m):
        if kind == "S":
            weights[w].start(j, m)
        else:
            weights[w].add(j, m)

    def point(at):
        if dp == 16 and at in MLP_PLAN:

            @pl.when(step == at[0])
            def _():
                for a in MLP_PLAN[at]:
                    act(*a)

    halves = [
        pltpu.make_async_copy(src, dst, load_sem.at[i])
        for i, (src, dst) in enumerate(((ru, hu), (ku, keep_u), (rd, hd), (kd, keep_d)))
    ]
    wloads = [
        pltpu.make_async_copy(src, dst, w_sem.at[i]) for i, (src, dst) in enumerate(((fu, stage_u), (fd, stage_d)))
    ]

    @pl.when(step == 0)
    def _():
        for c in halves + wloads:
            c.start()
        barrier = pltpu.get_barrier_semaphore()
        for j in range(1, 4):
            pl.semaphore_signal(barrier, inc=1, device_id={"dp": flipped(me, j)}, device_id_type=MESH)
        small[...] = jnp.zeros_like(small)
        pl.semaphore_wait(barrier, 3)
        for i, (home, keep) in enumerate(((hu, keep_u), (hd, keep_d))):
            halves[2 * i].wait()
            halves[2 * i + 1].wait()

            @pl.loop(0, dp // 2)
            def _(b):
                home[b] = home[b] + keep[b]

            if dp == 16:
                for a in MLP_PLAN[0, 0]:
                    if a[1] == "ud"[i]:
                        act(*a)
        for c, src, dst in zip(wloads, (stage_u, stage_d), (wup, wdown)):
            c.wait()
            dst[...] = src[...].astype(BF)

    for i in range(1, 4):
        point((i, 0))

    x = tok[...].astype(F32) + mask_column(mask, step, tok.shape[0]) * line(mvec)
    attn = attn_ref[...]
    middle = x + mods[2:3, :] * attn
    n2, rs = normed(middle)
    g = cot[...].astype(F32)
    gf = (mods[5:6, :] * g).astype(BF)
    feed, gh = hidden(h_ref[...], gf, wup, line(bup), wdown)
    feed = (feed_ref[...] + feed) + line(bdown)
    gh = gh_ref[...] + gh

    for i in range(4):
        point((i, 1))
    res_ref[...] = (middle + mods[5:6, :] * feed).astype(BF)
    opened = 1.0 + mods[4:5, :]
    e = gh * (opened * line(gain))
    inner = jnp.mean(e * n2, axis=-1, keepdims=True)
    gmid = g + (e - jnp.mean(e, axis=-1, keepdims=True) - n2 * inner) * rs
    gmid_ref[...] = gmid
    ga = (mods[2:3, :] * gmid).astype(BF)
    gm_ref[0] = dot(ga, wo[...], 1, 1).astype(BF)
    gm_ref[1] = dot(ga, wx[...], 1, 1).astype(BF)
    col = lambda v: jnp.sum(v, axis=0, keepdims=True)
    small[0:1, :] += col(g * feed)
    small[1:2, :] += col(gf.astype(F32))
    small[2:3, :] += col(gh)
    small[3:4, :] += col(gh * n2)
    small[4:5, :] += col(gmid * attn)
    dw = dot(ga, mo[...], 0, 0)

    @pl.when(step == 0)
    def _():
        acc[...] = dw

    @pl.when(step > 0)
    def _():
        acc[...] += dw

    @pl.when(step == last)
    def _():
        width = mods.shape[1]
        small[5:6, :] = small[3:4, :] * opened
        small[3:4, :] = small[3:4, :] * line(gain)
        for i in range(gbup.shape[1] // width):
            small[8 + i : 9 + i, :] = gbup[:, i * width : (i + 1) * width]
        small[6:7, 0 : cond.shape[1]] = cond[...]
        store_blocks(dw_ref, acc[...])
        if dp == 16:
            for a in MLP_END:
                act(*a)
            for todo in (*MLP_PLAN.values(), MLP_END):
                for kind, w, j, m in todo:
                    if kind == "S":
                        weights[w].finish_send(j, m)
        stores = [
            pltpu.make_async_copy(src, dst, w_sem.at[k]) for k, (src, dst) in enumerate(((hu, hu_out), (hd, hd_out)))
        ]
        for c in stores:
            c.start()
        for c in stores:
            c.wait()


def mlp_other(dp, tokens, mask2, mvec, mods, gain, attn, h, feed, gh, cot, bup, bdown, os, wo, wx, gbup, cond, ku, kd, ru, rd, fu, fd):
    rows, width = tokens.shape
    ff, cols = fu.shape[1], wo.shape[0]
    part = width // dp
    blk = lambda c: pl.BlockSpec((RB, c), lambda i: (i, 0))
    half = (dp // 2, part, ff)
    vm = pltpu.VMEM
    return pl.pallas_call(
        functools.partial(mlp_other_kernel, dp),
        grid=(rows // RB,),
        in_specs=[
            blk(width), one(mask2.shape), one(mvec.shape), one(mods.shape), one(gain.shape),
            blk(width), blk(width), blk(width), blk(width), blk(width), one(bup.shape), one(bdown.shape),
            pl.BlockSpec((None, RB, cols), lambda i: (0, i, 0)), one(wo.shape), one(wx.shape), one(gbup.shape),
            one(cond.shape), *[ANYS] * 6,
        ],
        out_specs=[
            blk(width), blk(width), pl.BlockSpec((2, RB, cols), lambda i: (0, i, 0)), one((16, width)),
            one((dp, part, cols)), ANYS, ANYS,
        ],
        out_shape=[
            sds((rows, width), BF), sds((rows, width), F32), sds((2, rows, cols), BF), sds((16, width), F32),
            sds((dp, part, cols), F32), sds(half, F32), sds(half, F32),
        ],
        scratch_shapes=[
            vm((width, cols), F32), vm(half, F32), vm(half, F32), pltpu.SemaphoreType.DMA((4,)),
            vm(fu.shape, F32), vm(fd.shape, F32), vm(fu.shape, BF), vm(fd.shape, BF), pltpu.SemaphoreType.DMA((2,)),
            *reduce_scratch(dp, part, ff), *reduce_scratch(dp, part, ff),
        ],
        compiler_params=params(collective_id=3, has_side_effects=True),
        name="mlp_other",
    )(tokens, mask2, mvec, mods, gain, attn, h, feed, gh, cot, bup, bdown, os, wo, wx, gbup, cond, ku, kd, ru, rd, fu, fd)


def attend_back_pair(q_ref, k_ref, v_ref, o_ref, do_ref, lse_ref, cosT, sinT, g_ref, at, gT, between):
    length = q_ref.shape[0]
    kk, vv = k_ref[...], v_ref[...]
    kT, qT, doT = kk.T, q_ref[...].T, do_ref[...].T
    oT = o_ref[...].T
    prod = doT.astype(F32) * oT.astype(F32)
    row = lax.broadcasted_iota(jnp.int32, (128, length), 0)
    half = HD // 2
    for h in range(2):
        hs = slice(h * HD, (h + 1) * HD)
        sel = (row < HD) == (h == 0)
        qm = jnp.where(sel, qT, jnp.zeros_like(qT))
        dm = jnp.where(sel, doT, jnp.zeros_like(doT))
        inner = jnp.sum(prod[hs, :], axis=0, keepdims=True)
        p = jnp.exp2(dot(kk, qm) * C2 - lse_ref[h : h + 1, :])
        ds = (p * (dot(vv, dm) - inner)).astype(BF)
        dv = dot(doT[hs, :], p.astype(BF), 1, 1)
        dk = dot(qT[hs, :], ds, 1, 1) * 0.125
        dq = dot(kT[hs, :], ds) * 0.125
        c, s = cosT[...], sinT[...]
        for i, d in ((0, dq), (1, dk)):
            a, b = d[:half, :], d[half:, :]
            gT[i, h * HD : h * HD + half, :] = a * c + b * s
            gT[i, h * HD + half : (h + 1) * HD, :] = b * c - a * s
        gT[2, hs, :] = dv
        if h == 0:
            between()
    for i in range(3):
        g_ref[i, :, at] = gT[i].T.astype(BF)


def backward_kernel(
    dp, nb, pairs, q_ref, k_ref, v_ref, o_ref, do_ref, lse_ref, cosT, sinT, h1_h, w_h, wx_h, tok, mask, mvec,
    mods, gain, gmid_ref, small, dw_hbm, hu_in, hd_in,
    gt_ref, up_ref, down_ref, out_ref, qkv_ref, got_ref,
    gT, g, h1, w, wx, dw_out, dqs, late_s, pack, got, own_sem, gsend, grecv, load_sem, *scratch,
):
    step, last = pl.program_id(0), pl.num_programs(0) - 1
    me, tensor = lax.axis_index("dp"), lax.axis_index("tensor")
    names = ["u", "d", "o"] + [f"q{p}" for p in range(pairs)]
    sources = [None, None, dw_out] + [dqs.at[p] for p in range(pairs)]
    weights = {
        n: Reduce(dp, me, n, src, *scratch[4 * i : 4 * i + 4]) for i, (n, src) in enumerate(zip(names, sources))
    }
    hops = weights["u"].hops
    width, cols = mods.shape[1], w.shape[2]
    loads = [
        pltpu.make_async_copy(src, dst, load_sem.at[i])
        for i, (src, dst) in enumerate(((dw_hbm, dw_out), (hu_in, weights["u"].home), (hd_in, weights["d"].home)))
    ]
    later = [
        pltpu.make_async_copy(src, dst, load_sem.at[3 + i]) for i, (src, dst) in enumerate(((h1_h, h1), (w_h, w), (wx_h, wx)))
    ]
    s_x, s_end = pairs, 2 * pairs
    n = width // dp

    def act(kind, n, j, m):
        if kind == "S":
            weights[n].start(j, m)
        else:
            weights[n].add(j, m)

    def point(at):
        if dp == 16 and at in BACK_PLAN:

            @pl.when(step == at[0])
            def _():
                for a in BACK_PLAN[at]:
                    act(*a)

    def pack_rows(summed, gmod, cond):
        for d in range(dp):
            for i in range(4):
                if summed[i] is not None:
                    pack[d, :, i * n : (i + 1) * n] = summed[i][:, d * n : (d + 1) * n]
            row, off = 4 + 2 * n * d // width, 2 * n * d % width
            if summed[row] is not None:
                pack[d, :, 4 * n : 6 * n] = summed[row][:, off : off + 2 * n]
            done, need = 0, 6 * n
            while done < need:
                row, off = (need * d + done) // width, (need * d + done) % width
                take = min(need - done, width - off)
                if gmod[row] is not None:
                    pack[d, :, PACK_MOD + done : PACK_MOD + done + take] = gmod[row][:, off : off + take]
                done += take
            if cond is not None:
                pack[d, :, PACK_COND : PACK_COND + 128] = cond

    def spread(r):
        to = (me + r) % dp
        return pltpu.make_async_remote_copy(
            src_ref=pack.at[to], dst_ref=got.at[me], send_sem=gsend.at[r], recv_sem=grecv.at[r],
            device_id=(to, tensor), device_id_type=MESH,
        )

    @pl.when(step == 0)
    def _():
        for c in loads:
            c.start()
        barrier = pltpu.get_barrier_semaphore()

        @pl.loop(1, dp)
        def _(r):
            pl.semaphore_signal(barrier, inc=1, device_id=((me + r) % dp, tensor), device_id_type=MESH)

        pl.semaphore_wait(barrier, dp - 1)
        for c in loads:
            c.wait()
        for c in later:
            c.start()
        late_s[...] = jnp.zeros_like(late_s)
        pack[...] = jnp.zeros_like(pack)
        summed = [None, None, small[5:6, :], small[1:2, :], small[8:9, :], small[9:10, :]]
        gmod = [None, None, small[4:5, :], small[2:3, :], small[3:4, :], small[0:1, :]]
        pack_rows(summed, gmod, small[6:7, 0:128])

    for i in range(2 * pairs + nb):
        point((i, 0))

    def between():
        for p in range(2 * pairs):
            point((p, 1))

    @pl.when(step < s_end)
    def _():
        half = step // pairs
        at = pl.ds(pl.multiple_of((step - half * pairs) * 128, 128), 128)
        attend_back_pair(q_ref, k_ref, v_ref, o_ref, do_ref, lse_ref, cosT, sinT, g.at[half], at, gT, between)

    @pl.when(step == 0)
    def _():
        for c in later:
            c.wait()

    @pl.when(step < s_x)
    def _():
        at = pl.ds(pl.multiple_of(step * 128, 128), 128)
        gp = jnp.concatenate([g[0, i, :, at] for i in range(3)], axis=1)
        store_blocks(dqs.at[step], dot(h1[...], gp, 0, 0))

    @pl.when(step >= s_end)
    def _():
        i = step - s_end
        rows = pl.ds(pl.multiple_of(i * RB, RB), RB)
        m = mask_column(mask, i, RB)
        n1, rs = normed(tok[...].astype(F32) + m * line(mvec))
        parts = [
            dot(d[0, rows, :], ww[0], 1, 1) + dot(d[1, rows, :], ww[1], 1, 1) + dot(d[2, rows, :], ww[2], 1, 1)
            for d, ww in ((g.at[0], w), (g.at[1], wx))
        ]
        gh = parts[0] + parts[1]
        e = gh * ((1.0 + mods[1:2, :]) * line(gain))
        inner = jnp.mean(e * n1, axis=-1, keepdims=True)
        gs = gmid_ref[...] + (e - jnp.mean(e, axis=-1, keepdims=True) - n1 * inner) * rs
        gt_ref[...] = gs.astype(BF)
        col = lambda v: jnp.sum(v, axis=0, keepdims=True)
        late_s[0:1, :] += col(gh)
        late_s[1:2, :] += col(gh * n1)
        late_s[3:4, :] += col(m * gs)

    @pl.when(step == last)
    def _():
        late_s[2:3, :] = late_s[1:2, :] * (1.0 + mods[1:2, :])
        late_s[1:2, :] = late_s[1:2, :] * line(gain)
        none = [None] * 4
        pack_rows([late_s[3:4, :], late_s[2:3, :]] + none, [late_s[0:1, :], late_s[1:2, :]] + none, None)
        if dp == 16:
            for a in BACK_END[:2]:
                act(*a)
        own = pltpu.make_async_copy(pack.at[me], got.at[me], own_sem)
        own.start()

        @pl.loop(1, dp)
        def _(r):
            spread(r).start()

        if dp == 16:
            for a in BACK_END[2:]:
                act(*a)
            todo = [a for v in BACK_PLAN.values() for a in v] + BACK_END
            for kind, n, j, m in todo:
                if kind == "S":
                    weights[n].finish_send(j, m)
        else:
            for n, r in weights.items():
                for j in range(1 if n in "ud" else 0, hops):
                    r.every(j, lambda m: r.start(j, m))
                    r.every(j, lambda m: r.add(j, m))
                    r.every(j, lambda m: r.finish_send(j, m))
        up_ref[...] = weights["u"].home[me // 2]
        down_ref[...] = weights["d"].home[me // 2]
        out_ref[...] = weights["o"].home[me // 2]
        for p in range(pairs):
            qkv_ref[p] = weights[f"q{p}"].home[me // 2]
        own.wait()

        @pl.loop(1, dp)
        def _(r):
            spread(r).wait()

        got_ref[...] = got[...]


PACK_MOD, PACK_COND, PACK = 384, 768, 896


def backward(dp, qs, ks, vs, os, gm, lses, cosT, sinT, h1, w, wx, tokens, mask2, mvec, mods, gain, gmid, small, dw_out, hu, hd):
    rows, width = tokens.shape
    cols = w.shape[2]
    nb, pairs = rows // RB, cols // 128
    part, ff = hu.shape[1], hu.shape[2]
    s_end = 2 * pairs
    pick = lambda i: jnp.minimum(i, 2 * pairs - 1)
    pair = pl.BlockSpec((None, rows, 128), lambda i: (pick(i) // pairs, 0, pick(i) % pairs))
    blk = pl.BlockSpec((RB, width), lambda i: (jnp.maximum(i - s_end, 0), 0))
    vm = pltpu.VMEM
    return pl.pallas_call(
        functools.partial(backward_kernel, dp, nb, pairs),
        grid=(s_end + nb,),
        in_specs=[pair] * 5 + [
            pl.BlockSpec((None, 2, rows), lambda i: (pick(i), 0, 0)), one(cosT.shape), one(sinT.shape),
            ANYS, ANYS, ANYS, blk, one(mask2.shape), one(mvec.shape), one(mods.shape),
            one(gain.shape), blk, one(small.shape), ANYS, ANYS, ANYS,
        ],
        out_specs=[
            blk, one((part, ff)), one((part, ff)), one((part, cols)), one((pairs, part, 384)), one((dp, 1, PACK)),
        ],
        out_shape=[
            sds((rows, width), BF), sds((part, ff), F32), sds((part, ff), F32), sds((part, cols), F32),
            sds((pairs, part, 384), F32), sds((dp, 1, PACK), F32),
        ],
        scratch_shapes=[
            vm((3, 128, rows), F32), vm((2, 3, rows, cols), BF), vm(h1.shape, BF), vm(w.shape, BF), vm(wx.shape, BF),
            vm((dp, part, cols), F32),
            vm((pairs, dp, part, 384), F32), vm((8, width), F32), vm((dp, 1, PACK), F32), vm((dp, 1, PACK), F32),
            pltpu.SemaphoreType.DMA, pltpu.SemaphoreType.DMA((dp,)), pltpu.SemaphoreType.DMA((dp,)),
            pltpu.SemaphoreType.DMA((6,)),
            *reduce_scratch(dp, part, ff), *reduce_scratch(dp, part, ff), *reduce_scratch(dp, part, cols),
            *[s for _ in range(pairs) for s in reduce_scratch(dp, part, 384)],
        ],
        compiler_params=params(collective_id=4, has_side_effects=True),
        name="backward",
    )(qs, ks, vs, os, gm, lses, cosT, sinT, h1, w, wx, tokens, mask2, mvec, mods, gain, gmid, small, dw_out, hu, hd)


def finish_kernel(res_in, gt_in, got, up, down, out, qkv, res, gt, mask, ln1, wqkv, wout, ln2, wup, bup, wdown, bdown, wada, bada):
    res[...] = res_in[...]
    gt[...] = gt_in[...]

    @pl.when(pl.program_id(0) == 1)
    def _():
        finish_rest(got, up, down, out, qkv, mask, ln1, wqkv, wout, ln2, wup, bup, wdown, bdown, wada, bada)


def finish_rest(got, up, down, out, qkv, mask, ln1, wqkv, wout, ln2, wup, bup, wdown, bdown, wada, bada):
    dp = got.shape[0]
    g = got[...].reshape(dp, got.shape[2])
    n = wup.shape[0]
    total = jnp.sum(g, axis=0, keepdims=True)
    for i, ref in enumerate((mask, ln1, ln2, bdown)):
        ref[...] = total[:, i * n : (i + 1) * n].reshape(n)
    bup[...] = total[:, 4 * n : 6 * n].reshape(2 * n)
    bada[...] = total[:, PACK_MOD : PACK_MOD + 6 * n].reshape(6 * n)
    wada[...] = lax.dot_general(
        g[:, PACK_MOD : PACK_MOD + 6 * n], g[:, PACK_COND : PACK_COND + wada.shape[1]], (((0,), (0,)), ((), ())),
        precision=lax.Precision.HIGHEST, preferred_element_type=F32,
    )
    wup[...] = up[...]
    wdown[...] = down[...]
    wout[...] = out[...]
    for p in range(qkv.shape[0]):
        for i in range(3):
            wqkv[i, :, p * 128 : (p + 1) * 128] = qkv[p, :, i * 128 : (i + 1) * 128]


def finish(result, grad_tokens, got, up, down, out, qkv, tdim):
    n, ff = up.shape
    cols = out.shape[1]
    shapes = [(n,), (n,), (3, n, cols), (n, cols), (n,), (n, ff), (2 * n,), (n, ff), (n,), (6 * n, tdim), (6 * n,)]
    ins = (got, up, down, out, qkv)
    blk = pl.BlockSpec((result.shape[0] // 2, result.shape[1]), lambda i: (i, 0))
    return pl.pallas_call(
        finish_kernel,
        grid=(2,),
        in_specs=[blk, blk] + [one(x.shape) for x in ins],
        out_specs=[blk, blk] + [one(s) for s in shapes],
        out_shape=[sds(result.shape, BF)] * 2 + [sds(s, F32) for s in shapes],
        compiler_params=params(),
        name="finish",
    )(result, grad_tokens, *ins)


def rope_tables(length):
    half = HD // 2
    freq = 10000.0 ** (-(np.arange(half, dtype=np.float64) / half))
    angle = np.arange(length, dtype=np.float64)[:, None] * freq[None, :]
    return np.cos(angle).astype(np.float32), np.sin(angle).astype(np.float32)


def body(
    dp, tokens, cotangent, bucket, mask, time_embed, mask_vec, ln1_gain, w_qkv, w_out, ln2_gain,
    w_up, b_up, w_down, b_down, w_ada, b_ada,
):
    rows, width = tokens.shape
    mask2 = mask.reshape(rows // 128, 128)
    c, s = rope_tables(rows)
    cosT, sinT = jnp.asarray(np.ascontiguousarray(c.T)), jnp.asarray(np.ascontiguousarray(s.T))
    (h1, qs, ks, vs, mods, cond, os, lses, wx_qkv, wx_out, attn, h2, feed, gh2, gbup, fu, fd, bup_x, ku, kd, ru, rd) = forward(
        dp, bucket.reshape(1, 1), tokens, mask2, mask_vec, ln1_gain, ln2_gain, time_embed, w_ada, b_ada, w_qkv,
        cosT, sinT, b_up, w_out, w_up, w_down, cotangent,
    )
    result, gmid, gm, small, dw_out, hu, hd = mlp_other(
        dp, tokens, mask2, mask_vec, mods, ln2_gain, attn, h2, feed, gh2, cotangent, bup_x, b_down,
        os, w_out, wx_out, gbup, cond, ku, kd, ru, rd, fu, fd,
    )
    grad_tokens, sum_up, sum_down, sum_out, sum_qkv, got = backward(
        dp, qs, ks, vs, os, gm, lses, cosT, sinT, h1, w_qkv, wx_qkv, tokens, mask2, mask_vec, mods, ln1_gain, gmid,
        small, dw_out, hu, hd,
    )
    out = finish(result, grad_tokens, got, sum_up, sum_down, sum_out, sum_qkv, time_embed.shape[1])
    return tuple(x.T if i in (5, 9, 11) else x for i, x in enumerate(out))


def solution(mesh):
    in_specs = (
        P("dp", None), P("dp", None), P("dp"), P("dp"), P(), P(), P(), P(None, None, "tensor"),
        P("tensor", None), P(), P(None, "tensor"), P("tensor"), P("tensor", None), P(), P(), P(),
    )
    out_specs = (
        P("dp", None), P("dp", None), P("dp"), P("dp"), P(None, "dp", "tensor"), P("tensor", "dp"),
        P("dp"), P("dp", "tensor"), P(("tensor", "dp")), P("tensor", "dp"), P("dp"), P(None, "dp"), P("dp"),
    )
    step = functools.partial(body, mesh.shape["dp"])
    return jax.shard_map(step, mesh=mesh, in_specs=in_specs, out_specs=out_specs, check_vma=False)
```
